256 devices in a mesh: rad: 8 (over z), azi: 8 (over y, core), ax: 4 (over x).
Axes of the slice: x: 4, y: 4, z: 8, core: 2. Of those that a mesh axis runs over, the one named last changes fastest.
Arguments:
- primal: float32 [5, 128, 256, 512], P(None, 'rad', 'azi', 'ax'), may hold values from -1 to 4, as said below
- adjoint: float32 [5, 128, 256, 512], P(None, 'rad', 'azi', 'ax'), may hold values from -6 to 6
- refine_flag: int32 [8, 16, 32], P('rad', 'azi', 'ax'), may hold values 0 or 1
- owner_map: int32 [8, 16, 32], P('rad', 'azi', 'ax'), may hold values from 0 to 255
- migrate_weight: int32 [8, 16, 32], P('rad', 'azi', 'ax'), may hold values from 1 to 16
- neighbor_list: int32 [8, 16, 32, 6], P('rad', 'azi', 'ax'), may hold values from 0 to 4095
Outputs:
- indicator: float32 [128, 256, 512], P('rad', 'azi', 'ax')
- block_cost: float32 [8, 16, 32], P('rad', 'azi', 'ax')
- owner_load: float32 [8, 8, 4], P('rad', 'azi', 'ax')
The draws below stay inside these ranges and needn't reach their ends.
Inputs may be any that keep to these rules, and one draw needn't show every extreme that they name: `primal`: density (field 0) lies in [0.5, 2], momenta (fields 1 to 3) in [-1, 1], energy (field 4) in [2, 4].
All inputs are finite; a program needn't handle non-finite values. No bound on the sum of `refine_flag` on one device may be relied on, other than what follows from the above.
Results may differ from the reference program's by a relative error of at most 0.00002.
Values sent between devices are 32-bit elements; how exact they have to be, the bound alone decides.
A program may use at most 64 MiB of HBM per device.

```python
import math
import jax
import jax.numpy as jnp
import numpy as np
from jax import lax

FIELDS = 5
BLK = 16
CR = 16
CA = 32
CX = 128
NR = 128
NA = 256
NX = 512
NBR = 8
NBA = 16
NBX = 32
NBLK = 4096
N_RAD = 8
N_AZI = 8
N_AX = 4


def draw_primal(key, part):
    keys = jax.random.split(key, 3)
    shape = (NR, NA, NX)
    first = jax.random.uniform(keys[0], shape, jnp.float32)
    rough = jax.random.uniform(keys[1], (3, NR, NA, NX), jnp.float32, -1.0, 1.0)
    third = jax.random.uniform(keys[2], shape, jnp.float32)
    density = 0.5 + 1.5 * first
    momenta = rough
    energy = 2.0 + 2.0 * third
    return jnp.concatenate([density[None], momenta, energy[None]], axis=0).astype(jnp.float32)


def set_ends(result, key, smallest, high):
    longest = result.shape.index(max(result.shape))
    spots = []
    for shift in (0, 1):
        where = [jax.random.randint(jax.random.fold_in(key, axis), (), 0, length) for axis, length in enumerate(result.shape)]
        where[longest] = (where[longest] + shift) % result.shape[longest]
        spots.append(tuple(where))
    return result.at[spots[0]].set(smallest).at[spots[1]].set(high)


def block_levels(key, extent, shards, smallest, top_value):
    gain = 1.0
    for axis_at, parts in shards:
        heights = jax.random.uniform(jax.random.fold_in(jax.random.fold_in(key, 6), axis_at), (parts,), jnp.float32, smallest / len(shards), top_value / len(shards))
        gain = gain * jnp.repeat(jnp.exp(heights), extent[axis_at] // parts).reshape((-1,) + (1,) * (len(extent) - 1 - axis_at))
    return gain


def cumulative_ranks(count, slope):
    portions = [(1 << 20) // math.isqrt(rank ** slope) + 1 for rank in range(1, count + 1)]
    spread = 1 + sum(portions) // (1 << 30)
    return np.cumsum(np.array([max(1, weight // spread) for weight in portions]))


def ranked_ids(own_key, extent, count, slope):
    table = cumulative_ranks(count, slope)
    pick = jax.random.randint(jax.random.fold_in(own_key, 1), extent, 0, int(table[count - 1]))
    rank = jnp.searchsorted(jnp.asarray(table, jnp.int32), pick, side="right")
    return jax.random.permutation(jax.random.fold_in(own_key, 2), count)[rank].astype(jnp.int32)


def gaussian(rng, dims, scale, limit, shards=(), kind=jnp.bfloat16):
    loudness = block_levels(rng, dims, shards, -0.22, 0.18) if shards else 1.0
    values = jax.random.normal(rng, dims, jnp.float32) * scale * loudness
    return jnp.minimum(jnp.maximum(values, -limit), limit).astype(kind)


def setup_inputs(seed: int = 0) -> dict:
    streams_of = jax.random.split(jax.random.key(seed), 7)
    primal = draw_primal(jax.random.fold_in(streams_of[6], 71), 0)
    adjoint = gaussian(streams_of[1], (FIELDS, NR, NA, NX), 1.0, 6.0, ((1, 8), (2, 8), (3, 4)), jnp.float32)
    refine_flag = set_ends((jax.random.randint(streams_of[2], (NBR, NBA, NBX), 0, 4) < 1).astype(jnp.int32), jax.random.fold_in(streams_of[2], 1), 0, 1)
    owner_map = set_ends(ranked_ids(streams_of[3], (NBR, NBA, NBX), N_RAD * N_AZI * N_AX, 2), jax.random.fold_in(streams_of[3], 3), 0, (N_RAD * N_AZI * N_AX) - 1).astype(jnp.int32)
    migrate_weight = set_ends(jax.random.randint(streams_of[4], (NBR, NBA, NBX), 1, 17), jax.random.fold_in(streams_of[4], 1), 1, 16).astype(jnp.int32)
    neighbor_list = set_ends(jax.random.randint(streams_of[5], (NBR, NBA, NBX, 6), 0, NBLK), jax.random.fold_in(streams_of[5], 1), 0, NBLK - 1).astype(jnp.int32)
    return {"primal": primal, "adjoint": adjoint, "refine_flag": refine_flag, "owner_map": owner_map, "migrate_weight": migrate_weight, "neighbor_list": neighbor_list}


def euler_flux(face_state, along):
    density = face_state[0]
    momenta = face_state[1:4]
    energy = face_state[4]
    velocity = momenta[along] / density
    kinetic = 0.5 * (momenta[0] * momenta[0] + momenta[1] * momenta[1] + momenta[2] * momenta[2]) / density
    pressure = 0.4 * (energy - kinetic)
    columns = [momenta[along], momenta[0] * velocity, momenta[1] * velocity, momenta[2] * velocity, (energy + pressure) * velocity]
    columns[1 + along] = columns[1 + along] + pressure
    return jnp.stack(columns)


def window(extended, along, start, count, padded_axes):
    pieces = [slice(None)] * 4
    for spatial in padded_axes:
        pieces[spatial] = slice(2, extended.shape[spatial] - 2)
    pieces[along] = slice(start, start + count)
    return extended[tuple(pieces)]


def axis_terms(ext_primal, ext_adjoint, along, padded_axes):
    length = ext_primal.shape[along] - 4
    high = (7.0 * window(ext_primal, along, 1, length + 1, padded_axes) - window(ext_primal, along, 0, length + 1, padded_axes)) / 12.0
    low = (7.0 * window(ext_primal, along, 2, length + 1, padded_axes) - window(ext_primal, along, 3, length + 1, padded_axes)) / 12.0
    fluxes = euler_flux(high + low, along - 1)
    balance = lax.slice_in_dim(fluxes, 1, length + 1, axis=along) - lax.slice_in_dim(fluxes, 0, length, axis=along)
    fourth = (window(ext_adjoint, along, 0, length, padded_axes) - 4.0 * window(ext_adjoint, along, 1, length, padded_axes)
              + 6.0 * window(ext_adjoint, along, 2, length, padded_axes) - 4.0 * window(ext_adjoint, along, 3, length, padded_axes)
              + window(ext_adjoint, along, 4, length, padded_axes)) / 12.0
    return balance, fourth


def extend(fields):
    wrapped = jnp.concatenate([fields[:, :, -2:], fields, fields[:, :, :2]], axis=2)
    return jnp.pad(wrapped, ((0, 0), (2, 2), (0, 0), (2, 2)))


def reference(primal, adjoint, refine_flag, owner_map, migrate_weight, neighbor_list):
    ext_primal = extend(primal)
    ext_adjoint = extend(adjoint)
    balance = jnp.zeros(primal.shape, jnp.float32)
    weight = jnp.zeros(primal.shape, jnp.float32)
    for along in (1, 2, 3):
        part_balance, part_weight = axis_terms(ext_primal, ext_adjoint, along, (1, 2, 3))
        balance = balance + part_balance
        weight = weight + part_weight
    indicator = jnp.abs(jnp.sum(weight * balance, axis=0))
    block_mean = indicator.reshape(NBR, BLK, NBA, BLK, NBX, BLK).mean(axis=(1, 3, 5))
    beside_all = jnp.mean(jnp.take(block_mean.reshape(-1), neighbor_list), axis=-1)
    smooth = 0.5 * block_mean + 0.5 * beside_all
    per_rad = CR // BLK
    per_azi = CA // BLK
    per_ax = CX // BLK
    rad_home = (jnp.arange(NBR, dtype=jnp.int32) // per_rad)[:, None, None]
    azi_home = (jnp.arange(NBA, dtype=jnp.int32) // per_azi)[None, :, None]
    ax_home = (jnp.arange(NBX, dtype=jnp.int32) // per_ax)[None, None, :]
    home = (rad_home * N_AZI + azi_home) * N_AX + ax_home
    moved = (owner_map != home).astype(jnp.float32)
    block_cost = smooth * (1.0 + 7.0 * refine_flag.astype(jnp.float32)) + 0.25 * migrate_weight.astype(jnp.float32) * moved
    devices = N_RAD * N_AZI * N_AX
    totals = jax.ops.segment_sum(block_cost.reshape(-1), owner_map.reshape(-1), num_segments=devices)
    owner_load = (totals / (NBLK // devices)).reshape(N_RAD, N_AZI, N_AX)
    return indicator, block_cost, owner_load
```

```python
import functools
import jax
import jax.numpy as jnp
from jax import lax
from jax.experimental import pallas as pl
from jax.experimental.pallas import tpu as pltpu
from jax.sharding import PartitionSpec as P

BLK = 16
AXES = ("rad", "azi", "ax")
MESH = pl.DeviceIdType.MESH


def gather_kernel(sizes, x_ref, o_ref, lsem, ssem, rsem):
    n_r, n_a, n_x = sizes
    r = lax.axis_index("rad")
    a = lax.axis_index("azi")
    x = lax.axis_index("ax")

    def at(rr, aa, xx):
        return (rr, aa, xx)

    stages = [
        (n_x, lambda k: at(r, a, lax.rem(x + k, n_x)), lambda k: at(r, a, lax.rem(x + n_x - k, n_x))),
        (n_a, lambda k: at(r, lax.rem(a + k, n_a), x), lambda k: at(r, lax.rem(a + n_a - k, n_a), x)),
        (n_r, lambda k: at(lax.rem(r + k, n_r), a, x), lambda k: at(lax.rem(r + n_r - k, n_r), a, x)),
    ]
    barrier = pltpu.get_barrier_semaphore()
    count = 0
    for n, to, _ in stages:
        for k in range(1, n):
            pl.semaphore_signal(barrier, 1, device_id=to(k), device_id_type=MESH)
            count += 1
    pl.semaphore_wait(barrier, count)

    def region(stage, dev):
        rr, aa, xx = dev
        if stage == 0:
            return o_ref.at[pl.ds(rr, 1), pl.ds(aa, 1), pl.ds(xx, 1)]
        if stage == 1:
            return o_ref.at[pl.ds(rr, 1), pl.ds(aa, 1)]
        return o_ref.at[pl.ds(rr, 1)]

    local = pltpu.make_async_copy(x_ref, region(0, (r, a, x)), lsem)
    local.start()
    sends = []
    slot = 0
    for stage, (n, to, frm) in enumerate(stages):
        src = x_ref if stage == 0 else region(stage, (r, a, x))
        first = slot
        for k in range(1, n):
            copy = pltpu.make_async_remote_copy(
                src_ref=src,
                dst_ref=region(stage, (r, a, x)),
                send_sem=ssem.at[slot],
                recv_sem=rsem.at[slot],
                device_id=to(k),
                device_id_type=MESH,
            )
            copy.start()
            sends.append(copy)
            slot += 1
        slot = first
        for k in range(1, n):
            incoming = pltpu.make_async_remote_copy(
                src_ref=src,
                dst_ref=region(stage, frm(k)),
                send_sem=ssem.at[slot],
                recv_sem=rsem.at[slot],
                device_id=frm(k),
                device_id_type=MESH,
            )
            incoming.wait_recv()
            slot += 1
        if stage == 0:
            local.wait()
    for copy in sends:
        copy.wait_send()


def gather_all(values, cid):
    n_r, n_a, n_x = (lax.axis_size(ax) for ax in AXES)
    width = values.shape[0]
    links = (n_r - 1) + (n_a - 1) + (n_x - 1)
    out = pl.pallas_call(
        functools.partial(gather_kernel, (n_r, n_a, n_x)),
        out_shape=jax.ShapeDtypeStruct((n_r, n_a, n_x, width), jnp.float32),
        in_specs=[pl.BlockSpec(memory_space=pltpu.VMEM)],
        out_specs=pl.BlockSpec(memory_space=pltpu.VMEM),
        scratch_shapes=[
            pltpu.SemaphoreType.DMA(()),
            pltpu.SemaphoreType.DMA((links,)),
            pltpu.SemaphoreType.DMA((links,)),
        ],
        compiler_params=pltpu.CompilerParams(collective_id=cid, has_side_effects=True),
    )(values.reshape(1, 1, 1, width))
    return out.reshape(-1)


def halo_pair(parts, axis, dim, periodic):
    count = lax.axis_size(axis)
    forward = [(i, i + 1) for i in range(count - 1)]
    if periodic:
        forward.append((count - 1, 0))
    backward = [(target, source) for source, target in forward]
    tails = tuple(lax.slice_in_dim(p, p.shape[dim] - 2, None, axis=dim) for p in parts)
    heads = tuple(lax.slice_in_dim(p, 0, 2, axis=dim) for p in parts)
    low = lax.ppermute(tails, axis, forward)
    high = lax.ppermute(heads, axis, backward)
    return tuple(jnp.concatenate([lo, p, hi], axis=dim) for lo, p, hi in zip(low, parts, high))


def euler_flux(face_state, along):
    density = face_state[0]
    momenta = face_state[1:4]
    energy = face_state[4]
    velocity = momenta[along] / density
    kinetic = (
        0.5
        * (momenta[0] * momenta[0] + momenta[1] * momenta[1] + momenta[2] * momenta[2])
        / density
    )
    pressure = 0.4 * (energy - kinetic)
    columns = [
        momenta[along],
        momenta[0] * velocity,
        momenta[1] * velocity,
        momenta[2] * velocity,
        (energy + pressure) * velocity,
    ]
    columns[1 + along] = columns[1 + along] + pressure
    return jnp.stack(columns)


def axis_terms(ext_p, ext_a, dim):
    length = ext_p.shape[dim] - 4
    win = lambda e, s, c: lax.slice_in_dim(e, s, s + c, axis=dim)
    high = (7.0 * win(ext_p, 1, length + 1) - win(ext_p, 0, length + 1)) / 12.0
    low = (7.0 * win(ext_p, 2, length + 1) - win(ext_p, 3, length + 1)) / 12.0
    fluxes = euler_flux(high + low, dim - 1)
    balance = win(fluxes, 1, length) - win(fluxes, 0, length)
    fourth = (
        win(ext_a, 0, length)
        - 4.0 * win(ext_a, 1, length)
        + 6.0 * win(ext_a, 2, length)
        - 4.0 * win(ext_a, 3, length)
        + win(ext_a, 4, length)
    ) / 12.0
    return balance, fourth


def on_device(primal, adjoint, refine_flag, owner_map, migrate_weight, neighbor_list):
    ext = {
        1: halo_pair((primal, adjoint), "rad", 1, False),
        2: halo_pair((primal, adjoint), "azi", 2, True),
        3: halo_pair((primal, adjoint), "ax", 3, False),
    }
    balance = None
    weight = None
    for along in (1, 2, 3):
        part_balance, part_weight = axis_terms(ext[along][0], ext[along][1], along)
        balance = part_balance if balance is None else balance + part_balance
        weight = part_weight if weight is None else weight + part_weight
    indicator = jnp.abs(jnp.sum(weight * balance, axis=0))
    rows_rad, rows_azi, rows_ax = indicator.shape
    per_rad = rows_rad // BLK
    per_azi = rows_azi // BLK
    per_ax = rows_ax // BLK
    block_mean = indicator.reshape(per_rad, BLK, per_azi, BLK, per_ax, BLK).mean(axis=(1, 3, 5))
    all_means = gather_all(block_mean.reshape(-1), 0)
    size_rad = lax.axis_size("rad")
    size_azi = lax.axis_size("azi")
    size_ax = lax.axis_size("ax")
    blocks_azi = per_azi * size_azi
    blocks_ax = per_ax * size_ax
    block_rad = neighbor_list // (blocks_azi * blocks_ax)
    block_azi = neighbor_list // blocks_ax % blocks_azi
    block_ax = neighbor_list % blocks_ax
    owner_dev = (
        block_rad // per_rad * size_azi + block_azi // per_azi
    ) * size_ax + block_ax // per_ax
    local_pos = (block_rad % per_rad * per_azi + block_azi % per_azi) * per_ax + block_ax % per_ax
    position = owner_dev * (per_rad * per_azi * per_ax) + local_pos
    beside_all = jnp.mean(jnp.take(all_means, position), axis=-1)
    smooth = 0.5 * block_mean + 0.5 * beside_all
    own_index = (
        lax.axis_index("rad") * size_azi + lax.axis_index("azi")
    ) * size_ax + lax.axis_index("ax")
    moved = (owner_map != own_index).astype(jnp.float32)
    block_cost = (
        smooth * (1.0 + 7.0 * refine_flag.astype(jnp.float32))
        + 0.25 * migrate_weight.astype(jnp.float32) * moved
    )
    width = block_cost.size
    payload = jnp.concatenate([block_cost.reshape(-1), owner_map.reshape(-1).astype(jnp.float32)])
    gathered = gather_all(payload, 1).reshape(-1, 2 * width)
    cost_all = gathered[:, :width]
    owner_all = gathered[:, width:]
    total = jnp.sum(jnp.where(owner_all == own_index.astype(jnp.float32), cost_all, 0.0))
    owner_load = (total / (per_rad * per_azi * per_ax)).reshape(1, 1, 1)
    return (indicator, block_cost, owner_load)


def solution(mesh):
    return jax.shard_map(
        on_device,
        mesh=mesh,
        in_specs=(
            P(None, "rad", "azi", "ax"),
            P(None, "rad", "azi", "ax"),
            P("rad", "azi", "ax"),
            P("rad", "azi", "ax"),
            P("rad", "azi", "ax"),
            P("rad", "azi", "ax", None),
        ),
        out_specs=(P("rad", "azi", "ax"), P("rad", "azi", "ax"), P("rad", "azi", "ax")),
        check_vma=False,
    )
```

```python
import functools
import jax
import jax.numpy as jnp
from jax import lax
from jax.experimental import pallas as pl
from jax.experimental.pallas import tpu as pltpu
from jax.sharding import PartitionSpec as P

BLK = 16
AXES = ("rad", "azi", "ax")
MESH = pl.DeviceIdType.MESH


def gather_kernel(sizes, x_ref, o_ref, lsem, ssem, rsem):
    n_r, n_a, n_x = sizes
    r = lax.axis_index("rad")
    a = lax.axis_index("azi")
    x = lax.axis_index("ax")

    def at(rr, aa, xx):
        return (rr, aa, xx)

    stages = [
        (n_x, lambda k: at(r, a, lax.rem(x + k, n_x)), lambda k: at(r, a, lax.rem(x + n_x - k, n_x))),
        (n_a, lambda k: at(r, lax.rem(a + k, n_a), x), lambda k: at(r, lax.rem(a + n_a - k, n_a), x)),
        (n_r, lambda k: at(lax.rem(r + k, n_r), a, x), lambda k: at(lax.rem(r + n_r - k, n_r), a, x)),
    ]
    barrier = pltpu.get_barrier_semaphore()
    count = 0
    for n, to, _ in stages:
        for k in range(1, n):
            pl.semaphore_signal(barrier, 1, device_id=to(k), device_id_type=MESH)
            count += 1
    pl.semaphore_wait(barrier, count)

    def region(stage, dev):
        rr, aa, xx = dev
        if stage == 0:
            return o_ref.at[pl.ds(rr, 1), pl.ds(aa, 1), pl.ds(xx, 1)]
        if stage == 1:
            return o_ref.at[pl.ds(rr, 1), pl.ds(aa, 1)]
        return o_ref.at[pl.ds(rr, 1)]

    local = pltpu.make_async_copy(x_ref, region(0, (r, a, x)), lsem)
    local.start()
    sends = []
    slot = 0
    for stage, (n, to, frm) in enumerate(stages):
        src = x_ref if stage == 0 else region(stage, (r, a, x))
        first = slot
        for k in range(1, n):
            copy = pltpu.make_async_remote_copy(
                src_ref=src,
                dst_ref=region(stage, (r, a, x)),
                send_sem=ssem.at[slot],
                recv_sem=rsem.at[slot],
                device_id=to(k),
                device_id_type=MESH,
            )
            copy.start()
            sends.append(copy)
            slot += 1
        slot = first
        for k in range(1, n):
            incoming = pltpu.make_async_remote_copy(
                src_ref=src,
                dst_ref=region(stage, frm(k)),
                send_sem=ssem.at[slot],
                recv_sem=rsem.at[slot],
                device_id=frm(k),
                device_id_type=MESH,
            )
            incoming.wait_recv()
            slot += 1
        if stage == 0:
            local.wait()
    for copy in sends:
        copy.wait_send()


def gather_all(values, cid):
    n_r, n_a, n_x = (lax.axis_size(ax) for ax in AXES)
    width = values.shape[0]
    links = (n_r - 1) + (n_a - 1) + (n_x - 1)
    out = pl.pallas_call(
        functools.partial(gather_kernel, (n_r, n_a, n_x)),
        out_shape=jax.ShapeDtypeStruct((n_r, n_a, n_x, width), jnp.float32),
        in_specs=[pl.BlockSpec(memory_space=pltpu.VMEM)],
        out_specs=pl.BlockSpec(memory_space=pltpu.VMEM),
        scratch_shapes=[
            pltpu.SemaphoreType.DMA(()),
            pltpu.SemaphoreType.DMA((links,)),
            pltpu.SemaphoreType.DMA((links,)),
        ],
        compiler_params=pltpu.CompilerParams(collective_id=cid, has_side_effects=True),
    )(values.reshape(1, 1, 1, width))
    return out.reshape(-1)


def dense(x):
    return x.reshape(-1, 128)


def exchange(tail, head, axis, periodic):
    count = lax.axis_size(axis)
    forward = [(i, i + 1) for i in range(count - 1)]
    if periodic:
        forward.append((count - 1, 0))
    backward = [(target, source) for source, target in forward]
    low = lax.ppermute(dense(tail), axis, forward).reshape(tail.shape)
    high = lax.ppermute(dense(head), axis, backward).reshape(head.shape)
    return low, high


def flux_pair(state_lo, state_hi, along):
    return [h - l for h, l in zip(euler_flux(state_hi, along), euler_flux(state_lo, along))]


def euler_flux(s, along):
    density, m0, m1, m2, energy = s
    momenta = (m0, m1, m2)
    inv = 1.0 / density
    velocity = momenta[along] * inv
    kinetic = 0.5 * (m0 * m0 + m1 * m1 + m2 * m2) * inv
    pressure = 0.4 * (energy - kinetic)
    columns = [momenta[along], m0 * velocity, m1 * velocity, m2 * velocity, (energy + pressure) * velocity]
    columns[1 + along] = columns[1 + along] + pressure
    return columns


def faces(um2, um1, u, up1, up2):
    lower = (7.0 * um1 - um2) / 12.0 + (7.0 * u - up1) / 12.0
    upper = (7.0 * u - um1) / 12.0 + (7.0 * up1 - up2) / 12.0
    return lower, upper


def fourth(zm2, zm1, z, zp1, zp2):
    return (zm2 - 4.0 * zm1 + 6.0 * z - 4.0 * zp1 + zp2) / 12.0


def stencil_kernel(p_hbm, a_hbm, rl, rh, al, ah, xl, xh, out_ref, ep, ea, sems):
    fields, rows = ep.shape[0], ep.shape[1] - 4
    copies = [
        pltpu.make_async_copy(p_hbm, ep.at[:, pl.ds(2, rows)], sems.at[0]),
        pltpu.make_async_copy(a_hbm, ea.at[:, pl.ds(2, rows)], sems.at[1]),
    ]
    for c in copies:
        c.start()
    ep[:, 0:2] = rl[0]
    ea[:, 0:2] = rl[1]
    ep[:, rows + 2:rows + 4] = rh[0]
    ea[:, rows + 2:rows + 4] = rh[1]
    for c in copies:
        c.wait()
    n_a, n_x = ep.shape[2], ep.shape[3]
    sub = lax.broadcasted_iota(jnp.int32, (n_a, n_x), 0)
    lane = lax.broadcasted_iota(jnp.int32, (n_a, n_x), 1)

    def shifted_azi(u, lo, hi):
        um1 = jnp.where(sub == 0, jnp.broadcast_to(lo[1:2], u.shape), pltpu.roll(u, 1, 0))
        um2 = jnp.where(sub == 0, jnp.broadcast_to(lo[0:1], u.shape),
                        jnp.where(sub == 1, jnp.broadcast_to(lo[1:2], u.shape), pltpu.roll(u, 2, 0)))
        up1 = jnp.where(sub == n_a - 1, jnp.broadcast_to(hi[0:1], u.shape), pltpu.roll(u, n_a - 1, 0))
        up2 = jnp.where(sub == n_a - 1, jnp.broadcast_to(hi[1:2], u.shape),
                        jnp.where(sub == n_a - 2, jnp.broadcast_to(hi[0:1], u.shape), pltpu.roll(u, n_a - 2, 0)))
        return um2, um1, u, up1, up2

    def shifted_ax(u, lo, hi):
        um1 = jnp.where(lane == 0, jnp.broadcast_to(lo[:, 1:2], u.shape), pltpu.roll(u, 1, 1))
        um2 = jnp.where(lane == 0, jnp.broadcast_to(lo[:, 0:1], u.shape),
                        jnp.where(lane == 1, jnp.broadcast_to(lo[:, 1:2], u.shape), pltpu.roll(u, 2, 1)))
        up1 = jnp.where(lane == n_x - 1, jnp.broadcast_to(hi[:, 0:1], u.shape), pltpu.roll(u, n_x - 1, 1))
        up2 = jnp.where(lane == n_x - 1, jnp.broadcast_to(hi[:, 1:2], u.shape),
                        jnp.where(lane == n_x - 2, jnp.broadcast_to(hi[:, 0:1], u.shape), pltpu.roll(u, n_x - 2, 1)))
        return um2, um1, u, up1, up2

    def row(r, carry):
        balance = None
        weight = None
        lo_s, hi_s = [], []
        w = []
        for f in range(fields):
            e = [ep[f, r + k] for k in range(5)]
            lo, hi = faces(*e)
            lo_s.append(lo)
            hi_s.append(hi)
            w.append(fourth(*[ea[f, r + k] for k in range(5)]))
        balance = flux_pair(lo_s, hi_s, 0)
        weight = w
        lo_s, hi_s, w = [], [], []
        for f in range(fields):
            lo, hi = faces(*shifted_azi(ep[f, r + 2], al[0, f, r], ah[0, f, r]))
            lo_s.append(lo)
            hi_s.append(hi)
            w.append(fourth(*shifted_azi(ea[f, r + 2], al[1, f, r], ah[1, f, r])))
        part = flux_pair(lo_s, hi_s, 1)
        balance = [b + p for b, p in zip(balance, part)]
        weight = [a + b for a, b in zip(weight, w)]
        lo_s, hi_s, w = [], [], []
        for f in range(fields):
            lo, hi = faces(*shifted_ax(ep[f, r + 2], xl[0, f, r], xh[0, f, r]))
            lo_s.append(lo)
            hi_s.append(hi)
            w.append(fourth(*shifted_ax(ea[f, r + 2], xl[1, f, r], xh[1, f, r])))
        part = flux_pair(lo_s, hi_s, 2)
        balance = [b + p for b, p in zip(balance, part)]
        weight = [a + b for a, b in zip(weight, w)]
        total = weight[0] * balance[0]
        for f in range(1, fields):
            total = total + weight[f] * balance[f]
        out_ref[r] = jnp.abs(total)
        return carry

    lax.fori_loop(0, rows, row, 0)


def stencil(primal, adjoint, rl, rh, al, ah, xl, xh):
    fields, rows, n_a, n_x = primal.shape
    vmem = pl.BlockSpec(memory_space=pltpu.VMEM)
    anywhere = pl.BlockSpec(memory_space=pl.ANY)
    return pl.pallas_call(
        stencil_kernel,
        out_shape=jax.ShapeDtypeStruct((rows, n_a, n_x), jnp.float32),
        in_specs=[anywhere, anywhere] + [vmem] * 6,
        out_specs=vmem,
        scratch_shapes=[
            pltpu.VMEM((fields, rows + 4, n_a, n_x), jnp.float32),
            pltpu.VMEM((fields, rows + 4, n_a, n_x), jnp.float32),
            pltpu.SemaphoreType.DMA((2,)),
        ],
        compiler_params=pltpu.CompilerParams(vmem_limit_bytes=48 * 1024 * 1024),
    )(primal, adjoint, rl, rh, al, ah, xl, xh)


def on_device(primal, adjoint, refine_flag, owner_map, migrate_weight, neighbor_list):
    both = jnp.stack([primal, adjoint])
    rl, rh = exchange(both[:, :, -2:], both[:, :, :2], "rad", False)
    al, ah = exchange(both[:, :, :, -2:], both[:, :, :, :2], "azi", True)
    xl, xh = exchange(
        jnp.swapaxes(both[..., -2:], -1, -2), jnp.swapaxes(both[..., :2], -1, -2), "ax", False
    )
    xl, xh = jnp.swapaxes(xl, -1, -2), jnp.swapaxes(xh, -1, -2)
    indicator = stencil(primal, adjoint, rl, rh, al, ah, xl, xh)
    rows_rad, rows_azi, rows_ax = indicator.shape
    per_rad = rows_rad // BLK
    per_azi = rows_azi // BLK
    per_ax = rows_ax // BLK
    block_mean = indicator.reshape(per_rad, BLK, per_azi, BLK, per_ax, BLK).mean(axis=(1, 3, 5))
    all_means = gather_all(block_mean.reshape(-1), 0)
    size_rad = lax.axis_size("rad")
    size_azi = lax.axis_size("azi")
    size_ax = lax.axis_size("ax")
    blocks_azi = per_azi * size_azi
    blocks_ax = per_ax * size_ax
    block_rad = neighbor_list // (blocks_azi * blocks_ax)
    block_azi = neighbor_list // blocks_ax % blocks_azi
    block_ax = neighbor_list % blocks_ax
    owner_dev = (
        block_rad // per_rad * size_azi + block_azi // per_azi
    ) * size_ax + block_ax // per_ax
    local_pos = (block_rad % per_rad * per_azi + block_azi % per_azi) * per_ax + block_ax % per_ax
    position = owner_dev * (per_rad * per_azi * per_ax) + local_pos
    beside_all = jnp.mean(jnp.take(all_means, position), axis=-1)
    smooth = 0.5 * block_mean + 0.5 * beside_all
    own_index = (
        lax.axis_index("rad") * size_azi + lax.axis_index("azi")
    ) * size_ax + lax.axis_index("ax")
    moved = (owner_map != own_index).astype(jnp.float32)
    block_cost = (
        smooth * (1.0 + 7.0 * refine_flag.astype(jnp.float32))
        + 0.25 * migrate_weight.astype(jnp.float32) * moved
    )
    width = block_cost.size
    payload = jnp.concatenate([block_cost.reshape(-1), owner_map.reshape(-1).astype(jnp.float32)])
    gathered = gather_all(payload, 1).reshape(-1, 2 * width)
    cost_all = gathered[:, :width]
    owner_all = gathered[:, width:]
    total = jnp.sum(jnp.where(owner_all == own_index.astype(jnp.float32), cost_all, 0.0))
    owner_load = (total / (per_rad * per_azi * per_ax)).reshape(1, 1, 1)
    return (indicator, block_cost, owner_load)


def solution(mesh):
    return jax.shard_map(
        on_device,
        mesh=mesh,
        in_specs=(
            P(None, "rad", "azi", "ax"),
            P(None, "rad", "azi", "ax"),
            P("rad", "azi", "ax"),
            P("rad", "azi", "ax"),
            P("rad", "azi", "ax"),
            P("rad", "azi", "ax", None),
        ),
        out_specs=(P("rad", "azi", "ax"), P("rad", "azi", "ax"), P("rad", "azi", "ax")),
        check_vma=False,
    )
```

```python
import functools
import jax
import jax.numpy as jnp
from jax import lax
from jax.experimental import pallas as pl
from jax.experimental.pallas import tpu as pltpu
from jax.sharding import PartitionSpec as P

BLK = 16
AXES = ("rad", "azi", "ax")
MESH = pl.DeviceIdType.MESH


def gather_kernel(sizes, x_ref, o_ref, lsem, ssem, rsem):
    n_r, n_a, n_x = sizes
    r = lax.axis_index("rad")
    a = lax.axis_index("azi")
    x = lax.axis_index("ax")

    def at(rr, aa, xx):
        return (rr, aa, xx)

    stages = [
        (n_x, lambda k: at(r, a, lax.rem(x + k, n_x)), lambda k: at(r, a, lax.rem(x + n_x - k, n_x))),
        (n_a, lambda k: at(r, lax.rem(a + k, n_a), x), lambda k: at(r, lax.rem(a + n_a - k, n_a), x)),
        (n_r, lambda k: at(lax.rem(r + k, n_r), a, x), lambda k: at(lax.rem(r + n_r - k, n_r), a, x)),
    ]
    barrier = pltpu.get_barrier_semaphore()
    count = 0
    for n, to, _ in stages:
        for k in range(1, n):
            pl.semaphore_signal(barrier, 1, device_id=to(k), device_id_type=MESH)
            count += 1
    pl.semaphore_wait(barrier, count)

    def region(stage, dev):
        rr, aa, xx = dev
        if stage == 0:
            return o_ref.at[pl.ds(rr, 1), pl.ds(aa, 1), pl.ds(xx, 1)]
        if stage == 1:
            return o_ref.at[pl.ds(rr, 1), pl.ds(aa, 1)]
        return o_ref.at[pl.ds(rr, 1)]

    local = pltpu.make_async_copy(x_ref, region(0, (r, a, x)), lsem)
    local.start()
    sends = []
    slot = 0
    for stage, (n, to, frm) in enumerate(stages):
        src = x_ref if stage == 0 else region(stage, (r, a, x))
        first = slot
        for k in range(1, n):
            copy = pltpu.make_async_remote_copy(
                src_ref=src,
                dst_ref=region(stage, (r, a, x)),
                send_sem=ssem.at[slot],
                recv_sem=rsem.at[slot],
                device_id=to(k),
                device_id_type=MESH,
            )
            copy.start()
            sends.append(copy)
            slot += 1
        slot = first
        for k in range(1, n):
            incoming = pltpu.make_async_remote_copy(
                src_ref=src,
                dst_ref=region(stage, frm(k)),
                send_sem=ssem.at[slot],
                recv_sem=rsem.at[slot],
                device_id=frm(k),
                device_id_type=MESH,
            )
            incoming.wait_recv()
            slot += 1
        if stage == 0:
            local.wait()
    for copy in sends:
        copy.wait_send()


def gather_all(values, cid):
    n_r, n_a, n_x = (lax.axis_size(ax) for ax in AXES)
    width = values.shape[0]
    links = (n_r - 1) + (n_a - 1) + (n_x - 1)
    out = pl.pallas_call(
        functools.partial(gather_kernel, (n_r, n_a, n_x)),
        out_shape=jax.ShapeDtypeStruct((n_r, n_a, n_x, width), jnp.float32),
        in_specs=[pl.BlockSpec(memory_space=pltpu.VMEM)],
        out_specs=pl.BlockSpec(memory_space=pltpu.VMEM),
        scratch_shapes=[
            pltpu.SemaphoreType.DMA(()),
            pltpu.SemaphoreType.DMA((links,)),
            pltpu.SemaphoreType.DMA((links,)),
        ],
        compiler_params=pltpu.CompilerParams(collective_id=cid, has_side_effects=True),
    )(values.reshape(1, 1, 1, width))
    return out.reshape(-1)


def dense(x):
    return x.reshape(-1, 128)


def exchange(tail, head, axis, periodic):
    count = lax.axis_size(axis)
    forward = [(i, i + 1) for i in range(count - 1)]
    if periodic:
        forward.append((count - 1, 0))
    backward = [(target, source) for source, target in forward]
    low = lax.ppermute(dense(tail), axis, forward).reshape(tail.shape)
    high = lax.ppermute(dense(head), axis, backward).reshape(head.shape)
    return low, high


def flux_pair(state_lo, state_hi, along):
    return [h - l for h, l in zip(euler_flux(state_hi, along), euler_flux(state_lo, along))]


def euler_flux(s, along):
    density, m0, m1, m2, energy = s
    momenta = (m0, m1, m2)
    inv = 1.0 / density
    velocity = momenta[along] * inv
    kinetic = 0.5 * (m0 * m0 + m1 * m1 + m2 * m2) * inv
    pressure = 0.4 * (energy - kinetic)
    columns = [momenta[along], m0 * velocity, m1 * velocity, m2 * velocity, (energy + pressure) * velocity]
    columns[1 + along] = columns[1 + along] + pressure
    return columns


def faces(um2, um1, u, up1, up2):
    lower = (7.0 * um1 - um2) / 12.0 + (7.0 * u - up1) / 12.0
    upper = (7.0 * u - um1) / 12.0 + (7.0 * up1 - up2) / 12.0
    return lower, upper


def fourth(zm2, zm1, z, zp1, zp2):
    return (zm2 - 4.0 * zm1 + 6.0 * z - 4.0 * zp1 + zp2) / 12.0


def stencil_kernel(p_hbm, a_hbm, out_ref, e, az_send, az_recv, az_exp, x_send, x_recv, xt, sems, ssem, rsem):
    _, fields, ext_rows, n_a, n_x = e.shape
    rows = ext_rows - 4
    n_r_dev, n_a_dev, n_x_dev = (lax.axis_size(ax) for ax in AXES)
    me_r, me_a, me_x = (lax.axis_index(ax) for ax in AXES)
    has_r_lo, has_r_hi = me_r > 0, me_r < n_r_dev - 1
    has_x_lo, has_x_hi = me_x > 0, me_x < n_x_dev - 1
    r_lo, r_hi = (me_r - 1, me_a, me_x), (me_r + 1, me_a, me_x)
    a_lo = (me_r, lax.rem(me_a + n_a_dev - 1, n_a_dev), me_x)
    a_hi = (me_r, lax.rem(me_a + 1, n_a_dev), me_x)
    x_lo, x_hi = (me_r, me_a, me_x - 1), (me_r, me_a, me_x + 1)

    loads = [
        pltpu.make_async_copy(p_hbm, e.at[0, :, pl.ds(2, rows)], sems.at[0]),
        pltpu.make_async_copy(a_hbm, e.at[1, :, pl.ds(2, rows)], sems.at[1]),
    ]
    for c in loads:
        c.start()

    barrier = pltpu.get_barrier_semaphore()
    for cond, dev in ((has_r_lo, r_lo), (has_r_hi, r_hi), (has_x_lo, x_lo), (has_x_hi, x_hi)):
        @pl.when(cond)
        def _():
            pl.semaphore_signal(barrier, 1, device_id=dev, device_id_type=MESH)
    pl.semaphore_signal(barrier, 1, device_id=a_lo, device_id_type=MESH)
    pl.semaphore_signal(barrier, 1, device_id=a_hi, device_id_type=MESH)
    count = 2 + sum(c.astype(jnp.int32) for c in (has_r_lo, has_r_hi, has_x_lo, has_x_hi))
    pl.semaphore_wait(barrier, count)

    x_recv[:, x_send.shape[1]:, :] = jnp.zeros((2, x_recv.shape[1] - x_send.shape[1], x_recv.shape[2]), jnp.float32)
    x_send[:, 4 * fields:, :] = jnp.zeros((2, x_send.shape[1] - 4 * fields, x_send.shape[2]), jnp.float32)
    for c in loads:
        c.wait()

    for k in range(2):
        for f in range(fields):
            for r in range(rows):
                row = ((k * fields + f) * rows + r) * 2
                az_send[0, row:row + 2, :] = e[k, f, 2 + r, 0:2, :]
                az_send[1, row:row + 2, :] = e[k, f, 2 + r, n_a - 2:n_a, :]
            plane = e[k, f, 2:2 + rows].reshape(rows * n_a, n_x)
            cols = plane.T
            row = (k * fields + f) * 2
            x_send[0, row:row + 2, :] = cols[0:2]
            x_send[1, row:row + 2, :] = cols[n_x - 2:n_x]

    def remote(src, dst, i, dev):
        return pltpu.make_async_remote_copy(
            src_ref=src, dst_ref=dst, send_sem=ssem.at[i], recv_sem=rsem.at[i],
            device_id=dev, device_id_type=MESH,
        )

    n_kx = x_send.shape[1]
    sends = [
        (has_r_hi, remote(e.at[:, :, pl.ds(rows, 2)], e.at[:, :, pl.ds(0, 2)], 0, r_hi)),
        (has_r_lo, remote(e.at[:, :, pl.ds(2, 2)], e.at[:, :, pl.ds(rows + 2, 2)], 1, r_lo)),
        (None, remote(az_send.at[1], az_recv.at[0], 2, a_hi)),
        (None, remote(az_send.at[0], az_recv.at[1], 3, a_lo)),
        (has_x_hi, remote(x_send.at[1], x_recv.at[0, pl.ds(0, n_kx)], 4, x_hi)),
        (has_x_lo, remote(x_send.at[0], x_recv.at[1, pl.ds(0, n_kx)], 5, x_lo)),
    ]
    recvs = [
        (has_r_lo, remote(e.at[:, :, pl.ds(rows, 2)], e.at[:, :, pl.ds(0, 2)], 0, r_lo)),
        (has_r_hi, remote(e.at[:, :, pl.ds(2, 2)], e.at[:, :, pl.ds(rows + 2, 2)], 1, r_hi)),
        (None, remote(az_send.at[1], az_recv.at[0], 2, a_lo)),
        (None, remote(az_send.at[0], az_recv.at[1], 3, a_hi)),
        (has_x_lo, remote(x_send.at[1], x_recv.at[0, pl.ds(0, n_kx)], 4, x_lo)),
        (has_x_hi, remote(x_send.at[0], x_recv.at[1, pl.ds(0, n_kx)], 5, x_hi)),
    ]

    def when(cond, fn):
        if cond is None:
            fn()
        else:
            pl.when(cond)(fn)

    for cond, c in sends:
        when(cond, c.start)

    @pl.when(jnp.logical_not(has_r_lo))
    def _():
        e[:, :, 0:2] = jnp.zeros((2, fields, 2, n_a, n_x), jnp.float32)

    @pl.when(jnp.logical_not(has_r_hi))
    def _():
        e[:, :, rows + 2:rows + 4] = jnp.zeros((2, fields, 2, n_a, n_x), jnp.float32)

    @pl.when(jnp.logical_not(has_x_lo))
    def _():
        x_recv[0, 0:n_kx, :] = jnp.zeros((n_kx, x_recv.shape[2]), jnp.float32)

    @pl.when(jnp.logical_not(has_x_hi))
    def _():
        x_recv[1, 0:n_kx, :] = jnp.zeros((n_kx, x_recv.shape[2]), jnp.float32)

    for cond, c in recvs:
        when(cond, c.wait_recv)

    for side in range(2):
        xt[side] = x_recv[side].T
        for k in range(2):
            for f in range(fields):
                for r in range(rows):
                    row = ((k * fields + f) * rows + r) * 2
                    az_exp[side, r, k * fields + f, 0:2, :] = az_recv[side, row:row + 2, :]

    sub = lax.broadcasted_iota(jnp.int32, (n_a, n_x), 0)
    lane = lax.broadcasted_iota(jnp.int32, (n_a, n_x), 1)

    def shifted_azi(u, lo, hi):
        um1 = jnp.where(sub == 0, jnp.broadcast_to(lo[1:2], u.shape), pltpu.roll(u, 1, 0))
        um2 = jnp.where(sub == 0, jnp.broadcast_to(lo[0:1], u.shape),
                        jnp.where(sub == 1, jnp.broadcast_to(lo[1:2], u.shape), pltpu.roll(u, 2, 0)))
        up1 = jnp.where(sub == n_a - 1, jnp.broadcast_to(hi[0:1], u.shape), pltpu.roll(u, n_a - 1, 0))
        up2 = jnp.where(sub == n_a - 1, jnp.broadcast_to(hi[1:2], u.shape),
                        jnp.where(sub == n_a - 2, jnp.broadcast_to(hi[0:1], u.shape), pltpu.roll(u, n_a - 2, 0)))
        return um2, um1, u, up1, up2

    def shifted_ax(u, lo0, lo1, hi0, hi1):
        um1 = jnp.where(lane == 0, jnp.broadcast_to(lo1, u.shape), pltpu.roll(u, 1, 1))
        um2 = jnp.where(lane == 0, jnp.broadcast_to(lo0, u.shape),
                        jnp.where(lane == 1, jnp.broadcast_to(lo1, u.shape), pltpu.roll(u, 2, 1)))
        up1 = jnp.where(lane == n_x - 1, jnp.broadcast_to(hi0, u.shape), pltpu.roll(u, n_x - 1, 1))
        up2 = jnp.where(lane == n_x - 1, jnp.broadcast_to(hi1, u.shape),
                        jnp.where(lane == n_x - 2, jnp.broadcast_to(hi0, u.shape), pltpu.roll(u, n_x - 2, 1)))
        return um2, um1, u, up1, up2

    def row_body(r, carry):
        base = pl.multiple_of(r * n_a, n_a)
        xlo = xt[0, pl.ds(base, n_a), :]
        xhi = xt[1, pl.ds(base, n_a), :]
        lo_s, hi_s, w = [], [], []
        for f in range(fields):
            lo, hi = faces(*[e[0, f, r + k] for k in range(5)])
            lo_s.append(lo)
            hi_s.append(hi)
            w.append(fourth(*[e[1, f, r + k] for k in range(5)]))
        balance = flux_pair(lo_s, hi_s, 0)
        weight = w
        lo_s, hi_s, w = [], [], []
        for f in range(fields):
            lo, hi = faces(*shifted_azi(e[0, f, r + 2], az_exp[0, r, f], az_exp[1, r, f]))
            lo_s.append(lo)
            hi_s.append(hi)
            w.append(fourth(*shifted_azi(e[1, f, r + 2], az_exp[0, r, fields + f], az_exp[1, r, fields + f])))
        part = flux_pair(lo_s, hi_s, 1)
        balance = [b + p for b, p in zip(balance, part)]
        weight = [a + b for a, b in zip(weight, w)]
        lo_s, hi_s, w = [], [], []
        for f in range(fields):
            cp, ca = 2 * f, 2 * (fields + f)
            lo, hi = faces(*shifted_ax(e[0, f, r + 2], xlo[:, cp:cp + 1], xlo[:, cp + 1:cp + 2],
                                       xhi[:, cp:cp + 1], xhi[:, cp + 1:cp + 2]))
            lo_s.append(lo)
            hi_s.append(hi)
            w.append(fourth(*shifted_ax(e[1, f, r + 2], xlo[:, ca:ca + 1], xlo[:, ca + 1:ca + 2],
                                        xhi[:, ca:ca + 1], xhi[:, ca + 1:ca + 2])))
        part = flux_pair(lo_s, hi_s, 2)
        balance = [b + p for b, p in zip(balance, part)]
        weight = [a + b for a, b in zip(weight, w)]
        total = weight[0] * balance[0]
        for f in range(1, fields):
            total = total + weight[f] * balance[f]
        out_ref[r] = jnp.abs(total)
        return carry

    lax.fori_loop(0, rows, row_body, 0)

    for cond, c in sends:
        when(cond, c.wait_send)


def stencil(primal, adjoint):
    fields, rows, n_a, n_x = primal.shape
    anywhere = pl.BlockSpec(memory_space=pl.ANY)
    return pl.pallas_call(
        stencil_kernel,
        out_shape=jax.ShapeDtypeStruct((rows, n_a, n_x), jnp.float32),
        in_specs=[anywhere, anywhere],
        out_specs=pl.BlockSpec(memory_space=pltpu.VMEM),
        scratch_shapes=[
            pltpu.VMEM((2, fields, rows + 4, n_a, n_x), jnp.float32),
            pltpu.VMEM((2, 2 * fields * rows * 2, n_x), jnp.float32),
            pltpu.VMEM((2, 2 * fields * rows * 2, n_x), jnp.float32),
            pltpu.VMEM((2, rows, 2 * fields, 8, n_x), jnp.float32),
            pltpu.VMEM((2, -(-4 * fields // 8) * 8, rows * n_a), jnp.float32),
            pltpu.VMEM((2, 128, rows * n_a), jnp.float32),
            pltpu.VMEM((2, rows * n_a, 128), jnp.float32),
            pltpu.SemaphoreType.DMA((2,)),
            pltpu.SemaphoreType.DMA((6,)),
            pltpu.SemaphoreType.DMA((6,)),
        ],
        compiler_params=pltpu.CompilerParams(
            collective_id=2, has_side_effects=True, vmem_limit_bytes=48 * 1024 * 1024
        ),
    )(primal, adjoint)


def on_device(primal, adjoint, refine_flag, owner_map, migrate_weight, neighbor_list):
    indicator = stencil(primal, adjoint)
    rows_rad, rows_azi, rows_ax = indicator.shape
    per_rad = rows_rad // BLK
    per_azi = rows_azi // BLK
    per_ax = rows_ax // BLK
    block_mean = indicator.reshape(per_rad, BLK, per_azi, BLK, per_ax, BLK).mean(axis=(1, 3, 5))
    all_means = gather_all(block_mean.reshape(-1), 0)
    size_rad = lax.axis_size("rad")
    size_azi = lax.axis_size("azi")
    size_ax = lax.axis_size("ax")
    blocks_azi = per_azi * size_azi
    blocks_ax = per_ax * size_ax
    block_rad = neighbor_list // (blocks_azi * blocks_ax)
    block_azi = neighbor_list // blocks_ax % blocks_azi
    block_ax = neighbor_list % blocks_ax
    owner_dev = (
        block_rad // per_rad * size_azi + block_azi // per_azi
    ) * size_ax + block_ax // per_ax
    local_pos = (block_rad % per_rad * per_azi + block_azi % per_azi) * per_ax + block_ax % per_ax
    position = owner_dev * (per_rad * per_azi * per_ax) + local_pos
    beside_all = jnp.mean(jnp.take(all_means, position), axis=-1)
    smooth = 0.5 * block_mean + 0.5 * beside_all
    own_index = (
        lax.axis_index("rad") * size_azi + lax.axis_index("azi")
    ) * size_ax + lax.axis_index("ax")
    moved = (owner_map != own_index).astype(jnp.float32)
    block_cost = (
        smooth * (1.0 + 7.0 * refine_flag.astype(jnp.float32))
        + 0.25 * migrate_weight.astype(jnp.float32) * moved
    )
    width = block_cost.size
    payload = jnp.concatenate([block_cost.reshape(-1), owner_map.reshape(-1).astype(jnp.float32)])
    gathered = gather_all(payload, 1).reshape(-1, 2 * width)
    cost_all = gathered[:, :width]
    owner_all = gathered[:, width:]
    total = jnp.sum(jnp.where(owner_all == own_index.astype(jnp.float32), cost_all, 0.0))
    owner_load = (total / (per_rad * per_azi * per_ax)).reshape(1, 1, 1)
    return (indicator, block_cost, owner_load)


def solution(mesh):
    return jax.shard_map(
        on_device,
        mesh=mesh,
        in_specs=(
            P(None, "rad", "azi", "ax"),
            P(None, "rad", "azi", "ax"),
            P("rad", "azi", "ax"),
            P("rad", "azi", "ax"),
            P("rad", "azi", "ax"),
            P("rad", "azi", "ax", None),
        ),
        out_specs=(P("rad", "azi", "ax"), P("rad", "azi", "ax"), P("rad", "azi", "ax")),
        check_vma=False,
    )
```

```python
import functools
import jax
import jax.numpy as jnp
from jax import lax
from jax.experimental import pallas as pl
from jax.experimental.pallas import tpu as pltpu
from jax.sharding import PartitionSpec as P

BLK = 16
AXES = ("rad", "azi", "ax")
MESH = pl.DeviceIdType.MESH


def gather_kernel(sizes, x_ref, o_ref, lsem, ssem, rsem):
    n_r, n_a, n_x = sizes
    r = lax.axis_index("rad")
    a = lax.axis_index("azi")
    x = lax.axis_index("ax")

    def at(rr, aa, xx):
        return (rr, aa, xx)

    stages = [
        (n_x, lambda k: at(r, a, lax.rem(x + k, n_x)), lambda k: at(r, a, lax.rem(x + n_x - k, n_x))),
        (n_a, lambda k: at(r, lax.rem(a + k, n_a), x), lambda k: at(r, lax.rem(a + n_a - k, n_a), x)),
        (n_r, lambda k: at(lax.rem(r + k, n_r), a, x), lambda k: at(lax.rem(r + n_r - k, n_r), a, x)),
    ]

    def region(stage, dev):
        rr, aa, xx = dev
        if stage == 0:
            return o_ref.at[pl.ds(rr, 1), pl.ds(aa, 1), pl.ds(xx, 1)]
        if stage == 1:
            return o_ref.at[pl.ds(rr, 1), pl.ds(aa, 1)]
        return o_ref.at[pl.ds(rr, 1)]

    local = pltpu.make_async_copy(x_ref, region(0, (r, a, x)), lsem)
    local.start()
    sends = []
    slot = 0
    for stage, (n, to, frm) in enumerate(stages):
        src = x_ref if stage == 0 else region(stage, (r, a, x))
        first = slot
        for k in range(1, n):
            copy = pltpu.make_async_remote_copy(
                src_ref=src,
                dst_ref=region(stage, (r, a, x)),
                send_sem=ssem.at[slot],
                recv_sem=rsem.at[slot],
                device_id=to(k),
                device_id_type=MESH,
            )
            copy.start()
            sends.append(copy)
            slot += 1
        slot = first
        for k in range(1, n):
            incoming = pltpu.make_async_remote_copy(
                src_ref=src,
                dst_ref=region(stage, frm(k)),
                send_sem=ssem.at[slot],
                recv_sem=rsem.at[slot],
                device_id=frm(k),
                device_id_type=MESH,
            )
            incoming.wait_recv()
            slot += 1
        if stage == 0:
            local.wait()
    for copy in sends:
        copy.wait_send()


def gather_all(values, cid):
    n_r, n_a, n_x = (lax.axis_size(ax) for ax in AXES)
    width = values.shape[0]
    links = (n_r - 1) + (n_a - 1) + (n_x - 1)
    out = pl.pallas_call(
        functools.partial(gather_kernel, (n_r, n_a, n_x)),
        out_shape=jax.ShapeDtypeStruct((n_r, n_a, n_x, width), jnp.float32),
        in_specs=[pl.BlockSpec(memory_space=pltpu.VMEM)],
        out_specs=pl.BlockSpec(memory_space=pltpu.VMEM),
        scratch_shapes=[
            pltpu.SemaphoreType.DMA(()),
            pltpu.SemaphoreType.DMA((links,)),
            pltpu.SemaphoreType.DMA((links,)),
        ],
        compiler_params=pltpu.CompilerParams(has_side_effects=True),
    )(values.reshape(1, 1, 1, width))
    return out.reshape(-1)


def dense(x):
    return x.reshape(-1, 128)


def exchange(tail, head, axis, periodic):
    count = lax.axis_size(axis)
    forward = [(i, i + 1) for i in range(count - 1)]
    if periodic:
        forward.append((count - 1, 0))
    backward = [(target, source) for source, target in forward]
    low = lax.ppermute(dense(tail), axis, forward).reshape(tail.shape)
    high = lax.ppermute(dense(head), axis, backward).reshape(head.shape)
    return low, high


def flux_pair(state_lo, state_hi, along):
    return [h - l for h, l in zip(euler_flux(state_hi, along), euler_flux(state_lo, along))]


def euler_flux(s, along):
    density, m0, m1, m2, energy = s
    momenta = (m0, m1, m2)
    inv = 1.0 / density
    velocity = momenta[along] * inv
    kinetic = 0.5 * (m0 * m0 + m1 * m1 + m2 * m2) * inv
    pressure = 0.4 * (energy - kinetic)
    columns = [momenta[along], m0 * velocity, m1 * velocity, m2 * velocity, (energy + pressure) * velocity]
    columns[1 + along] = columns[1 + along] + pressure
    return columns


def faces(um2, um1, u, up1, up2):
    lower = (7.0 * um1 - um2) / 12.0 + (7.0 * u - up1) / 12.0
    upper = (7.0 * u - um1) / 12.0 + (7.0 * up1 - up2) / 12.0
    return lower, upper


def fourth(zm2, zm1, z, zp1, zp2):
    return (zm2 - 4.0 * zm1 + 6.0 * z - 4.0 * zp1 + zp2) / 12.0


def stencil_kernel(p_hbm, a_hbm, out_ref, e, az_send, az_recv, az_exp, x_send, x_recv, xt, sems, ssem, rsem):
    _, fields, ext_rows, n_a, n_x = e.shape
    rows = ext_rows - 4
    n_r_dev, n_a_dev, n_x_dev = (lax.axis_size(ax) for ax in AXES)
    me_r, me_a, me_x = (lax.axis_index(ax) for ax in AXES)
    has_r_lo, has_r_hi = me_r > 0, me_r < n_r_dev - 1
    has_x_lo, has_x_hi = me_x > 0, me_x < n_x_dev - 1
    r_lo, r_hi = (me_r - 1, me_a, me_x), (me_r + 1, me_a, me_x)
    a_lo = (me_r, lax.rem(me_a + n_a_dev - 1, n_a_dev), me_x)
    a_hi = (me_r, lax.rem(me_a + 1, n_a_dev), me_x)
    x_lo, x_hi = (me_r, me_a, me_x - 1), (me_r, me_a, me_x + 1)

    loads = [
        pltpu.make_async_copy(p_hbm, e.at[0, :, pl.ds(2, rows)], sems.at[0]),
        pltpu.make_async_copy(a_hbm, e.at[1, :, pl.ds(2, rows)], sems.at[1]),
    ]
    for c in loads:
        c.start()

    barrier = pltpu.get_barrier_semaphore()
    for cond, dev in ((has_r_lo, r_lo), (has_r_hi, r_hi), (has_x_lo, x_lo), (has_x_hi, x_hi)):
        @pl.when(cond)
        def _():
            pl.semaphore_signal(barrier, 1, device_id=dev, device_id_type=MESH)
    pl.semaphore_signal(barrier, 1, device_id=a_lo, device_id_type=MESH)
    pl.semaphore_signal(barrier, 1, device_id=a_hi, device_id_type=MESH)
    count = 2 + sum(c.astype(jnp.int32) for c in (has_r_lo, has_r_hi, has_x_lo, has_x_hi))
    pl.semaphore_wait(barrier, count)

    x_recv[:, x_send.shape[1]:, :] = jnp.zeros((2, x_recv.shape[1] - x_send.shape[1], x_recv.shape[2]), jnp.float32)
    x_send[:, 4 * fields:, :] = jnp.zeros((2, x_send.shape[1] - 4 * fields, x_send.shape[2]), jnp.float32)
    for c in loads:
        c.wait()

    for k in range(2):
        for f in range(fields):
            for r in range(rows):
                row = ((k * fields + f) * rows + r) * 2
                az_send[0, row:row + 2, :] = e[k, f, 2 + r, 0:2, :]
                az_send[1, row:row + 2, :] = e[k, f, 2 + r, n_a - 2:n_a, :]
            plane = e[k, f, 2:2 + rows].reshape(rows * n_a, n_x)
            cols = plane.T
            row = (k * fields + f) * 2
            x_send[0, row:row + 2, :] = cols[0:2]
            x_send[1, row:row + 2, :] = cols[n_x - 2:n_x]

    def remote(src, dst, i, dev):
        return pltpu.make_async_remote_copy(
            src_ref=src, dst_ref=dst, send_sem=ssem.at[i], recv_sem=rsem.at[i],
            device_id=dev, device_id_type=MESH,
        )

    n_kx = x_send.shape[1]
    sends = [
        (has_r_hi, remote(e.at[:, :, pl.ds(rows, 2)], e.at[:, :, pl.ds(0, 2)], 0, r_hi)),
        (has_r_lo, remote(e.at[:, :, pl.ds(2, 2)], e.at[:, :, pl.ds(rows + 2, 2)], 1, r_lo)),
        (None, remote(az_send.at[1], az_recv.at[0], 2, a_hi)),
        (None, remote(az_send.at[0], az_recv.at[1], 3, a_lo)),
        (has_x_hi, remote(x_send.at[1], x_recv.at[0, pl.ds(0, n_kx)], 4, x_hi)),
        (has_x_lo, remote(x_send.at[0], x_recv.at[1, pl.ds(0, n_kx)], 5, x_lo)),
    ]
    recvs = [
        (has_r_lo, remote(e.at[:, :, pl.ds(rows, 2)], e.at[:, :, pl.ds(0, 2)], 0, r_lo)),
        (has_r_hi, remote(e.at[:, :, pl.ds(2, 2)], e.at[:, :, pl.ds(rows + 2, 2)], 1, r_hi)),
        (None, remote(az_send.at[1], az_recv.at[0], 2, a_lo)),
        (None, remote(az_send.at[0], az_recv.at[1], 3, a_hi)),
        (has_x_lo, remote(x_send.at[1], x_recv.at[0, pl.ds(0, n_kx)], 4, x_lo)),
        (has_x_hi, remote(x_send.at[0], x_recv.at[1, pl.ds(0, n_kx)], 5, x_hi)),
    ]

    def when(cond, fn):
        if cond is None:
            fn()
        else:
            pl.when(cond)(fn)

    for cond, c in sends:
        when(cond, c.start)

    @pl.when(jnp.logical_not(has_r_lo))
    def _():
        e[:, :, 0:2] = jnp.zeros((2, fields, 2, n_a, n_x), jnp.float32)

    @pl.when(jnp.logical_not(has_r_hi))
    def _():
        e[:, :, rows + 2:rows + 4] = jnp.zeros((2, fields, 2, n_a, n_x), jnp.float32)

    @pl.when(jnp.logical_not(has_x_lo))
    def _():
        x_recv[0, 0:n_kx, :] = jnp.zeros((n_kx, x_recv.shape[2]), jnp.float32)

    @pl.when(jnp.logical_not(has_x_hi))
    def _():
        x_recv[1, 0:n_kx, :] = jnp.zeros((n_kx, x_recv.shape[2]), jnp.float32)

    for cond, c in recvs:
        when(cond, c.wait_recv)

    for side in range(2):
        xt[side] = x_recv[side].T
        for k in range(2):
            for f in range(fields):
                for r in range(rows):
                    row = ((k * fields + f) * rows + r) * 2
                    az_exp[side, r, k * fields + f, 0:2, :] = az_recv[side, row:row + 2, :]

    sub = lax.broadcasted_iota(jnp.int32, (n_a, n_x), 0)
    lane = lax.broadcasted_iota(jnp.int32, (n_a, n_x), 1)

    def shifted_azi(u, lo, hi):
        um1 = jnp.where(sub == 0, jnp.broadcast_to(lo[1:2], u.shape), pltpu.roll(u, 1, 0))
        um2 = jnp.where(sub == 0, jnp.broadcast_to(lo[0:1], u.shape),
                        jnp.where(sub == 1, jnp.broadcast_to(lo[1:2], u.shape), pltpu.roll(u, 2, 0)))
        up1 = jnp.where(sub == n_a - 1, jnp.broadcast_to(hi[0:1], u.shape), pltpu.roll(u, n_a - 1, 0))
        up2 = jnp.where(sub == n_a - 1, jnp.broadcast_to(hi[1:2], u.shape),
                        jnp.where(sub == n_a - 2, jnp.broadcast_to(hi[0:1], u.shape), pltpu.roll(u, n_a - 2, 0)))
        return um2, um1, u, up1, up2

    def shifted_ax(u, lo0, lo1, hi0, hi1):
        um1 = jnp.where(lane == 0, jnp.broadcast_to(lo1, u.shape), pltpu.roll(u, 1, 1))
        um2 = jnp.where(lane == 0, jnp.broadcast_to(lo0, u.shape),
                        jnp.where(lane == 1, jnp.broadcast_to(lo1, u.shape), pltpu.roll(u, 2, 1)))
        up1 = jnp.where(lane == n_x - 1, jnp.broadcast_to(hi0, u.shape), pltpu.roll(u, n_x - 1, 1))
        up2 = jnp.where(lane == n_x - 1, jnp.broadcast_to(hi1, u.shape),
                        jnp.where(lane == n_x - 2, jnp.broadcast_to(hi0, u.shape), pltpu.roll(u, n_x - 2, 1)))
        return um2, um1, u, up1, up2

    def row_body(r, carry):
        base = pl.multiple_of(r * n_a, n_a)
        xlo = xt[0, pl.ds(base, n_a), :]
        xhi = xt[1, pl.ds(base, n_a), :]
        lo_s, hi_s, w = [], [], []
        for f in range(fields):
            lo, hi = faces(*[e[0, f, r + k] for k in range(5)])
            lo_s.append(lo)
            hi_s.append(hi)
            w.append(fourth(*[e[1, f, r + k] for k in range(5)]))
        balance = flux_pair(lo_s, hi_s, 0)
        weight = w
        lo_s, hi_s, w = [], [], []
        for f in range(fields):
            lo, hi = faces(*shifted_azi(e[0, f, r + 2], az_exp[0, r, f], az_exp[1, r, f]))
            lo_s.append(lo)
            hi_s.append(hi)
            w.append(fourth(*shifted_azi(e[1, f, r + 2], az_exp[0, r, fields + f], az_exp[1, r, fields + f])))
        part = flux_pair(lo_s, hi_s, 1)
        balance = [b + p for b, p in zip(balance, part)]
        weight = [a + b for a, b in zip(weight, w)]
        lo_s, hi_s, w = [], [], []
        for f in range(fields):
            cp, ca = 2 * f, 2 * (fields + f)
            lo, hi = faces(*shifted_ax(e[0, f, r + 2], xlo[:, cp:cp + 1], xlo[:, cp + 1:cp + 2],
                                       xhi[:, cp:cp + 1], xhi[:, cp + 1:cp + 2]))
            lo_s.append(lo)
            hi_s.append(hi)
            w.append(fourth(*shifted_ax(e[1, f, r + 2], xlo[:, ca:ca + 1], xlo[:, ca + 1:ca + 2],
                                        xhi[:, ca:ca + 1], xhi[:, ca + 1:ca + 2])))
        part = flux_pair(lo_s, hi_s, 2)
        balance = [b + p for b, p in zip(balance, part)]
        weight = [a + b for a, b in zip(weight, w)]
        total = weight[0] * balance[0]
        for f in range(1, fields):
            total = total + weight[f] * balance[f]
        out_ref[r] = jnp.abs(total)
        return carry

    lax.fori_loop(0, rows, row_body, 0)

    for cond, c in sends:
        when(cond, c.wait_send)


def stencil(primal, adjoint):
    fields, rows, n_a, n_x = primal.shape
    anywhere = pl.BlockSpec(memory_space=pl.ANY)
    return pl.pallas_call(
        stencil_kernel,
        out_shape=jax.ShapeDtypeStruct((rows, n_a, n_x), jnp.float32),
        in_specs=[anywhere, anywhere],
        out_specs=pl.BlockSpec(memory_space=pltpu.VMEM),
        scratch_shapes=[
            pltpu.VMEM((2, fields, rows + 4, n_a, n_x), jnp.float32),
            pltpu.VMEM((2, 2 * fields * rows * 2, n_x), jnp.float32),
            pltpu.VMEM((2, 2 * fields * rows * 2, n_x), jnp.float32),
            pltpu.VMEM((2, rows, 2 * fields, 8, n_x), jnp.float32),
            pltpu.VMEM((2, -(-4 * fields // 8) * 8, rows * n_a), jnp.float32),
            pltpu.VMEM((2, 128, rows * n_a), jnp.float32),
            pltpu.VMEM((2, rows * n_a, 128), jnp.float32),
            pltpu.SemaphoreType.DMA((2,)),
            pltpu.SemaphoreType.DMA((6,)),
            pltpu.SemaphoreType.DMA((6,)),
        ],
        compiler_params=pltpu.CompilerParams(
            collective_id=2, has_side_effects=True, vmem_limit_bytes=48 * 1024 * 1024
        ),
    )(primal, adjoint)


def on_device(primal, adjoint, refine_flag, owner_map, migrate_weight, neighbor_list):
    indicator = stencil(primal, adjoint)
    rows_rad, rows_azi, rows_ax = indicator.shape
    per_rad = rows_rad // BLK
    per_azi = rows_azi // BLK
    per_ax = rows_ax // BLK
    block_mean = indicator.reshape(per_rad, BLK, per_azi, BLK, per_ax, BLK).mean(axis=(1, 3, 5))
    all_means = gather_all(block_mean.reshape(-1), 0)
    size_rad = lax.axis_size("rad")
    size_azi = lax.axis_size("azi")
    size_ax = lax.axis_size("ax")
    blocks_azi = per_azi * size_azi
    blocks_ax = per_ax * size_ax
    block_rad = neighbor_list // (blocks_azi * blocks_ax)
    block_azi = neighbor_list // blocks_ax % blocks_azi
    block_ax = neighbor_list % blocks_ax
    owner_dev = (
        block_rad // per_rad * size_azi + block_azi // per_azi
    ) * size_ax + block_ax // per_ax
    local_pos = (block_rad % per_rad * per_azi + block_azi % per_azi) * per_ax + block_ax % per_ax
    position = owner_dev * (per_rad * per_azi * per_ax) + local_pos
    beside_all = jnp.mean(jnp.take(all_means, position), axis=-1)
    smooth = 0.5 * block_mean + 0.5 * beside_all
    own_index = (
        lax.axis_index("rad") * size_azi + lax.axis_index("azi")
    ) * size_ax + lax.axis_index("ax")
    moved = (owner_map != own_index).astype(jnp.float32)
    block_cost = (
        smooth * (1.0 + 7.0 * refine_flag.astype(jnp.float32))
        + 0.25 * migrate_weight.astype(jnp.float32) * moved
    )
    width = block_cost.size
    payload = jnp.concatenate([block_cost.reshape(-1), owner_map.reshape(-1).astype(jnp.float32)])
    gathered = gather_all(payload, 1).reshape(-1, 2 * width)
    cost_all = gathered[:, :width]
    owner_all = gathered[:, width:]
    total = jnp.sum(jnp.where(owner_all == own_index.astype(jnp.float32), cost_all, 0.0))
    owner_load = (total / (per_rad * per_azi * per_ax)).reshape(1, 1, 1)
    return (indicator, block_cost, owner_load)


def solution(mesh):
    return jax.shard_map(
        on_device,
        mesh=mesh,
        in_specs=(
            P(None, "rad", "azi", "ax"),
            P(None, "rad", "azi", "ax"),
            P("rad", "azi", "ax"),
            P("rad", "azi", "ax"),
            P("rad", "azi", "ax"),
            P("rad", "azi", "ax", None),
        ),
        out_specs=(P("rad", "azi", "ax"), P("rad", "azi", "ax"), P("rad", "azi", "ax")),
        check_vma=False,
    )
```

```python
import functools
import jax
import jax.numpy as jnp
from jax import lax
from jax.experimental import pallas as pl
from jax.experimental.pallas import tpu as pltpu
from jax.sharding import PartitionSpec as P

BLK = 16
AXES = ("rad", "azi", "ax")
MESH = pl.DeviceIdType.MESH


def gather_stages(sizes, pairs, local_sem, ssem, rsem):
    n_r, n_a, n_x = sizes
    r = lax.axis_index("rad")
    a = lax.axis_index("azi")
    x = lax.axis_index("ax")
    stages = [
        (n_x, lambda k: (r, a, lax.rem(x + k, n_x)), lambda k: (r, a, lax.rem(x + n_x - k, n_x))),
        (n_a, lambda k: (r, lax.rem(a + k, n_a), x), lambda k: (r, lax.rem(a + n_a - k, n_a), x)),
        (n_r, lambda k: (lax.rem(r + k, n_r), a, x), lambda k: (lax.rem(r + n_r - k, n_r), a, x)),
    ]

    def region(dst, stage, dev):
        rr, aa, xx = dev
        if stage == 0:
            return dst.at[pl.ds(rr, 1), pl.ds(aa, 1), pl.ds(xx, 1)]
        if stage == 1:
            return dst.at[pl.ds(rr, 1), pl.ds(aa, 1)]
        return dst.at[pl.ds(rr, 1)]

    locals_ = []
    for i, (src, dst) in enumerate(pairs):
        c = pltpu.make_async_copy(src, region(dst, 0, (r, a, x)), local_sem.at[i])
        c.start()
        locals_.append(c)
    sends = []
    slot = 0
    for stage, (n, to, frm) in enumerate(stages):
        first = slot
        for src, dst in pairs:
            s = src if stage == 0 else region(dst, stage, (r, a, x))
            for k in range(1, n):
                copy = pltpu.make_async_remote_copy(
                    src_ref=s, dst_ref=region(dst, stage, (r, a, x)),
                    send_sem=ssem.at[slot], recv_sem=rsem.at[slot],
                    device_id=to(k), device_id_type=MESH,
                )
                copy.start()
                sends.append(copy)
                slot += 1
        slot = first
        for src, dst in pairs:
            s = src if stage == 0 else region(dst, stage, (r, a, x))
            for k in range(1, n):
                incoming = pltpu.make_async_remote_copy(
                    src_ref=s, dst_ref=region(dst, stage, frm(k)),
                    send_sem=ssem.at[slot], recv_sem=rsem.at[slot],
                    device_id=frm(k), device_id_type=MESH,
                )
                incoming.wait_recv()
                slot += 1
        if stage == 0:
            for c in locals_:
                c.wait()
    return sends


def peer_barrier(sizes):
    n_r, n_a, n_x = sizes
    r = lax.axis_index("rad")
    a = lax.axis_index("azi")
    x = lax.axis_index("ax")
    barrier = pltpu.get_barrier_semaphore()
    count = 0
    for k in range(1, n_x):
        pl.semaphore_signal(barrier, 1, device_id=(r, a, lax.rem(x + k, n_x)), device_id_type=MESH)
        count += 1
    for k in range(1, n_a):
        pl.semaphore_signal(barrier, 1, device_id=(r, lax.rem(a + k, n_a), x), device_id_type=MESH)
        count += 1
    for k in range(1, n_r):
        pl.semaphore_signal(barrier, 1, device_id=(lax.rem(r + k, n_r), a, x), device_id_type=MESH)
        count += 1
    pl.semaphore_wait(barrier, count)


def post_kernel(sizes, blocks, bm_ref, nl_ref, rf_ref, mw_ref, ow_ref, cost_out, load_out,
                g_mean, g_mean_s, sums_s, sums_v, pay_c, pay_o, g_cost, g_own, lsem, ssem, rsem):
    n_r, n_a, n_x = sizes
    per_rad, per_azi, per_ax = blocks
    n_links = (n_r - 1) + (n_a - 1) + (n_x - 1)
    peer_barrier(sizes)
    sends = gather_stages(sizes, [(bm_ref, g_mean)], lsem.at[0:1], ssem.at[0:n_links], rsem.at[0:n_links])
    to_smem = pltpu.make_async_copy(g_mean, g_mean_s, lsem.at[1])
    to_smem.start()
    to_smem.wait()
    blocks_azi = per_azi * n_a
    blocks_ax = per_ax * n_x
    width = per_rad * per_azi * per_ax
    for b in range(width):
        total = None
        for k in range(6):
            v = nl_ref[b * 6 + k]
            br = v // (blocks_azi * blocks_ax)
            ba = v // blocks_ax % blocks_azi
            bx = v % blocks_ax
            local = (br % per_rad * per_azi + ba % per_azi) * per_ax + bx % per_ax
            val = g_mean_s[br // per_rad, ba // per_azi, bx // per_ax, local]
            total = val if total is None else total + val
        sums_s[0, b] = total
    to_vmem = pltpu.make_async_copy(sums_s, sums_v, lsem.at[2])
    to_vmem.start()
    to_vmem.wait()
    me = (lax.axis_index("rad") * n_a + lax.axis_index("azi")) * n_x + lax.axis_index("ax")
    me_f = me.astype(jnp.float32)
    bm = bm_ref[0, 0]
    owner = ow_ref[...]
    smooth = 0.5 * bm + 0.5 * (sums_v[...] / 6.0)
    moved = jnp.where(owner != me_f, 1.0, 0.0)
    cost = smooth * (1.0 + 7.0 * rf_ref[...]) + 0.25 * mw_ref[...] * moved
    cost_out[...] = cost
    pay_c[0, 0] = cost
    pay_o[0, 0] = owner
    sends += gather_stages(
        sizes, [(pay_c, g_cost), (pay_o, g_own)], lsem.at[3:5],
        ssem.at[n_links:3 * n_links], rsem.at[n_links:3 * n_links],
    )
    costs = g_cost[...]
    owners = g_own[...]
    picked = jnp.where(owners == me_f, costs, 0.0)
    part = jnp.sum(picked, axis=(0, 1))
    total = jnp.sum(part, axis=0, keepdims=True)
    total = jnp.sum(total, axis=1, keepdims=True)
    load_out[...] = (total / float(width)).reshape(1, 1, 1)
    for c in sends:
        c.wait_send()


def post(block_mean, neighbor_list, refine_flag, migrate_weight, owner_map, blocks):
    sizes = tuple(lax.axis_size(ax) for ax in AXES)
    n_r, n_a, n_x = sizes
    width = block_mean.size
    n_links = (n_r - 1) + (n_a - 1) + (n_x - 1)
    vmem = pl.BlockSpec(memory_space=pltpu.VMEM)
    smem = pl.BlockSpec(memory_space=pltpu.SMEM)
    row = lambda v: v.reshape(1, width).astype(jnp.float32)
    cost, load = pl.pallas_call(
        functools.partial(post_kernel, sizes, blocks),
        out_shape=(jax.ShapeDtypeStruct((1, width), jnp.float32), jax.ShapeDtypeStruct((1, 1, 1), jnp.float32)),
        in_specs=[vmem, smem, vmem, vmem, vmem],
        out_specs=(vmem, vmem),
        scratch_shapes=[
            pltpu.VMEM((n_r, n_a, n_x, width), jnp.float32),
            pltpu.SMEM((n_r, n_a, n_x, width), jnp.float32),
            pltpu.SMEM((1, width), jnp.float32),
            pltpu.VMEM((1, width), jnp.float32),
            pltpu.VMEM((1, 1, 1, width), jnp.float32),
            pltpu.VMEM((1, 1, 1, width), jnp.float32),
            pltpu.VMEM((n_r, n_a, n_x, width), jnp.float32),
            pltpu.VMEM((n_r, n_a, n_x, width), jnp.float32),
            pltpu.SemaphoreType.DMA((5,)),
            pltpu.SemaphoreType.DMA((3 * n_links,)),
            pltpu.SemaphoreType.DMA((3 * n_links,)),
        ],
        compiler_params=pltpu.CompilerParams(collective_id=0, has_side_effects=True),
    )(
        block_mean.reshape(1, 1, 1, width), neighbor_list.reshape(-1),
        row(refine_flag), row(migrate_weight), row(owner_map),
    )
    return cost.reshape(refine_flag.shape), load


def dense(x):
    return x.reshape(-1, 128)


def exchange(tail, head, axis, periodic):
    count = lax.axis_size(axis)
    forward = [(i, i + 1) for i in range(count - 1)]
    if periodic:
        forward.append((count - 1, 0))
    backward = [(target, source) for source, target in forward]
    low = lax.ppermute(dense(tail), axis, forward).reshape(tail.shape)
    high = lax.ppermute(dense(head), axis, backward).reshape(head.shape)
    return low, high


def flux_pair(state_lo, state_hi, along):
    return [h - l for h, l in zip(euler_flux(state_hi, along), euler_flux(state_lo, along))]


def euler_flux(s, along):
    density, m0, m1, m2, energy = s
    momenta = (m0, m1, m2)
    inv = 1.0 / density
    velocity = momenta[along] * inv
    kinetic = 0.5 * (m0 * m0 + m1 * m1 + m2 * m2) * inv
    pressure = 0.4 * (energy - kinetic)
    columns = [momenta[along], m0 * velocity, m1 * velocity, m2 * velocity, (energy + pressure) * velocity]
    columns[1 + along] = columns[1 + along] + pressure
    return columns


def faces(um2, um1, u, up1, up2):
    lower = (7.0 * um1 - um2) / 12.0 + (7.0 * u - up1) / 12.0
    upper = (7.0 * u - um1) / 12.0 + (7.0 * up1 - up2) / 12.0
    return lower, upper


def fourth(zm2, zm1, z, zp1, zp2):
    return (zm2 - 4.0 * zm1 + 6.0 * z - 4.0 * zp1 + zp2) / 12.0


def stencil_kernel(p_hbm, a_hbm, out_ref, e, az_send, az_recv, az_exp, x_send, x_recv, xt, sems, ssem, rsem):
    _, fields, ext_rows, n_a, n_x = e.shape
    rows = ext_rows - 4
    n_r_dev, n_a_dev, n_x_dev = (lax.axis_size(ax) for ax in AXES)
    me_r, me_a, me_x = (lax.axis_index(ax) for ax in AXES)
    has_r_lo, has_r_hi = me_r > 0, me_r < n_r_dev - 1
    has_x_lo, has_x_hi = me_x > 0, me_x < n_x_dev - 1
    r_lo, r_hi = (me_r - 1, me_a, me_x), (me_r + 1, me_a, me_x)
    a_lo = (me_r, lax.rem(me_a + n_a_dev - 1, n_a_dev), me_x)
    a_hi = (me_r, lax.rem(me_a + 1, n_a_dev), me_x)
    x_lo, x_hi = (me_r, me_a, me_x - 1), (me_r, me_a, me_x + 1)

    loads = [
        pltpu.make_async_copy(p_hbm, e.at[0, :, pl.ds(2, rows)], sems.at[0]),
        pltpu.make_async_copy(a_hbm, e.at[1, :, pl.ds(2, rows)], sems.at[1]),
    ]
    for c in loads:
        c.start()

    barrier = pltpu.get_barrier_semaphore()
    for cond, dev in ((has_r_lo, r_lo), (has_r_hi, r_hi), (has_x_lo, x_lo), (has_x_hi, x_hi)):
        @pl.when(cond)
        def _():
            pl.semaphore_signal(barrier, 1, device_id=dev, device_id_type=MESH)
    pl.semaphore_signal(barrier, 1, device_id=a_lo, device_id_type=MESH)
    pl.semaphore_signal(barrier, 1, device_id=a_hi, device_id_type=MESH)
    count = 2 + sum(c.astype(jnp.int32) for c in (has_r_lo, has_r_hi, has_x_lo, has_x_hi))
    pl.semaphore_wait(barrier, count)

    x_recv[:, x_send.shape[1]:, :] = jnp.zeros((2, x_recv.shape[1] - x_send.shape[1], x_recv.shape[2]), jnp.float32)
    x_send[:, 4 * fields:, :] = jnp.zeros((2, x_send.shape[1] - 4 * fields, x_send.shape[2]), jnp.float32)
    for c in loads:
        c.wait()

    for k in range(2):
        for f in range(fields):
            for r in range(rows):
                row = ((k * fields + f) * rows + r) * 2
                az_send[0, row:row + 2, :] = e[k, f, 2 + r, 0:2, :]
                az_send[1, row:row + 2, :] = e[k, f, 2 + r, n_a - 2:n_a, :]
            plane = e[k, f, 2:2 + rows].reshape(rows * n_a, n_x)
            cols = plane.T
            row = (k * fields + f) * 2
            x_send[0, row:row + 2, :] = cols[0:2]
            x_send[1, row:row + 2, :] = cols[n_x - 2:n_x]

    def remote(src, dst, i, dev):
        return pltpu.make_async_remote_copy(
            src_ref=src, dst_ref=dst, send_sem=ssem.at[i], recv_sem=rsem.at[i],
            device_id=dev, device_id_type=MESH,
        )

    n_kx = x_send.shape[1]
    sends = [
        (has_r_hi, remote(e.at[:, :, pl.ds(rows, 2)], e.at[:, :, pl.ds(0, 2)], 0, r_hi)),
        (has_r_lo, remote(e.at[:, :, pl.ds(2, 2)], e.at[:, :, pl.ds(rows + 2, 2)], 1, r_lo)),
        (None, remote(az_send.at[1], az_recv.at[0], 2, a_hi)),
        (None, remote(az_send.at[0], az_recv.at[1], 3, a_lo)),
        (has_x_hi, remote(x_send.at[1], x_recv.at[0, pl.ds(0, n_kx)], 4, x_hi)),
        (has_x_lo, remote(x_send.at[0], x_recv.at[1, pl.ds(0, n_kx)], 5, x_lo)),
    ]
    recvs = [
        (has_r_lo, remote(e.at[:, :, pl.ds(rows, 2)], e.at[:, :, pl.ds(0, 2)], 0, r_lo)),
        (has_r_hi, remote(e.at[:, :, pl.ds(2, 2)], e.at[:, :, pl.ds(rows + 2, 2)], 1, r_hi)),
        (None, remote(az_send.at[1], az_recv.at[0], 2, a_lo)),
        (None, remote(az_send.at[0], az_recv.at[1], 3, a_hi)),
        (has_x_lo, remote(x_send.at[1], x_recv.at[0, pl.ds(0, n_kx)], 4, x_lo)),
        (has_x_hi, remote(x_send.at[0], x_recv.at[1, pl.ds(0, n_kx)], 5, x_hi)),
    ]

    def when(cond, fn):
        if cond is None:
            fn()
        else:
            pl.when(cond)(fn)

    for cond, c in sends:
        when(cond, c.start)

    @pl.when(jnp.logical_not(has_r_lo))
    def _():
        e[:, :, 0:2] = jnp.zeros((2, fields, 2, n_a, n_x), jnp.float32)

    @pl.when(jnp.logical_not(has_r_hi))
    def _():
        e[:, :, rows + 2:rows + 4] = jnp.zeros((2, fields, 2, n_a, n_x), jnp.float32)

    @pl.when(jnp.logical_not(has_x_lo))
    def _():
        x_recv[0, 0:n_kx, :] = jnp.zeros((n_kx, x_recv.shape[2]), jnp.float32)

    @pl.when(jnp.logical_not(has_x_hi))
    def _():
        x_recv[1, 0:n_kx, :] = jnp.zeros((n_kx, x_recv.shape[2]), jnp.float32)

    for cond, c in recvs:
        when(cond, c.wait_recv)

    for side in range(2):
        xt[side] = x_recv[side].T
        for k in range(2):
            for f in range(fields):
                for r in range(rows):
                    row = ((k * fields + f) * rows + r) * 2
                    az_exp[side, r, k * fields + f, 0:2, :] = az_recv[side, row:row + 2, :]

    sub = lax.broadcasted_iota(jnp.int32, (n_a, n_x), 0)
    lane = lax.broadcasted_iota(jnp.int32, (n_a, n_x), 1)

    def shifted_azi(u, lo, hi):
        um1 = jnp.where(sub == 0, jnp.broadcast_to(lo[1:2], u.shape), pltpu.roll(u, 1, 0))
        um2 = jnp.where(sub == 0, jnp.broadcast_to(lo[0:1], u.shape),
                        jnp.where(sub == 1, jnp.broadcast_to(lo[1:2], u.shape), pltpu.roll(u, 2, 0)))
        up1 = jnp.where(sub == n_a - 1, jnp.broadcast_to(hi[0:1], u.shape), pltpu.roll(u, n_a - 1, 0))
        up2 = jnp.where(sub == n_a - 1, jnp.broadcast_to(hi[1:2], u.shape),
                        jnp.where(sub == n_a - 2, jnp.broadcast_to(hi[0:1], u.shape), pltpu.roll(u, n_a - 2, 0)))
        return um2, um1, u, up1, up2

    def shifted_ax(u, lo0, lo1, hi0, hi1):
        um1 = jnp.where(lane == 0, jnp.broadcast_to(lo1, u.shape), pltpu.roll(u, 1, 1))
        um2 = jnp.where(lane == 0, jnp.broadcast_to(lo0, u.shape),
                        jnp.where(lane == 1, jnp.broadcast_to(lo1, u.shape), pltpu.roll(u, 2, 1)))
        up1 = jnp.where(lane == n_x - 1, jnp.broadcast_to(hi0, u.shape), pltpu.roll(u, n_x - 1, 1))
        up2 = jnp.where(lane == n_x - 1, jnp.broadcast_to(hi1, u.shape),
                        jnp.where(lane == n_x - 2, jnp.broadcast_to(hi0, u.shape), pltpu.roll(u, n_x - 2, 1)))
        return um2, um1, u, up1, up2

    def row_body(r, carry):
        base = pl.multiple_of(r * n_a, n_a)
        xlo = xt[0, pl.ds(base, n_a), :]
        xhi = xt[1, pl.ds(base, n_a), :]
        lo_s, hi_s, w = [], [], []
        for f in range(fields):
            lo, hi = faces(*[e[0, f, r + k] for k in range(5)])
            lo_s.append(lo)
            hi_s.append(hi)
            w.append(fourth(*[e[1, f, r + k] for k in range(5)]))
        balance = flux_pair(lo_s, hi_s, 0)
        weight = w
        lo_s, hi_s, w = [], [], []
        for f in range(fields):
            lo, hi = faces(*shifted_azi(e[0, f, r + 2], az_exp[0, r, f], az_exp[1, r, f]))
            lo_s.append(lo)
            hi_s.append(hi)
            w.append(fourth(*shifted_azi(e[1, f, r + 2], az_exp[0, r, fields + f], az_exp[1, r, fields + f])))
        part = flux_pair(lo_s, hi_s, 1)
        balance = [b + p for b, p in zip(balance, part)]
        weight = [a + b for a, b in zip(weight, w)]
        lo_s, hi_s, w = [], [], []
        for f in range(fields):
            cp, ca = 2 * f, 2 * (fields + f)
            lo, hi = faces(*shifted_ax(e[0, f, r + 2], xlo[:, cp:cp + 1], xlo[:, cp + 1:cp + 2],
                                       xhi[:, cp:cp + 1], xhi[:, cp + 1:cp + 2]))
            lo_s.append(lo)
            hi_s.append(hi)
            w.append(fourth(*shifted_ax(e[1, f, r + 2], xlo[:, ca:ca + 1], xlo[:, ca + 1:ca + 2],
                                        xhi[:, ca:ca + 1], xhi[:, ca + 1:ca + 2])))
        part = flux_pair(lo_s, hi_s, 2)
        balance = [b + p for b, p in zip(balance, part)]
        weight = [a + b for a, b in zip(weight, w)]
        total = weight[0] * balance[0]
        for f in range(1, fields):
            total = total + weight[f] * balance[f]
        out_ref[r] = jnp.abs(total)
        return carry

    lax.fori_loop(0, rows, row_body, 0)

    for cond, c in sends:
        when(cond, c.wait_send)


def stencil(primal, adjoint):
    fields, rows, n_a, n_x = primal.shape
    anywhere = pl.BlockSpec(memory_space=pl.ANY)
    return pl.pallas_call(
        stencil_kernel,
        out_shape=jax.ShapeDtypeStruct((rows, n_a, n_x), jnp.float32),
        in_specs=[anywhere, anywhere],
        out_specs=pl.BlockSpec(memory_space=pltpu.VMEM),
        scratch_shapes=[
            pltpu.VMEM((2, fields, rows + 4, n_a, n_x), jnp.float32),
            pltpu.VMEM((2, 2 * fields * rows * 2, n_x), jnp.float32),
            pltpu.VMEM((2, 2 * fields * rows * 2, n_x), jnp.float32),
            pltpu.VMEM((2, rows, 2 * fields, 8, n_x), jnp.float32),
            pltpu.VMEM((2, -(-4 * fields // 8) * 8, rows * n_a), jnp.float32),
            pltpu.VMEM((2, 128, rows * n_a), jnp.float32),
            pltpu.VMEM((2, rows * n_a, 128), jnp.float32),
            pltpu.SemaphoreType.DMA((2,)),
            pltpu.SemaphoreType.DMA((6,)),
            pltpu.SemaphoreType.DMA((6,)),
        ],
        compiler_params=pltpu.CompilerParams(
            collective_id=2, has_side_effects=True, vmem_limit_bytes=48 * 1024 * 1024
        ),
    )(primal, adjoint)


def on_device(primal, adjoint, refine_flag, owner_map, migrate_weight, neighbor_list):
    indicator = stencil(primal, adjoint)
    rows_rad, rows_azi, rows_ax = indicator.shape
    per_rad = rows_rad // BLK
    per_azi = rows_azi // BLK
    per_ax = rows_ax // BLK
    block_mean = indicator.reshape(per_rad, BLK, per_azi, BLK, per_ax, BLK).mean(axis=(1, 3, 5))
    block_cost, owner_load = post(block_mean, neighbor_list, refine_flag, migrate_weight, owner_map, (per_rad, per_azi, per_ax))
    return (indicator, block_cost, owner_load)


def solution(mesh):
    return jax.shard_map(
        on_device,
        mesh=mesh,
        in_specs=(
            P(None, "rad", "azi", "ax"),
            P(None, "rad", "azi", "ax"),
            P("rad", "azi", "ax"),
            P("rad", "azi", "ax"),
            P("rad", "azi", "ax"),
            P("rad", "azi", "ax", None),
        ),
        out_specs=(P("rad", "azi", "ax"), P("rad", "azi", "ax"), P("rad", "azi", "ax")),
        check_vma=False,
    )
```

```python
import functools
import itertools
import jax
import jax.numpy as jnp
from jax import lax
from jax.experimental import pallas as pl
from jax.experimental.pallas import tpu as pltpu
from jax.sharding import PartitionSpec as P

BLK = 16
AXES = ("rad", "azi", "ax")
MESH = pl.DeviceIdType.MESH


def stage_plan(sizes, groups):
    plan = []
    for axes in groups:
        offs = [o for o in itertools.product(*[range(sizes[i]) for i in axes]) if any(o)]
        plan.append((axes, offs))
    return plan


def gen_gather_kernel(sizes, groups, x_ref, o_ref, lsem, ssem, rsem):
    me = tuple(lax.axis_index(a) for a in AXES)
    plan = stage_plan(sizes, groups)

    def shift(off_axes, off, sign):
        dev = list(me)
        for i, o in zip(off_axes, off):
            dev[i] = lax.rem(me[i] + (o if sign > 0 else sizes[i] - o), sizes[i])
        return tuple(dev)

    barrier = pltpu.get_barrier_semaphore()
    count = 0
    for axes, offs in plan:
        for off in offs:
            pl.semaphore_signal(barrier, 1, device_id=shift(axes, off, 1), device_id_type=MESH)
            count += 1
    pl.semaphore_wait(barrier, count)

    covered = set()

    def region(dev):
        idx = []
        for i in range(3):
            if i in covered:
                break
            idx.append(pl.ds(dev[i], 1))
        return o_ref.at[tuple(idx)] if idx else o_ref

    def region_full(dev):
        n_fixed = 3 - len(covered)
        return o_ref.at[tuple(pl.ds(dev[i], 1) for i in range(n_fixed))]

    local = pltpu.make_async_copy(x_ref, o_ref.at[tuple(pl.ds(m, 1) for m in me)], lsem)
    local.start()
    sends = []
    slot = 0
    for stage, (axes, offs) in enumerate(plan):
        src = x_ref if stage == 0 else region_full(me)
        first = slot
        for off in offs:
            c = pltpu.make_async_remote_copy(src_ref=src, dst_ref=region_full(me), send_sem=ssem.at[slot],
                                             recv_sem=rsem.at[slot], device_id=shift(axes, off, 1), device_id_type=MESH)
            c.start()
            sends.append(c)
            slot += 1
        slot = first
        for off in offs:
            frm = shift(axes, off, -1)
            c = pltpu.make_async_remote_copy(src_ref=src, dst_ref=region_full(frm), send_sem=ssem.at[slot],
                                             recv_sem=rsem.at[slot], device_id=frm, device_id_type=MESH)
            c.wait_recv()
            slot += 1
        if stage == 0:
            local.wait()
        covered.update(axes)
    for c in sends:
        c.wait_send()


def gather_all(values, cid, groups=((2, 1), (0,))):
    sizes = tuple(lax.axis_size(a) for a in AXES)
    width = values.shape[0]
    links = sum(len(offs) for _, offs in stage_plan(sizes, groups))
    out = pl.pallas_call(
        functools.partial(gen_gather_kernel, sizes, groups),
        out_shape=jax.ShapeDtypeStruct(sizes + (width,), jnp.float32),
        in_specs=[pl.BlockSpec(memory_space=pltpu.VMEM)],
        out_specs=pl.BlockSpec(memory_space=pltpu.VMEM),
        scratch_shapes=[pltpu.SemaphoreType.DMA(()), pltpu.SemaphoreType.DMA((links,)), pltpu.SemaphoreType.DMA((links,))],
        compiler_params=pltpu.CompilerParams(collective_id=cid, has_side_effects=True),
    )(values.reshape(1, 1, 1, width))
    return out.reshape(-1)


def dense(x):
    return x.reshape(-1, 128)


def exchange(tail, head, axis, periodic):
    count = lax.axis_size(axis)
    forward = [(i, i + 1) for i in range(count - 1)]
    if periodic:
        forward.append((count - 1, 0))
    backward = [(target, source) for source, target in forward]
    low = lax.ppermute(dense(tail), axis, forward).reshape(tail.shape)
    high = lax.ppermute(dense(head), axis, backward).reshape(head.shape)
    return low, high


def flux_pair(state_lo, state_hi, along):
    return [h - l for h, l in zip(euler_flux(state_hi, along), euler_flux(state_lo, along))]


def euler_flux(s, along):
    density, m0, m1, m2, energy = s
    momenta = (m0, m1, m2)
    inv = 1.0 / density
    velocity = momenta[along] * inv
    kinetic = 0.5 * (m0 * m0 + m1 * m1 + m2 * m2) * inv
    pressure = 0.4 * (energy - kinetic)
    columns = [momenta[along], m0 * velocity, m1 * velocity, m2 * velocity, (energy + pressure) * velocity]
    columns[1 + along] = columns[1 + along] + pressure
    return columns


def faces(um2, um1, u, up1, up2):
    lower = (7.0 * um1 - um2) / 12.0 + (7.0 * u - up1) / 12.0
    upper = (7.0 * u - um1) / 12.0 + (7.0 * up1 - up2) / 12.0
    return lower, upper


def fourth(zm2, zm1, z, zp1, zp2):
    return (zm2 - 4.0 * zm1 + 6.0 * z - 4.0 * zp1 + zp2) / 12.0


def stencil_kernel(p_hbm, a_hbm, out_ref, e, az_send, az_recv, az_exp, x_send, x_recv, xt, sems, ssem, rsem):
    _, fields, ext_rows, n_a, n_x = e.shape
    rows = ext_rows - 4
    n_r_dev, n_a_dev, n_x_dev = (lax.axis_size(ax) for ax in AXES)
    me_r, me_a, me_x = (lax.axis_index(ax) for ax in AXES)
    has_r_lo, has_r_hi = me_r > 0, me_r < n_r_dev - 1
    has_x_lo, has_x_hi = me_x > 0, me_x < n_x_dev - 1
    r_lo, r_hi = (me_r - 1, me_a, me_x), (me_r + 1, me_a, me_x)
    a_lo = (me_r, lax.rem(me_a + n_a_dev - 1, n_a_dev), me_x)
    a_hi = (me_r, lax.rem(me_a + 1, n_a_dev), me_x)
    x_lo, x_hi = (me_r, me_a, me_x - 1), (me_r, me_a, me_x + 1)

    loads = [
        pltpu.make_async_copy(p_hbm, e.at[0, :, pl.ds(2, rows)], sems.at[0]),
        pltpu.make_async_copy(a_hbm, e.at[1, :, pl.ds(2, rows)], sems.at[1]),
    ]
    for c in loads:
        c.start()

    barrier = pltpu.get_barrier_semaphore()
    for cond, dev in ((has_r_lo, r_lo), (has_r_hi, r_hi), (has_x_lo, x_lo), (has_x_hi, x_hi)):
        @pl.when(cond)
        def _():
            pl.semaphore_signal(barrier, 1, device_id=dev, device_id_type=MESH)
    pl.semaphore_signal(barrier, 1, device_id=a_lo, device_id_type=MESH)
    pl.semaphore_signal(barrier, 1, device_id=a_hi, device_id_type=MESH)
    count = 2 + sum(c.astype(jnp.int32) for c in (has_r_lo, has_r_hi, has_x_lo, has_x_hi))
    pl.semaphore_wait(barrier, count)

    x_recv[:, x_send.shape[1]:, :] = jnp.zeros((2, x_recv.shape[1] - x_send.shape[1], x_recv.shape[2]), jnp.float32)
    x_send[:, 4 * fields:, :] = jnp.zeros((2, x_send.shape[1] - 4 * fields, x_send.shape[2]), jnp.float32)
    for c in loads:
        c.wait()

    for k in range(2):
        for f in range(fields):
            for r in range(rows):
                row = ((k * fields + f) * rows + r) * 2
                az_send[0, row:row + 2, :] = e[k, f, 2 + r, 0:2, :]
                az_send[1, row:row + 2, :] = e[k, f, 2 + r, n_a - 2:n_a, :]
            plane = e[k, f, 2:2 + rows].reshape(rows * n_a, n_x)
            cols = plane.T
            row = (k * fields + f) * 2
            x_send[0, row:row + 2, :] = cols[0:2]
            x_send[1, row:row + 2, :] = cols[n_x - 2:n_x]

    def remote(src, dst, i, dev):
        return pltpu.make_async_remote_copy(
            src_ref=src, dst_ref=dst, send_sem=ssem.at[i], recv_sem=rsem.at[i],
            device_id=dev, device_id_type=MESH,
        )

    n_kx = x_send.shape[1]
    sends = [
        (has_r_hi, remote(e.at[:, :, pl.ds(rows, 2)], e.at[:, :, pl.ds(0, 2)], 0, r_hi)),
        (has_r_lo, remote(e.at[:, :, pl.ds(2, 2)], e.at[:, :, pl.ds(rows + 2, 2)], 1, r_lo)),
        (None, remote(az_send.at[1], az_recv.at[0], 2, a_hi)),
        (None, remote(az_send.at[0], az_recv.at[1], 3, a_lo)),
        (has_x_hi, remote(x_send.at[1], x_recv.at[0, pl.ds(0, n_kx)], 4, x_hi)),
        (has_x_lo, remote(x_send.at[0], x_recv.at[1, pl.ds(0, n_kx)], 5, x_lo)),
    ]
    recvs = [
        (has_r_lo, remote(e.at[:, :, pl.ds(rows, 2)], e.at[:, :, pl.ds(0, 2)], 0, r_lo)),
        (has_r_hi, remote(e.at[:, :, pl.ds(2, 2)], e.at[:, :, pl.ds(rows + 2, 2)], 1, r_hi)),
        (None, remote(az_send.at[1], az_recv.at[0], 2, a_lo)),
        (None, remote(az_send.at[0], az_recv.at[1], 3, a_hi)),
        (has_x_lo, remote(x_send.at[1], x_recv.at[0, pl.ds(0, n_kx)], 4, x_lo)),
        (has_x_hi, remote(x_send.at[0], x_recv.at[1, pl.ds(0, n_kx)], 5, x_hi)),
    ]

    def when(cond, fn):
        if cond is None:
            fn()
        else:
            pl.when(cond)(fn)

    for cond, c in sends:
        when(cond, c.start)

    @pl.when(jnp.logical_not(has_r_lo))
    def _():
        e[:, :, 0:2] = jnp.zeros((2, fields, 2, n_a, n_x), jnp.float32)

    @pl.when(jnp.logical_not(has_r_hi))
    def _():
        e[:, :, rows + 2:rows + 4] = jnp.zeros((2, fields, 2, n_a, n_x), jnp.float32)

    @pl.when(jnp.logical_not(has_x_lo))
    def _():
        x_recv[0, 0:n_kx, :] = jnp.zeros((n_kx, x_recv.shape[2]), jnp.float32)

    @pl.when(jnp.logical_not(has_x_hi))
    def _():
        x_recv[1, 0:n_kx, :] = jnp.zeros((n_kx, x_recv.shape[2]), jnp.float32)

    for cond, c in recvs:
        when(cond, c.wait_recv)

    for side in range(2):
        xt[side] = x_recv[side].T
        for k in range(2):
            for f in range(fields):
                for r in range(rows):
                    row = ((k * fields + f) * rows + r) * 2
                    az_exp[side, r, k * fields + f, 0:2, :] = az_recv[side, row:row + 2, :]

    sub = lax.broadcasted_iota(jnp.int32, (n_a, n_x), 0)
    lane = lax.broadcasted_iota(jnp.int32, (n_a, n_x), 1)

    def shifted_azi(u, lo, hi):
        um1 = jnp.where(sub == 0, jnp.broadcast_to(lo[1:2], u.shape), pltpu.roll(u, 1, 0))
        um2 = jnp.where(sub == 0, jnp.broadcast_to(lo[0:1], u.shape),
                        jnp.where(sub == 1, jnp.broadcast_to(lo[1:2], u.shape), pltpu.roll(u, 2, 0)))
        up1 = jnp.where(sub == n_a - 1, jnp.broadcast_to(hi[0:1], u.shape), pltpu.roll(u, n_a - 1, 0))
        up2 = jnp.where(sub == n_a - 1, jnp.broadcast_to(hi[1:2], u.shape),
                        jnp.where(sub == n_a - 2, jnp.broadcast_to(hi[0:1], u.shape), pltpu.roll(u, n_a - 2, 0)))
        return um2, um1, u, up1, up2

    def shifted_ax(u, lo0, lo1, hi0, hi1):
        um1 = jnp.where(lane == 0, jnp.broadcast_to(lo1, u.shape), pltpu.roll(u, 1, 1))
        um2 = jnp.where(lane == 0, jnp.broadcast_to(lo0, u.shape),
                        jnp.where(lane == 1, jnp.broadcast_to(lo1, u.shape), pltpu.roll(u, 2, 1)))
        up1 = jnp.where(lane == n_x - 1, jnp.broadcast_to(hi0, u.shape), pltpu.roll(u, n_x - 1, 1))
        up2 = jnp.where(lane == n_x - 1, jnp.broadcast_to(hi1, u.shape),
                        jnp.where(lane == n_x - 2, jnp.broadcast_to(hi0, u.shape), pltpu.roll(u, n_x - 2, 1)))
        return um2, um1, u, up1, up2

    def row_body(r, carry):
        base = pl.multiple_of(r * n_a, n_a)
        xlo = xt[0, pl.ds(base, n_a), :]
        xhi = xt[1, pl.ds(base, n_a), :]
        lo_s, hi_s, w = [], [], []
        for f in range(fields):
            lo, hi = faces(*[e[0, f, r + k] for k in range(5)])
            lo_s.append(lo)
            hi_s.append(hi)
            w.append(fourth(*[e[1, f, r + k] for k in range(5)]))
        balance = flux_pair(lo_s, hi_s, 0)
        weight = w
        lo_s, hi_s, w = [], [], []
        for f in range(fields):
            lo, hi = faces(*shifted_azi(e[0, f, r + 2], az_exp[0, r, f], az_exp[1, r, f]))
            lo_s.append(lo)
            hi_s.append(hi)
            w.append(fourth(*shifted_azi(e[1, f, r + 2], az_exp[0, r, fields + f], az_exp[1, r, fields + f])))
        part = flux_pair(lo_s, hi_s, 1)
        balance = [b + p for b, p in zip(balance, part)]
        weight = [a + b for a, b in zip(weight, w)]
        lo_s, hi_s, w = [], [], []
        for f in range(fields):
            cp, ca = 2 * f, 2 * (fields + f)
            lo, hi = faces(*shifted_ax(e[0, f, r + 2], xlo[:, cp:cp + 1], xlo[:, cp + 1:cp + 2],
                                       xhi[:, cp:cp + 1], xhi[:, cp + 1:cp + 2]))
            lo_s.append(lo)
            hi_s.append(hi)
            w.append(fourth(*shifted_ax(e[1, f, r + 2], xlo[:, ca:ca + 1], xlo[:, ca + 1:ca + 2],
                                        xhi[:, ca:ca + 1], xhi[:, ca + 1:ca + 2])))
        part = flux_pair(lo_s, hi_s, 2)
        balance = [b + p for b, p in zip(balance, part)]
        weight = [a + b for a, b in zip(weight, w)]
        total = weight[0] * balance[0]
        for f in range(1, fields):
            total = total + weight[f] * balance[f]
        out_ref[r] = jnp.abs(total)
        return carry

    lax.fori_loop(0, rows, row_body, 0)

    for cond, c in sends:
        when(cond, c.wait_send)


def stencil(primal, adjoint):
    fields, rows, n_a, n_x = primal.shape
    anywhere = pl.BlockSpec(memory_space=pltpu.HBM)
    return pl.pallas_call(
        stencil_kernel,
        out_shape=jax.ShapeDtypeStruct((rows, n_a, n_x), jnp.float32),
        in_specs=[anywhere, anywhere],
        out_specs=pl.BlockSpec(memory_space=pltpu.VMEM),
        scratch_shapes=[
            pltpu.VMEM((2, fields, rows + 4, n_a, n_x), jnp.float32),
            pltpu.VMEM((2, 2 * fields * rows * 2, n_x), jnp.float32),
            pltpu.VMEM((2, 2 * fields * rows * 2, n_x), jnp.float32),
            pltpu.VMEM((2, rows, 2 * fields, 8, n_x), jnp.float32),
            pltpu.VMEM((2, -(-4 * fields // 8) * 8, rows * n_a), jnp.float32),
            pltpu.VMEM((2, 128, rows * n_a), jnp.float32),
            pltpu.VMEM((2, rows * n_a, 128), jnp.float32),
            pltpu.SemaphoreType.DMA((2,)),
            pltpu.SemaphoreType.DMA((6,)),
            pltpu.SemaphoreType.DMA((6,)),
        ],
        compiler_params=pltpu.CompilerParams(
            collective_id=2, has_side_effects=True, vmem_limit_bytes=67043328
        ),
    )(primal, adjoint)


def on_device(primal, adjoint, refine_flag, owner_map, migrate_weight, neighbor_list):
    indicator = stencil(primal, adjoint)
    rows_rad, rows_azi, rows_ax = indicator.shape
    per_rad = rows_rad // BLK
    per_azi = rows_azi // BLK
    per_ax = rows_ax // BLK
    block_mean = indicator.reshape(per_rad, BLK, per_azi, BLK, per_ax, BLK).mean(axis=(1, 3, 5))
    all_means = gather_all(block_mean.reshape(-1), 0)
    size_rad = lax.axis_size("rad")
    size_azi = lax.axis_size("azi")
    size_ax = lax.axis_size("ax")
    blocks_azi = per_azi * size_azi
    blocks_ax = per_ax * size_ax
    block_rad = neighbor_list // (blocks_azi * blocks_ax)
    block_azi = neighbor_list // blocks_ax % blocks_azi
    block_ax = neighbor_list % blocks_ax
    owner_dev = (
        block_rad // per_rad * size_azi + block_azi // per_azi
    ) * size_ax + block_ax // per_ax
    local_pos = (block_rad % per_rad * per_azi + block_azi % per_azi) * per_ax + block_ax % per_ax
    position = owner_dev * (per_rad * per_azi * per_ax) + local_pos
    beside_all = jnp.mean(jnp.take(all_means, position), axis=-1)
    smooth = 0.5 * block_mean + 0.5 * beside_all
    own_index = (
        lax.axis_index("rad") * size_azi + lax.axis_index("azi")
    ) * size_ax + lax.axis_index("ax")
    moved = (owner_map != own_index).astype(jnp.float32)
    block_cost = (
        smooth * (1.0 + 7.0 * refine_flag.astype(jnp.float32))
        + 0.25 * migrate_weight.astype(jnp.float32) * moved
    )
    width = block_cost.size
    payload = jnp.concatenate([block_cost.reshape(-1), owner_map.reshape(-1).astype(jnp.float32)])
    gathered = gather_all(payload, 1).reshape(-1, 2 * width)
    cost_all = gathered[:, :width]
    owner_all = gathered[:, width:]
    total = jnp.sum(jnp.where(owner_all == own_index.astype(jnp.float32), cost_all, 0.0))
    owner_load = (total / (per_rad * per_azi * per_ax)).reshape(1, 1, 1)
    return (indicator, block_cost, owner_load)


def solution(mesh):
    return jax.shard_map(
        on_device,
        mesh=mesh,
        in_specs=(
            P(None, "rad", "azi", "ax"),
            P(None, "rad", "azi", "ax"),
            P("rad", "azi", "ax"),
            P("rad", "azi", "ax"),
            P("rad", "azi", "ax"),
            P("rad", "azi", "ax", None),
        ),
        out_specs=(P("rad", "azi", "ax"), P("rad", "azi", "ax"), P("rad", "azi", "ax")),
        check_vma=False,
    )
```

```python
import functools
import itertools
import jax
import jax.numpy as jnp
from jax import lax
from jax.experimental import pallas as pl
from jax.experimental.pallas import tpu as pltpu
from jax.sharding import PartitionSpec as P

BLK = 16
AXES = ("rad", "azi", "ax")
MESH = pl.DeviceIdType.MESH


def stage_plan(sizes, groups):
    plan = []
    for axes in groups:
        offs = [o for o in itertools.product(*[range(sizes[i]) for i in axes]) if any(o)]
        plan.append((axes, offs))
    return plan


def gen_gather_kernel(sizes, groups, x_ref, o_ref, lsem, ssem, rsem, with_barrier=True):
    me = tuple(lax.axis_index(a) for a in AXES)
    plan = stage_plan(sizes, groups)

    def shift(off_axes, off, sign):
        dev = list(me)
        for i, o in zip(off_axes, off):
            dev[i] = lax.rem(me[i] + (o if sign > 0 else sizes[i] - o), sizes[i])
        return tuple(dev)

    if with_barrier:
        barrier = pltpu.get_barrier_semaphore()
        count = 0
        for axes, offs in plan:
            for off in offs:
                pl.semaphore_signal(barrier, 1, device_id=shift(axes, off, 1), device_id_type=MESH)
                count += 1
        pl.semaphore_wait(barrier, count)

    covered = set()

    def region(dev):
        idx = []
        for i in range(3):
            if i in covered:
                break
            idx.append(pl.ds(dev[i], 1))
        return o_ref.at[tuple(idx)] if idx else o_ref

    def region_full(dev):
        n_fixed = 3 - len(covered)
        return o_ref.at[tuple(pl.ds(dev[i], 1) for i in range(n_fixed))]

    local = pltpu.make_async_copy(x_ref, o_ref.at[tuple(pl.ds(m, 1) for m in me)], lsem)
    local.start()
    sends = []
    slot = 0
    for stage, (axes, offs) in enumerate(plan):
        src = x_ref if stage == 0 else region_full(me)
        first = slot
        for off in offs:
            c = pltpu.make_async_remote_copy(src_ref=src, dst_ref=region_full(me), send_sem=ssem.at[slot],
                                             recv_sem=rsem.at[slot], device_id=shift(axes, off, 1), device_id_type=MESH)
            c.start()
            sends.append(c)
            slot += 1
        slot = first
        for off in offs:
            frm = shift(axes, off, -1)
            c = pltpu.make_async_remote_copy(src_ref=src, dst_ref=region_full(frm), send_sem=ssem.at[slot],
                                             recv_sem=rsem.at[slot], device_id=frm, device_id_type=MESH)
            c.wait_recv()
            slot += 1
        if stage == 0:
            local.wait()
        covered.update(axes)
    return sends


def gather_kernel(sizes, groups, x_ref, o_ref, lsem, ssem, rsem):
    for c in gen_gather_kernel(sizes, groups, x_ref, o_ref, lsem, ssem, rsem):
        c.wait_send()


def gather_all(values, cid, groups=((2, 1), (0,))):
    sizes = tuple(lax.axis_size(a) for a in AXES)
    width = values.shape[0]
    links = sum(len(offs) for _, offs in stage_plan(sizes, groups))
    out = pl.pallas_call(
        functools.partial(gather_kernel, sizes, groups),
        out_shape=jax.ShapeDtypeStruct(sizes + (width,), jnp.float32),
        in_specs=[pl.BlockSpec(memory_space=pltpu.VMEM)],
        out_specs=pl.BlockSpec(memory_space=pltpu.VMEM),
        scratch_shapes=[pltpu.SemaphoreType.DMA(()), pltpu.SemaphoreType.DMA((links,)), pltpu.SemaphoreType.DMA((links,))],
        compiler_params=pltpu.CompilerParams(collective_id=cid, has_side_effects=True),
    )(values.reshape(1, 1, 1, width))
    return out.reshape(-1)


def dense(x):
    return x.reshape(-1, 128)


def exchange(tail, head, axis, periodic):
    count = lax.axis_size(axis)
    forward = [(i, i + 1) for i in range(count - 1)]
    if periodic:
        forward.append((count - 1, 0))
    backward = [(target, source) for source, target in forward]
    low = lax.ppermute(dense(tail), axis, forward).reshape(tail.shape)
    high = lax.ppermute(dense(head), axis, backward).reshape(head.shape)
    return low, high


def flux_pair(state_lo, state_hi, along):
    return [h - l for h, l in zip(euler_flux(state_hi, along), euler_flux(state_lo, along))]


def euler_flux(s, along):
    density, m0, m1, m2, energy = s
    momenta = (m0, m1, m2)
    inv = 1.0 / density
    velocity = momenta[along] * inv
    kinetic = 0.5 * (m0 * m0 + m1 * m1 + m2 * m2) * inv
    pressure = 0.4 * (energy - kinetic)
    columns = [momenta[along], m0 * velocity, m1 * velocity, m2 * velocity, (energy + pressure) * velocity]
    columns[1 + along] = columns[1 + along] + pressure
    return columns


def faces(um2, um1, u, up1, up2):
    lower = (7.0 * um1 - um2) / 12.0 + (7.0 * u - up1) / 12.0
    upper = (7.0 * u - um1) / 12.0 + (7.0 * up1 - up2) / 12.0
    return lower, upper


def fourth(zm2, zm1, z, zp1, zp2):
    return (zm2 - 4.0 * zm1 + 6.0 * z - 4.0 * zp1 + zp2) / 12.0


def stencil_kernel(groups, p_hbm, a_hbm, out_ref, g_out, e, az_send, az_recv, az_exp, x_send, x_recv, xt, sems, ssem, rsem,
                   pay, glsem, gssem, grsem):
    _, fields, ext_rows, n_a, n_x = e.shape
    rows = ext_rows - 4
    n_r_dev, n_a_dev, n_x_dev = (lax.axis_size(ax) for ax in AXES)
    me_r, me_a, me_x = (lax.axis_index(ax) for ax in AXES)
    has_r_lo, has_r_hi = me_r > 0, me_r < n_r_dev - 1
    has_x_lo, has_x_hi = me_x > 0, me_x < n_x_dev - 1
    r_lo, r_hi = (me_r - 1, me_a, me_x), (me_r + 1, me_a, me_x)
    a_lo = (me_r, lax.rem(me_a + n_a_dev - 1, n_a_dev), me_x)
    a_hi = (me_r, lax.rem(me_a + 1, n_a_dev), me_x)
    x_lo, x_hi = (me_r, me_a, me_x - 1), (me_r, me_a, me_x + 1)

    loads = [
        pltpu.make_async_copy(p_hbm, e.at[0, :, pl.ds(2, rows)], sems.at[0]),
        pltpu.make_async_copy(a_hbm, e.at[1, :, pl.ds(2, rows)], sems.at[1]),
    ]
    for c in loads:
        c.start()

    sizes = (n_r_dev, n_a_dev, n_x_dev)
    me = (me_r, me_a, me_x)
    barrier = pltpu.get_barrier_semaphore()
    n_peers = 0
    for axes, offs in stage_plan(sizes, groups):
        for off in offs:
            dev = list(me)
            for i, o in zip(axes, off):
                dev[i] = lax.rem(me[i] + o, sizes[i])
            pl.semaphore_signal(barrier, 1, device_id=tuple(dev), device_id_type=MESH)
            n_peers += 1
    pl.semaphore_wait(barrier, n_peers)

    x_recv[:, x_send.shape[1]:, :] = jnp.zeros((2, x_recv.shape[1] - x_send.shape[1], x_recv.shape[2]), jnp.float32)
    x_send[:, 4 * fields:, :] = jnp.zeros((2, x_send.shape[1] - 4 * fields, x_send.shape[2]), jnp.float32)
    for c in loads:
        c.wait()

    for k in range(2):
        for f in range(fields):
            for r in range(rows):
                row = ((k * fields + f) * rows + r) * 2
                az_send[0, row:row + 2, :] = e[k, f, 2 + r, 0:2, :]
                az_send[1, row:row + 2, :] = e[k, f, 2 + r, n_a - 2:n_a, :]
            plane = e[k, f, 2:2 + rows].reshape(rows * n_a, n_x)
            cols = plane.T
            row = (k * fields + f) * 2
            x_send[0, row:row + 2, :] = cols[0:2]
            x_send[1, row:row + 2, :] = cols[n_x - 2:n_x]

    def remote(src, dst, i, dev):
        return pltpu.make_async_remote_copy(
            src_ref=src, dst_ref=dst, send_sem=ssem.at[i], recv_sem=rsem.at[i],
            device_id=dev, device_id_type=MESH,
        )

    n_kx = x_send.shape[1]
    sends = [
        (has_r_hi, remote(e.at[:, :, pl.ds(rows, 2)], e.at[:, :, pl.ds(0, 2)], 0, r_hi)),
        (has_r_lo, remote(e.at[:, :, pl.ds(2, 2)], e.at[:, :, pl.ds(rows + 2, 2)], 1, r_lo)),
        (None, remote(az_send.at[1], az_recv.at[0], 2, a_hi)),
        (None, remote(az_send.at[0], az_recv.at[1], 3, a_lo)),
        (has_x_hi, remote(x_send.at[1], x_recv.at[0, pl.ds(0, n_kx)], 4, x_hi)),
        (has_x_lo, remote(x_send.at[0], x_recv.at[1, pl.ds(0, n_kx)], 5, x_lo)),
    ]
    recvs = [
        (has_r_lo, remote(e.at[:, :, pl.ds(rows, 2)], e.at[:, :, pl.ds(0, 2)], 0, r_lo)),
        (has_r_hi, remote(e.at[:, :, pl.ds(2, 2)], e.at[:, :, pl.ds(rows + 2, 2)], 1, r_hi)),
        (None, remote(az_send.at[1], az_recv.at[0], 2, a_lo)),
        (None, remote(az_send.at[0], az_recv.at[1], 3, a_hi)),
        (has_x_lo, remote(x_send.at[1], x_recv.at[0, pl.ds(0, n_kx)], 4, x_lo)),
        (has_x_hi, remote(x_send.at[0], x_recv.at[1, pl.ds(0, n_kx)], 5, x_hi)),
    ]

    def when(cond, fn):
        if cond is None:
            fn()
        else:
            pl.when(cond)(fn)

    for cond, c in sends:
        when(cond, c.start)

    @pl.when(jnp.logical_not(has_r_lo))
    def _():
        e[:, :, 0:2] = jnp.zeros((2, fields, 2, n_a, n_x), jnp.float32)

    @pl.when(jnp.logical_not(has_r_hi))
    def _():
        e[:, :, rows + 2:rows + 4] = jnp.zeros((2, fields, 2, n_a, n_x), jnp.float32)

    @pl.when(jnp.logical_not(has_x_lo))
    def _():
        x_recv[0, 0:n_kx, :] = jnp.zeros((n_kx, x_recv.shape[2]), jnp.float32)

    @pl.when(jnp.logical_not(has_x_hi))
    def _():
        x_recv[1, 0:n_kx, :] = jnp.zeros((n_kx, x_recv.shape[2]), jnp.float32)

    for cond, c in recvs:
        when(cond, c.wait_recv)

    for side in range(2):
        xt[side] = x_recv[side].T
        for k in range(2):
            for f in range(fields):
                for r in range(rows):
                    row = ((k * fields + f) * rows + r) * 2
                    az_exp[side, r, k * fields + f, 0:2, :] = az_recv[side, row:row + 2, :]

    sub = lax.broadcasted_iota(jnp.int32, (n_a, n_x), 0)
    lane = lax.broadcasted_iota(jnp.int32, (n_a, n_x), 1)

    def shifted_azi(u, lo, hi):
        um1 = jnp.where(sub == 0, jnp.broadcast_to(lo[1:2], u.shape), pltpu.roll(u, 1, 0))
        um2 = jnp.where(sub == 0, jnp.broadcast_to(lo[0:1], u.shape),
                        jnp.where(sub == 1, jnp.broadcast_to(lo[1:2], u.shape), pltpu.roll(u, 2, 0)))
        up1 = jnp.where(sub == n_a - 1, jnp.broadcast_to(hi[0:1], u.shape), pltpu.roll(u, n_a - 1, 0))
        up2 = jnp.where(sub == n_a - 1, jnp.broadcast_to(hi[1:2], u.shape),
                        jnp.where(sub == n_a - 2, jnp.broadcast_to(hi[0:1], u.shape), pltpu.roll(u, n_a - 2, 0)))
        return um2, um1, u, up1, up2

    def shifted_ax(u, lo0, lo1, hi0, hi1):
        um1 = jnp.where(lane == 0, jnp.broadcast_to(lo1, u.shape), pltpu.roll(u, 1, 1))
        um2 = jnp.where(lane == 0, jnp.broadcast_to(lo0, u.shape),
                        jnp.where(lane == 1, jnp.broadcast_to(lo1, u.shape), pltpu.roll(u, 2, 1)))
        up1 = jnp.where(lane == n_x - 1, jnp.broadcast_to(hi0, u.shape), pltpu.roll(u, n_x - 1, 1))
        up2 = jnp.where(lane == n_x - 1, jnp.broadcast_to(hi1, u.shape),
                        jnp.where(lane == n_x - 2, jnp.broadcast_to(hi0, u.shape), pltpu.roll(u, n_x - 2, 1)))
        return um2, um1, u, up1, up2

    def row_body(r, carry):
        base = pl.multiple_of(r * n_a, n_a)
        xlo = xt[0, pl.ds(base, n_a), :]
        xhi = xt[1, pl.ds(base, n_a), :]
        lo_s, hi_s, w = [], [], []
        for f in range(fields):
            lo, hi = faces(*[e[0, f, r + k] for k in range(5)])
            lo_s.append(lo)
            hi_s.append(hi)
            w.append(fourth(*[e[1, f, r + k] for k in range(5)]))
        balance = flux_pair(lo_s, hi_s, 0)
        weight = w
        lo_s, hi_s, w = [], [], []
        for f in range(fields):
            lo, hi = faces(*shifted_azi(e[0, f, r + 2], az_exp[0, r, f], az_exp[1, r, f]))
            lo_s.append(lo)
            hi_s.append(hi)
            w.append(fourth(*shifted_azi(e[1, f, r + 2], az_exp[0, r, fields + f], az_exp[1, r, fields + f])))
        part = flux_pair(lo_s, hi_s, 1)
        balance = [b + p for b, p in zip(balance, part)]
        weight = [a + b for a, b in zip(weight, w)]
        lo_s, hi_s, w = [], [], []
        for f in range(fields):
            cp, ca = 2 * f, 2 * (fields + f)
            lo, hi = faces(*shifted_ax(e[0, f, r + 2], xlo[:, cp:cp + 1], xlo[:, cp + 1:cp + 2],
                                       xhi[:, cp:cp + 1], xhi[:, cp + 1:cp + 2]))
            lo_s.append(lo)
            hi_s.append(hi)
            w.append(fourth(*shifted_ax(e[1, f, r + 2], xlo[:, ca:ca + 1], xlo[:, ca + 1:ca + 2],
                                        xhi[:, ca:ca + 1], xhi[:, ca + 1:ca + 2])))
        part = flux_pair(lo_s, hi_s, 2)
        balance = [b + p for b, p in zip(balance, part)]
        weight = [a + b for a, b in zip(weight, w)]
        total = weight[0] * balance[0]
        for f in range(1, fields):
            total = total + weight[f] * balance[f]
        value = jnp.abs(total)
        out_ref[r] = value
        return carry + value

    acc = lax.fori_loop(0, rows, row_body, jnp.zeros((n_a, n_x), jnp.float32))
    per_azi, per_ax = n_a // BLK, n_x // BLK
    width = per_azi * per_ax
    lane_l = lax.broadcasted_iota(jnp.int32, (n_x, width), 0)
    col_j = lax.broadcasted_iota(jnp.int32, (n_x, width), 1)
    means = None
    for ba in range(per_azi):
        half = jnp.sum(acc[ba * BLK:(ba + 1) * BLK], axis=0, keepdims=True)
        pick = jnp.where((col_j // per_ax == ba) & (lane_l // BLK == col_j % per_ax), 1.0, 0.0)
        part = jnp.dot(half, pick, precision=lax.Precision.HIGHEST, preferred_element_type=jnp.float32)
        means = part if means is None else means + part
    pay[0, 0] = means / float(rows * BLK * BLK)
    sends_g = gen_gather_kernel(sizes, groups, pay, g_out, glsem, gssem, grsem, with_barrier=False)

    for cond, c in sends:
        when(cond, c.wait_send)
    for c in sends_g:
        c.wait_send()


def stencil(primal, adjoint, groups=((2, 1), (0,))):
    fields, rows, n_a, n_x = primal.shape
    anywhere = pl.BlockSpec(memory_space=pltpu.HBM)
    sizes = tuple(lax.axis_size(a) for a in AXES)
    width = (n_a // BLK) * (n_x // BLK)
    links = sum(len(offs) for _, offs in stage_plan(sizes, groups))
    return pl.pallas_call(
        functools.partial(stencil_kernel, groups),
        out_shape=(jax.ShapeDtypeStruct((rows, n_a, n_x), jnp.float32), jax.ShapeDtypeStruct(sizes + (width,), jnp.float32)),
        in_specs=[anywhere, anywhere],
        out_specs=(pl.BlockSpec(memory_space=pltpu.VMEM), pl.BlockSpec(memory_space=pltpu.VMEM)),
        scratch_shapes=[
            pltpu.VMEM((2, fields, rows + 4, n_a, n_x), jnp.float32),
            pltpu.VMEM((2, 2 * fields * rows * 2, n_x), jnp.float32),
            pltpu.VMEM((2, 2 * fields * rows * 2, n_x), jnp.float32),
            pltpu.VMEM((2, rows, 2 * fields, 8, n_x), jnp.float32),
            pltpu.VMEM((2, -(-4 * fields // 8) * 8, rows * n_a), jnp.float32),
            pltpu.VMEM((2, 128, rows * n_a), jnp.float32),
            pltpu.VMEM((2, rows * n_a, 128), jnp.float32),
            pltpu.SemaphoreType.DMA((2,)),
            pltpu.SemaphoreType.DMA((6,)),
            pltpu.SemaphoreType.DMA((6,)),
            pltpu.VMEM((1, 1, 1, width), jnp.float32),
            pltpu.SemaphoreType.DMA(()),
            pltpu.SemaphoreType.DMA((links,)),
            pltpu.SemaphoreType.DMA((links,)),
        ],
        compiler_params=pltpu.CompilerParams(
            collective_id=2, has_side_effects=True, vmem_limit_bytes=67043328
        ),
    )(primal, adjoint)


def on_device(primal, adjoint, refine_flag, owner_map, migrate_weight, neighbor_list):
    indicator, gathered_means = stencil(primal, adjoint)
    rows_rad, rows_azi, rows_ax = indicator.shape
    per_rad = rows_rad // BLK
    per_azi = rows_azi // BLK
    per_ax = rows_ax // BLK
    all_means = gathered_means.reshape(-1)
    me_dev = (lax.axis_index("rad") * lax.axis_size("azi") + lax.axis_index("azi")) * lax.axis_size("ax") + lax.axis_index("ax")
    block_mean = lax.dynamic_slice_in_dim(all_means, me_dev * (per_rad * per_azi * per_ax), per_rad * per_azi * per_ax).reshape(per_rad, per_azi, per_ax)
    size_rad = lax.axis_size("rad")
    size_azi = lax.axis_size("azi")
    size_ax = lax.axis_size("ax")
    blocks_azi = per_azi * size_azi
    blocks_ax = per_ax * size_ax
    block_rad = neighbor_list // (blocks_azi * blocks_ax)
    block_azi = neighbor_list // blocks_ax % blocks_azi
    block_ax = neighbor_list % blocks_ax
    owner_dev = (
        block_rad // per_rad * size_azi + block_azi // per_azi
    ) * size_ax + block_ax // per_ax
    local_pos = (block_rad % per_rad * per_azi + block_azi % per_azi) * per_ax + block_ax % per_ax
    position = owner_dev * (per_rad * per_azi * per_ax) + local_pos
    beside_all = jnp.mean(jnp.take(all_means, position), axis=-1)
    smooth = 0.5 * block_mean + 0.5 * beside_all
    own_index = (
        lax.axis_index("rad") * size_azi + lax.axis_index("azi")
    ) * size_ax + lax.axis_index("ax")
    moved = (owner_map != own_index).astype(jnp.float32)
    block_cost = (
        smooth * (1.0 + 7.0 * refine_flag.astype(jnp.float32))
        + 0.25 * migrate_weight.astype(jnp.float32) * moved
    )
    width = block_cost.size
    payload = jnp.concatenate([block_cost.reshape(-1), owner_map.reshape(-1).astype(jnp.float32)])
    gathered = gather_all(payload, 1).reshape(-1, 2 * width)
    cost_all = gathered[:, :width]
    owner_all = gathered[:, width:]
    total = jnp.sum(jnp.where(owner_all == own_index.astype(jnp.float32), cost_all, 0.0))
    owner_load = (total / (per_rad * per_azi * per_ax)).reshape(1, 1, 1)
    return (indicator, block_cost, owner_load)


def solution(mesh):
    return jax.shard_map(
        on_device,
        mesh=mesh,
        in_specs=(
            P(None, "rad", "azi", "ax"),
            P(None, "rad", "azi", "ax"),
            P("rad", "azi", "ax"),
            P("rad", "azi", "ax"),
            P("rad", "azi", "ax"),
            P("rad", "azi", "ax", None),
        ),
        out_specs=(P("rad", "azi", "ax"), P("rad", "azi", "ax"), P("rad", "azi", "ax")),
        check_vma=False,
    )
```

```python
import functools
import itertools
import jax
import jax.numpy as jnp
from jax import lax
from jax.experimental import pallas as pl
from jax.experimental.pallas import tpu as pltpu
from jax.sharding import PartitionSpec as P

BLK = 16
AXES = ("rad", "azi", "ax")
MESH = pl.DeviceIdType.MESH


def stage_plan(sizes, groups):
    plan = []
    for axes in groups:
        offs = [o for o in itertools.product(*[range(sizes[i]) for i in axes]) if any(o)]
        plan.append((axes, offs))
    return plan


def gen_gather_kernel(sizes, groups, x_ref, o_ref, lsem, ssem, rsem, with_barrier=True):
    me = tuple(lax.axis_index(a) for a in AXES)
    plan = stage_plan(sizes, groups)

    def shift(off_axes, off, sign):
        dev = list(me)
        for i, o in zip(off_axes, off):
            dev[i] = lax.rem(me[i] + (o if sign > 0 else sizes[i] - o), sizes[i])
        return tuple(dev)

    if with_barrier:
        barrier = pltpu.get_barrier_semaphore()
        count = 0
        for axes, offs in plan:
            for off in offs:
                pl.semaphore_signal(barrier, 1, device_id=shift(axes, off, 1), device_id_type=MESH)
                count += 1
        pl.semaphore_wait(barrier, count)

    covered = set()

    def region(dev):
        idx = []
        for i in range(3):
            if i in covered:
                break
            idx.append(pl.ds(dev[i], 1))
        return o_ref.at[tuple(idx)] if idx else o_ref

    def region_full(dev):
        n_fixed = 3 - len(covered)
        return o_ref.at[tuple(pl.ds(dev[i], 1) for i in range(n_fixed))]

    local = pltpu.make_async_copy(x_ref, o_ref.at[tuple(pl.ds(m, 1) for m in me)], lsem)
    local.start()
    sends = []
    slot = 0
    for stage, (axes, offs) in enumerate(plan):
        src = x_ref if stage == 0 else region_full(me)
        first = slot
        for off in offs:
            c = pltpu.make_async_remote_copy(src_ref=src, dst_ref=region_full(me), send_sem=ssem.at[slot],
                                             recv_sem=rsem.at[slot], device_id=shift(axes, off, 1), device_id_type=MESH)
            c.start()
            sends.append(c)
            slot += 1
        slot = first
        for off in offs:
            frm = shift(axes, off, -1)
            c = pltpu.make_async_remote_copy(src_ref=src, dst_ref=region_full(frm), send_sem=ssem.at[slot],
                                             recv_sem=rsem.at[slot], device_id=frm, device_id_type=MESH)
            c.wait_recv()
            slot += 1
        if stage == 0:
            local.wait()
        covered.update(axes)
    return sends


def gather_kernel(sizes, groups, x_ref, o_ref, lsem, ssem, rsem):
    for c in gen_gather_kernel(sizes, groups, x_ref, o_ref, lsem, ssem, rsem):
        c.wait_send()


def gather_all(values, cid, groups=((2, 1), (0,))):
    sizes = tuple(lax.axis_size(a) for a in AXES)
    width = values.shape[0]
    links = sum(len(offs) for _, offs in stage_plan(sizes, groups))
    out = pl.pallas_call(
        functools.partial(gather_kernel, sizes, groups),
        out_shape=jax.ShapeDtypeStruct(sizes + (width,), jnp.float32),
        in_specs=[pl.BlockSpec(memory_space=pltpu.VMEM)],
        out_specs=pl.BlockSpec(memory_space=pltpu.VMEM),
        scratch_shapes=[pltpu.SemaphoreType.DMA(()), pltpu.SemaphoreType.DMA((links,)), pltpu.SemaphoreType.DMA((links,))],
        compiler_params=pltpu.CompilerParams(collective_id=cid, has_side_effects=True),
    )(values.reshape(1, 1, 1, width))
    return out.reshape(-1)


def dense(x):
    return x.reshape(-1, 128)


def exchange(tail, head, axis, periodic):
    count = lax.axis_size(axis)
    forward = [(i, i + 1) for i in range(count - 1)]
    if periodic:
        forward.append((count - 1, 0))
    backward = [(target, source) for source, target in forward]
    low = lax.ppermute(dense(tail), axis, forward).reshape(tail.shape)
    high = lax.ppermute(dense(head), axis, backward).reshape(head.shape)
    return low, high


def flux_pair(state_lo, state_hi, along):
    return [h - l for h, l in zip(euler_flux(state_hi, along), euler_flux(state_lo, along))]


def euler_flux(s, along):
    density, m0, m1, m2, energy = s
    momenta = (m0, m1, m2)
    inv = 1.0 / density
    velocity = momenta[along] * inv
    kinetic = 0.5 * (m0 * m0 + m1 * m1 + m2 * m2) * inv
    pressure = 0.4 * (energy - kinetic)
    columns = [momenta[along], m0 * velocity, m1 * velocity, m2 * velocity, (energy + pressure) * velocity]
    columns[1 + along] = columns[1 + along] + pressure
    return columns


def faces(um2, um1, u, up1, up2):
    lower = (7.0 * um1 - um2) / 12.0 + (7.0 * u - up1) / 12.0
    upper = (7.0 * u - um1) / 12.0 + (7.0 * up1 - up2) / 12.0
    return lower, upper


def fourth(zm2, zm1, z, zp1, zp2):
    return (zm2 - 4.0 * zm1 + 6.0 * z - 4.0 * zp1 + zp2) / 12.0


def stencil_kernel(groups, p_hbm, a_hbm, out_ref, g_out, e, az_send, az_recv, az_exp, x_send, x_recv, xt, sems, ssem, rsem,
                   pay, glsem, gssem, grsem):
    _, fields, ext_rows, n_a, n_x = e.shape
    rows = ext_rows - 4
    n_r_dev, n_a_dev, n_x_dev = (lax.axis_size(ax) for ax in AXES)
    me_r, me_a, me_x = (lax.axis_index(ax) for ax in AXES)
    has_r_lo, has_r_hi = me_r > 0, me_r < n_r_dev - 1
    has_x_lo, has_x_hi = me_x > 0, me_x < n_x_dev - 1
    r_lo, r_hi = (me_r - 1, me_a, me_x), (me_r + 1, me_a, me_x)
    a_lo = (me_r, lax.rem(me_a + n_a_dev - 1, n_a_dev), me_x)
    a_hi = (me_r, lax.rem(me_a + 1, n_a_dev), me_x)
    x_lo, x_hi = (me_r, me_a, me_x - 1), (me_r, me_a, me_x + 1)

    loads = [
        pltpu.make_async_copy(p_hbm, e.at[0, :, pl.ds(2, rows)], sems.at[0]),
        pltpu.make_async_copy(a_hbm, e.at[1, :, pl.ds(2, rows)], sems.at[1]),
    ]
    for c in loads:
        c.start()

    sizes = (n_r_dev, n_a_dev, n_x_dev)
    me = (me_r, me_a, me_x)
    barrier = pltpu.get_barrier_semaphore()
    n_peers = 0
    for axes, offs in stage_plan(sizes, groups):
        for off in offs:
            dev = list(me)
            for i, o in zip(axes, off):
                dev[i] = lax.rem(me[i] + o, sizes[i])
            pl.semaphore_signal(barrier, 1, device_id=tuple(dev), device_id_type=MESH)
            n_peers += 1
    pl.semaphore_wait(barrier, n_peers)

    x_recv[:, x_send.shape[1]:, :] = jnp.zeros((2, x_recv.shape[1] - x_send.shape[1], x_recv.shape[2]), jnp.float32)
    x_send[:, 4 * fields:, :] = jnp.zeros((2, x_send.shape[1] - 4 * fields, x_send.shape[2]), jnp.float32)
    for c in loads:
        c.wait()

    def remote(src, dst, i, dev):
        return pltpu.make_async_remote_copy(
            src_ref=src, dst_ref=dst, send_sem=ssem.at[i], recv_sem=rsem.at[i],
            device_id=dev, device_id_type=MESH,
        )

    n_kx = x_send.shape[1]
    sends = [
        (has_r_hi, remote(e.at[:, :, pl.ds(rows, 2)], e.at[:, :, pl.ds(0, 2)], 0, r_hi)),
        (has_r_lo, remote(e.at[:, :, pl.ds(2, 2)], e.at[:, :, pl.ds(rows + 2, 2)], 1, r_lo)),
        (None, remote(az_send.at[1], az_recv.at[0], 2, a_hi)),
        (None, remote(az_send.at[0], az_recv.at[1], 3, a_lo)),
        (has_x_hi, remote(x_send.at[1], x_recv.at[0, pl.ds(0, n_kx)], 4, x_hi)),
        (has_x_lo, remote(x_send.at[0], x_recv.at[1, pl.ds(0, n_kx)], 5, x_lo)),
    ]
    recvs = [
        (has_r_lo, remote(e.at[:, :, pl.ds(rows, 2)], e.at[:, :, pl.ds(0, 2)], 0, r_lo)),
        (has_r_hi, remote(e.at[:, :, pl.ds(2, 2)], e.at[:, :, pl.ds(rows + 2, 2)], 1, r_hi)),
        (None, remote(az_send.at[1], az_recv.at[0], 2, a_lo)),
        (None, remote(az_send.at[0], az_recv.at[1], 3, a_hi)),
        (has_x_lo, remote(x_send.at[1], x_recv.at[0, pl.ds(0, n_kx)], 4, x_lo)),
        (has_x_hi, remote(x_send.at[0], x_recv.at[1, pl.ds(0, n_kx)], 5, x_hi)),
    ]

    def when(cond, fn):
        if cond is None:
            fn()
        else:
            pl.when(cond)(fn)

    for cond, c in sends[:2]:
        when(cond, c.start)

    for k in range(2):
        for f in range(fields):
            for r in range(rows):
                row = ((k * fields + f) * rows + r) * 2
                az_send[0, row:row + 2, :] = e[k, f, 2 + r, 0:2, :]
                az_send[1, row:row + 2, :] = e[k, f, 2 + r, n_a - 2:n_a, :]
            plane = e[k, f, 2:2 + rows].reshape(rows * n_a, n_x)
            cols = plane.T
            row = (k * fields + f) * 2
            x_send[0, row:row + 2, :] = cols[0:2]
            x_send[1, row:row + 2, :] = cols[n_x - 2:n_x]

    for cond, c in sends[2:]:
        when(cond, c.start)

    @pl.when(jnp.logical_not(has_r_lo))
    def _():
        e[:, :, 0:2] = jnp.zeros((2, fields, 2, n_a, n_x), jnp.float32)

    @pl.when(jnp.logical_not(has_r_hi))
    def _():
        e[:, :, rows + 2:rows + 4] = jnp.zeros((2, fields, 2, n_a, n_x), jnp.float32)

    @pl.when(jnp.logical_not(has_x_lo))
    def _():
        x_recv[0, 0:n_kx, :] = jnp.zeros((n_kx, x_recv.shape[2]), jnp.float32)

    @pl.when(jnp.logical_not(has_x_hi))
    def _():
        x_recv[1, 0:n_kx, :] = jnp.zeros((n_kx, x_recv.shape[2]), jnp.float32)

    for cond, c in recvs[2:]:
        when(cond, c.wait_recv)

    for side in range(2):
        xt[side] = x_recv[side].T
        for k in range(2):
            for f in range(fields):
                for r in range(rows):
                    row = ((k * fields + f) * rows + r) * 2
                    az_exp[side, r, k * fields + f, 0:2, :] = az_recv[side, row:row + 2, :]

    sub = lax.broadcasted_iota(jnp.int32, (n_a, n_x), 0)
    lane = lax.broadcasted_iota(jnp.int32, (n_a, n_x), 1)

    def shifted_azi(u, lo, hi):
        um1 = jnp.where(sub == 0, jnp.broadcast_to(lo[1:2], u.shape), pltpu.roll(u, 1, 0))
        um2 = jnp.where(sub == 0, jnp.broadcast_to(lo[0:1], u.shape),
                        jnp.where(sub == 1, jnp.broadcast_to(lo[1:2], u.shape), pltpu.roll(u, 2, 0)))
        up1 = jnp.where(sub == n_a - 1, jnp.broadcast_to(hi[0:1], u.shape), pltpu.roll(u, n_a - 1, 0))
        up2 = jnp.where(sub == n_a - 1, jnp.broadcast_to(hi[1:2], u.shape),
                        jnp.where(sub == n_a - 2, jnp.broadcast_to(hi[0:1], u.shape), pltpu.roll(u, n_a - 2, 0)))
        return um2, um1, u, up1, up2

    def shifted_ax(u, lo0, lo1, hi0, hi1):
        um1 = jnp.where(lane == 0, jnp.broadcast_to(lo1, u.shape), pltpu.roll(u, 1, 1))
        um2 = jnp.where(lane == 0, jnp.broadcast_to(lo0, u.shape),
                        jnp.where(lane == 1, jnp.broadcast_to(lo1, u.shape), pltpu.roll(u, 2, 1)))
        up1 = jnp.where(lane == n_x - 1, jnp.broadcast_to(hi0, u.shape), pltpu.roll(u, n_x - 1, 1))
        up2 = jnp.where(lane == n_x - 1, jnp.broadcast_to(hi1, u.shape),
                        jnp.where(lane == n_x - 2, jnp.broadcast_to(hi0, u.shape), pltpu.roll(u, n_x - 2, 1)))
        return um2, um1, u, up1, up2

    def row_body(r, carry):
        base = pl.multiple_of(r * n_a, n_a)
        xlo = xt[0, pl.ds(base, n_a), :]
        xhi = xt[1, pl.ds(base, n_a), :]
        lo_s, hi_s, w = [], [], []
        for f in range(fields):
            lo, hi = faces(*[e[0, f, r + k] for k in range(5)])
            lo_s.append(lo)
            hi_s.append(hi)
            w.append(fourth(*[e[1, f, r + k] for k in range(5)]))
        balance = flux_pair(lo_s, hi_s, 0)
        weight = w
        lo_s, hi_s, w = [], [], []
        for f in range(fields):
            lo, hi = faces(*shifted_azi(e[0, f, r + 2], az_exp[0, r, f], az_exp[1, r, f]))
            lo_s.append(lo)
            hi_s.append(hi)
            w.append(fourth(*shifted_azi(e[1, f, r + 2], az_exp[0, r, fields + f], az_exp[1, r, fields + f])))
        part = flux_pair(lo_s, hi_s, 1)
        balance = [b + p for b, p in zip(balance, part)]
        weight = [a + b for a, b in zip(weight, w)]
        lo_s, hi_s, w = [], [], []
        for f in range(fields):
            cp, ca = 2 * f, 2 * (fields + f)
            lo, hi = faces(*shifted_ax(e[0, f, r + 2], xlo[:, cp:cp + 1], xlo[:, cp + 1:cp + 2],
                                       xhi[:, cp:cp + 1], xhi[:, cp + 1:cp + 2]))
            lo_s.append(lo)
            hi_s.append(hi)
            w.append(fourth(*shifted_ax(e[1, f, r + 2], xlo[:, ca:ca + 1], xlo[:, ca + 1:ca + 2],
                                        xhi[:, ca:ca + 1], xhi[:, ca + 1:ca + 2])))
        part = flux_pair(lo_s, hi_s, 2)
        balance = [b + p for b, p in zip(balance, part)]
        weight = [a + b for a, b in zip(weight, w)]
        total = weight[0] * balance[0]
        for f in range(1, fields):
            total = total + weight[f] * balance[f]
        value = jnp.abs(total)
        out_ref[r] = value
        return carry + value

    acc = lax.fori_loop(2, rows - 2, row_body, jnp.zeros((n_a, n_x), jnp.float32))
    for cond, c in recvs[:2]:
        when(cond, c.wait_recv)
    acc = lax.fori_loop(0, 2, row_body, acc)
    acc = lax.fori_loop(rows - 2, rows, row_body, acc)
    per_azi, per_ax = n_a // BLK, n_x // BLK
    width = per_azi * per_ax
    lane_l = lax.broadcasted_iota(jnp.int32, (n_x, width), 0)
    col_j = lax.broadcasted_iota(jnp.int32, (n_x, width), 1)
    means = None
    for ba in range(per_azi):
        half = jnp.sum(acc[ba * BLK:(ba + 1) * BLK], axis=0, keepdims=True)
        pick = jnp.where((col_j // per_ax == ba) & (lane_l // BLK == col_j % per_ax), 1.0, 0.0)
        part = jnp.dot(half, pick, precision=lax.Precision.HIGHEST, preferred_element_type=jnp.float32)
        means = part if means is None else means + part
    pay[0, 0] = means / float(rows * BLK * BLK)
    sends_g = gen_gather_kernel(sizes, groups, pay, g_out, glsem, gssem, grsem, with_barrier=False)

    for cond, c in sends:
        when(cond, c.wait_send)
    for c in sends_g:
        c.wait_send()


def stencil(primal, adjoint, groups=((2, 1), (0,))):
    fields, rows, n_a, n_x = primal.shape
    anywhere = pl.BlockSpec(memory_space=pltpu.HBM)
    sizes = tuple(lax.axis_size(a) for a in AXES)
    width = (n_a // BLK) * (n_x // BLK)
    links = sum(len(offs) for _, offs in stage_plan(sizes, groups))
    return pl.pallas_call(
        functools.partial(stencil_kernel, groups),
        out_shape=(jax.ShapeDtypeStruct((rows, n_a, n_x), jnp.float32), jax.ShapeDtypeStruct(sizes + (width,), jnp.float32)),
        in_specs=[anywhere, anywhere],
        out_specs=(pl.BlockSpec(memory_space=pltpu.VMEM), pl.BlockSpec(memory_space=pltpu.VMEM)),
        scratch_shapes=[
            pltpu.VMEM((2, fields, rows + 4, n_a, n_x), jnp.float32),
            pltpu.VMEM((2, 2 * fields * rows * 2, n_x), jnp.float32),
            pltpu.VMEM((2, 2 * fields * rows * 2, n_x), jnp.float32),
            pltpu.VMEM((2, rows, 2 * fields, 8, n_x), jnp.float32),
            pltpu.VMEM((2, -(-4 * fields // 8) * 8, rows * n_a), jnp.float32),
            pltpu.VMEM((2, 128, rows * n_a), jnp.float32),
            pltpu.VMEM((2, rows * n_a, 128), jnp.float32),
            pltpu.SemaphoreType.DMA((2,)),
            pltpu.SemaphoreType.DMA((6,)),
            pltpu.SemaphoreType.DMA((6,)),
            pltpu.VMEM((1, 1, 1, width), jnp.float32),
            pltpu.SemaphoreType.DMA(()),
            pltpu.SemaphoreType.DMA((links,)),
            pltpu.SemaphoreType.DMA((links,)),
        ],
        compiler_params=pltpu.CompilerParams(
            collective_id=2, has_side_effects=True, vmem_limit_bytes=67043328
        ),
    )(primal, adjoint)


def on_device(primal, adjoint, refine_flag, owner_map, migrate_weight, neighbor_list):
    indicator, gathered_means = stencil(primal, adjoint)
    rows_rad, rows_azi, rows_ax = indicator.shape
    per_rad = rows_rad // BLK
    per_azi = rows_azi // BLK
    per_ax = rows_ax // BLK
    all_means = gathered_means.reshape(-1)
    me_dev = (lax.axis_index("rad") * lax.axis_size("azi") + lax.axis_index("azi")) * lax.axis_size("ax") + lax.axis_index("ax")
    block_mean = lax.dynamic_slice_in_dim(all_means, me_dev * (per_rad * per_azi * per_ax), per_rad * per_azi * per_ax).reshape(per_rad, per_azi, per_ax)
    size_rad = lax.axis_size("rad")
    size_azi = lax.axis_size("azi")
    size_ax = lax.axis_size("ax")
    blocks_azi = per_azi * size_azi
    blocks_ax = per_ax * size_ax
    block_rad = neighbor_list // (blocks_azi * blocks_ax)
    block_azi = neighbor_list // blocks_ax % blocks_azi
    block_ax = neighbor_list % blocks_ax
    owner_dev = (
        block_rad // per_rad * size_azi + block_azi // per_azi
    ) * size_ax + block_ax // per_ax
    local_pos = (block_rad % per_rad * per_azi + block_azi % per_azi) * per_ax + block_ax % per_ax
    position = owner_dev * (per_rad * per_azi * per_ax) + local_pos
    beside_all = jnp.mean(jnp.take(all_means, position), axis=-1)
    smooth = 0.5 * block_mean + 0.5 * beside_all
    own_index = (
        lax.axis_index("rad") * size_azi + lax.axis_index("azi")
    ) * size_ax + lax.axis_index("ax")
    moved = (owner_map != own_index).astype(jnp.float32)
    block_cost = (
        smooth * (1.0 + 7.0 * refine_flag.astype(jnp.float32))
        + 0.25 * migrate_weight.astype(jnp.float32) * moved
    )
    width = block_cost.size
    payload = jnp.concatenate([block_cost.reshape(-1), owner_map.reshape(-1).astype(jnp.float32)])
    gathered = gather_all(payload, 1).reshape(-1, 2 * width)
    cost_all = gathered[:, :width]
    owner_all = gathered[:, width:]
    total = jnp.sum(jnp.where(owner_all == own_index.astype(jnp.float32), cost_all, 0.0))
    owner_load = (total / (per_rad * per_azi * per_ax)).reshape(1, 1, 1)
    return (indicator, block_cost, owner_load)


def solution(mesh):
    return jax.shard_map(
        on_device,
        mesh=mesh,
        in_specs=(
            P(None, "rad", "azi", "ax"),
            P(None, "rad", "azi", "ax"),
            P("rad", "azi", "ax"),
            P("rad", "azi", "ax"),
            P("rad", "azi", "ax"),
            P("rad", "azi", "ax", None),
        ),
        out_specs=(P("rad", "azi", "ax"), P("rad", "azi", "ax"), P("rad", "azi", "ax")),
        check_vma=False,
    )
```

```python
import functools
import itertools
import jax
import jax.numpy as jnp
from jax import lax
from jax.experimental import pallas as pl
from jax.experimental.pallas import tpu as pltpu
from jax.sharding import PartitionSpec as P

BLK = 16
AXES = ("rad", "azi", "ax")
MESH = pl.DeviceIdType.MESH


def stage_plan(sizes, groups):
    plan = []
    for axes in groups:
        offs = [o for o in itertools.product(*[range(sizes[i]) for i in axes]) if any(o)]
        plan.append((axes, offs))
    return plan


def gen_gather_kernel(sizes, groups, x_ref, o_ref, lsem, ssem, rsem, with_barrier=True):
    me = tuple(lax.axis_index(a) for a in AXES)
    plan = stage_plan(sizes, groups)

    def shift(off_axes, off, sign):
        dev = list(me)
        for i, o in zip(off_axes, off):
            dev[i] = lax.rem(me[i] + (o if sign > 0 else sizes[i] - o), sizes[i])
        return tuple(dev)

    if with_barrier:
        barrier = pltpu.get_barrier_semaphore()
        count = 0
        for axes, offs in plan:
            for off in offs:
                pl.semaphore_signal(barrier, 1, device_id=shift(axes, off, 1), device_id_type=MESH)
                count += 1
        pl.semaphore_wait(barrier, count)

    covered = set()

    def region(dev):
        idx = []
        for i in range(3):
            if i in covered:
                break
            idx.append(pl.ds(dev[i], 1))
        return o_ref.at[tuple(idx)] if idx else o_ref

    def region_full(dev):
        n_fixed = 3 - len(covered)
        return o_ref.at[tuple(pl.ds(dev[i], 1) for i in range(n_fixed))]

    local = pltpu.make_async_copy(x_ref, o_ref.at[tuple(pl.ds(m, 1) for m in me)], lsem)
    local.start()
    sends = []
    slot = 0
    for stage, (axes, offs) in enumerate(plan):
        src = x_ref if stage == 0 else region_full(me)
        first = slot
        for off in offs:
            c = pltpu.make_async_remote_copy(src_ref=src, dst_ref=region_full(me), send_sem=ssem.at[slot],
                                             recv_sem=rsem.at[slot], device_id=shift(axes, off, 1), device_id_type=MESH)
            c.start()
            sends.append(c)
            slot += 1
        slot = first
        for off in offs:
            frm = shift(axes, off, -1)
            c = pltpu.make_async_remote_copy(src_ref=src, dst_ref=region_full(frm), send_sem=ssem.at[slot],
                                             recv_sem=rsem.at[slot], device_id=frm, device_id_type=MESH)
            c.wait_recv()
            slot += 1
        if stage == 0:
            local.wait()
        covered.update(axes)
    return sends


def gather_kernel(sizes, groups, x_ref, o_ref, lsem, ssem, rsem):
    for c in gen_gather_kernel(sizes, groups, x_ref, o_ref, lsem, ssem, rsem):
        c.wait_send()


def load_kernel(sizes, groups, width, x_ref, load_out, o_ref, lsem, ssem, rsem):
    sends = gen_gather_kernel(sizes, groups, x_ref, o_ref, lsem, ssem, rsem)
    me = (lax.axis_index("rad") * sizes[1] + lax.axis_index("azi")) * sizes[2] + lax.axis_index("ax")
    values = o_ref[...]
    owners = pltpu.roll(values, values.shape[-1] - width, 3)
    lane = lax.broadcasted_iota(jnp.int32, values.shape, 3)
    picked = jnp.where((lane < width) & (owners == me.astype(jnp.float32)), values, 0.0)
    part = jnp.sum(picked, axis=(0, 1))
    total = jnp.sum(part, axis=0, keepdims=True)
    total = jnp.sum(total, axis=1, keepdims=True)
    load_out[...] = (total / float(width)).reshape(1, 1, 1)
    for c in sends:
        c.wait_send()


def load_gather(payload, width, groups=((2, 1), (0,))):
    sizes = tuple(lax.axis_size(a) for a in AXES)
    lanes = payload.shape[0]
    links = sum(len(offs) for _, offs in stage_plan(sizes, groups))
    return pl.pallas_call(
        functools.partial(load_kernel, sizes, groups, width),
        out_shape=jax.ShapeDtypeStruct((1, 1, 1), jnp.float32),
        in_specs=[pl.BlockSpec(memory_space=pltpu.VMEM)],
        out_specs=pl.BlockSpec(memory_space=pltpu.VMEM),
        scratch_shapes=[
            pltpu.VMEM(sizes + (lanes,), jnp.float32),
            pltpu.SemaphoreType.DMA(()),
            pltpu.SemaphoreType.DMA((links,)),
            pltpu.SemaphoreType.DMA((links,)),
        ],
        compiler_params=pltpu.CompilerParams(collective_id=1, has_side_effects=True),
    )(payload.reshape(1, 1, 1, lanes))


def gather_all(values, cid, groups=((2, 1), (0,))):
    sizes = tuple(lax.axis_size(a) for a in AXES)
    width = values.shape[0]
    links = sum(len(offs) for _, offs in stage_plan(sizes, groups))
    out = pl.pallas_call(
        functools.partial(gather_kernel, sizes, groups),
        out_shape=jax.ShapeDtypeStruct(sizes + (width,), jnp.float32),
        in_specs=[pl.BlockSpec(memory_space=pltpu.VMEM)],
        out_specs=pl.BlockSpec(memory_space=pltpu.VMEM),
        scratch_shapes=[pltpu.SemaphoreType.DMA(()), pltpu.SemaphoreType.DMA((links,)), pltpu.SemaphoreType.DMA((links,))],
        compiler_params=pltpu.CompilerParams(collective_id=cid, has_side_effects=True),
    )(values.reshape(1, 1, 1, width))
    return out.reshape(-1)


def dense(x):
    return x.reshape(-1, 128)


def exchange(tail, head, axis, periodic):
    count = lax.axis_size(axis)
    forward = [(i, i + 1) for i in range(count - 1)]
    if periodic:
        forward.append((count - 1, 0))
    backward = [(target, source) for source, target in forward]
    low = lax.ppermute(dense(tail), axis, forward).reshape(tail.shape)
    high = lax.ppermute(dense(head), axis, backward).reshape(head.shape)
    return low, high


def flux_pair(state_lo, state_hi, along):
    return [h - l for h, l in zip(euler_flux(state_hi, along), euler_flux(state_lo, along))]


def euler_flux(s, along):
    density, m0, m1, m2, energy = s
    momenta = (m0, m1, m2)
    inv = 1.0 / density
    velocity = momenta[along] * inv
    kinetic = 0.5 * (m0 * m0 + m1 * m1 + m2 * m2) * inv
    pressure = 0.4 * (energy - kinetic)
    columns = [momenta[along], m0 * velocity, m1 * velocity, m2 * velocity, (energy + pressure) * velocity]
    columns[1 + along] = columns[1 + along] + pressure
    return columns


def faces(um2, um1, u, up1, up2):
    lower = (7.0 * um1 - um2) / 12.0 + (7.0 * u - up1) / 12.0
    upper = (7.0 * u - um1) / 12.0 + (7.0 * up1 - up2) / 12.0
    return lower, upper


def fourth(zm2, zm1, z, zp1, zp2):
    return (zm2 - 4.0 * zm1 + 6.0 * z - 4.0 * zp1 + zp2) / 12.0


def stencil_kernel(groups, p_hbm, a_hbm, out_ref, g_out, e, az_send, az_recv, az_exp, x_send, x_recv, xt, sems, ssem, rsem,
                   pay, glsem, gssem, grsem):
    _, fields, ext_rows, n_a, n_x = e.shape
    rows = ext_rows - 4
    n_r_dev, n_a_dev, n_x_dev = (lax.axis_size(ax) for ax in AXES)
    me_r, me_a, me_x = (lax.axis_index(ax) for ax in AXES)
    has_r_lo, has_r_hi = me_r > 0, me_r < n_r_dev - 1
    has_x_lo, has_x_hi = me_x > 0, me_x < n_x_dev - 1
    r_lo, r_hi = (me_r - 1, me_a, me_x), (me_r + 1, me_a, me_x)
    a_lo = (me_r, lax.rem(me_a + n_a_dev - 1, n_a_dev), me_x)
    a_hi = (me_r, lax.rem(me_a + 1, n_a_dev), me_x)
    x_lo, x_hi = (me_r, me_a, me_x - 1), (me_r, me_a, me_x + 1)

    loads = [
        pltpu.make_async_copy(p_hbm, e.at[0, :, pl.ds(2, rows)], sems.at[0]),
        pltpu.make_async_copy(a_hbm, e.at[1, :, pl.ds(2, rows)], sems.at[1]),
    ]
    for c in loads:
        c.start()

    sizes = (n_r_dev, n_a_dev, n_x_dev)
    me = (me_r, me_a, me_x)
    barrier = pltpu.get_barrier_semaphore()
    n_peers = 0
    for axes, offs in stage_plan(sizes, groups):
        for off in offs:
            dev = list(me)
            for i, o in zip(axes, off):
                dev[i] = lax.rem(me[i] + o, sizes[i])
            pl.semaphore_signal(barrier, 1, device_id=tuple(dev), device_id_type=MESH)
            n_peers += 1
    pl.semaphore_wait(barrier, n_peers)

    x_recv[:, x_send.shape[1]:, :] = jnp.zeros((2, x_recv.shape[1] - x_send.shape[1], x_recv.shape[2]), jnp.float32)
    x_send[:, 4 * fields:, :] = jnp.zeros((2, x_send.shape[1] - 4 * fields, x_send.shape[2]), jnp.float32)
    for c in loads:
        c.wait()

    def remote(src, dst, i, dev):
        return pltpu.make_async_remote_copy(
            src_ref=src, dst_ref=dst, send_sem=ssem.at[i], recv_sem=rsem.at[i],
            device_id=dev, device_id_type=MESH,
        )

    n_kx = x_send.shape[1]
    sends = [
        (has_r_hi, remote(e.at[:, :, pl.ds(rows, 2)], e.at[:, :, pl.ds(0, 2)], 0, r_hi)),
        (has_r_lo, remote(e.at[:, :, pl.ds(2, 2)], e.at[:, :, pl.ds(rows + 2, 2)], 1, r_lo)),
        (None, remote(az_send.at[1], az_recv.at[0], 2, a_hi)),
        (None, remote(az_send.at[0], az_recv.at[1], 3, a_lo)),
        (has_x_hi, remote(x_send.at[1], x_recv.at[0, pl.ds(0, n_kx)], 4, x_hi)),
        (has_x_lo, remote(x_send.at[0], x_recv.at[1, pl.ds(0, n_kx)], 5, x_lo)),
    ]
    recvs = [
        (has_r_lo, remote(e.at[:, :, pl.ds(rows, 2)], e.at[:, :, pl.ds(0, 2)], 0, r_lo)),
        (has_r_hi, remote(e.at[:, :, pl.ds(2, 2)], e.at[:, :, pl.ds(rows + 2, 2)], 1, r_hi)),
        (None, remote(az_send.at[1], az_recv.at[0], 2, a_lo)),
        (None, remote(az_send.at[0], az_recv.at[1], 3, a_hi)),
        (has_x_lo, remote(x_send.at[1], x_recv.at[0, pl.ds(0, n_kx)], 4, x_lo)),
        (has_x_hi, remote(x_send.at[0], x_recv.at[1, pl.ds(0, n_kx)], 5, x_hi)),
    ]

    def when(cond, fn):
        if cond is None:
            fn()
        else:
            pl.when(cond)(fn)

    for cond, c in sends[:2]:
        when(cond, c.start)

    for k in range(2):
        for f in range(fields):
            for r in range(rows):
                row = ((k * fields + f) * rows + r) * 2
                az_send[0, row:row + 2, :] = e[k, f, 2 + r, 0:2, :]
                az_send[1, row:row + 2, :] = e[k, f, 2 + r, n_a - 2:n_a, :]
            plane = e[k, f, 2:2 + rows].reshape(rows * n_a, n_x)
            cols = plane.T
            row = (k * fields + f) * 2
            x_send[0, row:row + 2, :] = cols[0:2]
            x_send[1, row:row + 2, :] = cols[n_x - 2:n_x]

    for cond, c in sends[2:]:
        when(cond, c.start)

    @pl.when(jnp.logical_not(has_r_lo))
    def _():
        e[:, :, 0:2] = jnp.zeros((2, fields, 2, n_a, n_x), jnp.float32)

    @pl.when(jnp.logical_not(has_r_hi))
    def _():
        e[:, :, rows + 2:rows + 4] = jnp.zeros((2, fields, 2, n_a, n_x), jnp.float32)

    @pl.when(jnp.logical_not(has_x_lo))
    def _():
        x_recv[0, 0:n_kx, :] = jnp.zeros((n_kx, x_recv.shape[2]), jnp.float32)

    @pl.when(jnp.logical_not(has_x_hi))
    def _():
        x_recv[1, 0:n_kx, :] = jnp.zeros((n_kx, x_recv.shape[2]), jnp.float32)

    for cond, c in recvs[2:]:
        when(cond, c.wait_recv)

    for side in range(2):
        xt[side] = x_recv[side].T
        for k in range(2):
            for f in range(fields):
                for r in range(rows):
                    row = ((k * fields + f) * rows + r) * 2
                    az_exp[side, r, k * fields + f, 0:2, :] = az_recv[side, row:row + 2, :]

    sub = lax.broadcasted_iota(jnp.int32, (n_a, n_x), 0)
    lane = lax.broadcasted_iota(jnp.int32, (n_a, n_x), 1)

    def shifted_azi(u, lo, hi):
        um1 = jnp.where(sub == 0, jnp.broadcast_to(lo[1:2], u.shape), pltpu.roll(u, 1, 0))
        um2 = jnp.where(sub == 0, jnp.broadcast_to(lo[0:1], u.shape),
                        jnp.where(sub == 1, jnp.broadcast_to(lo[1:2], u.shape), pltpu.roll(u, 2, 0)))
        up1 = jnp.where(sub == n_a - 1, jnp.broadcast_to(hi[0:1], u.shape), pltpu.roll(u, n_a - 1, 0))
        up2 = jnp.where(sub == n_a - 1, jnp.broadcast_to(hi[1:2], u.shape),
                        jnp.where(sub == n_a - 2, jnp.broadcast_to(hi[0:1], u.shape), pltpu.roll(u, n_a - 2, 0)))
        return um2, um1, u, up1, up2

    def shifted_ax(u, lo0, lo1, hi0, hi1):
        um1 = jnp.where(lane == 0, jnp.broadcast_to(lo1, u.shape), pltpu.roll(u, 1, 1))
        um2 = jnp.where(lane == 0, jnp.broadcast_to(lo0, u.shape),
                        jnp.where(lane == 1, jnp.broadcast_to(lo1, u.shape), pltpu.roll(u, 2, 1)))
        up1 = jnp.where(lane == n_x - 1, jnp.broadcast_to(hi0, u.shape), pltpu.roll(u, n_x - 1, 1))
        up2 = jnp.where(lane == n_x - 1, jnp.broadcast_to(hi1, u.shape),
                        jnp.where(lane == n_x - 2, jnp.broadcast_to(hi0, u.shape), pltpu.roll(u, n_x - 2, 1)))
        return um2, um1, u, up1, up2

    def row_body(r, carry):
        base = pl.multiple_of(r * n_a, n_a)
        xlo = xt[0, pl.ds(base, n_a), :]
        xhi = xt[1, pl.ds(base, n_a), :]
        lo_s, hi_s, w = [], [], []
        for f in range(fields):
            lo, hi = faces(*[e[0, f, r + k] for k in range(5)])
            lo_s.append(lo)
            hi_s.append(hi)
            w.append(fourth(*[e[1, f, r + k] for k in range(5)]))
        balance = flux_pair(lo_s, hi_s, 0)
        weight = w
        lo_s, hi_s, w = [], [], []
        for f in range(fields):
            lo, hi = faces(*shifted_azi(e[0, f, r + 2], az_exp[0, r, f], az_exp[1, r, f]))
            lo_s.append(lo)
            hi_s.append(hi)
            w.append(fourth(*shifted_azi(e[1, f, r + 2], az_exp[0, r, fields + f], az_exp[1, r, fields + f])))
        part = flux_pair(lo_s, hi_s, 1)
        balance = [b + p for b, p in zip(balance, part)]
        weight = [a + b for a, b in zip(weight, w)]
        lo_s, hi_s, w = [], [], []
        for f in range(fields):
            cp, ca = 2 * f, 2 * (fields + f)
            lo, hi = faces(*shifted_ax(e[0, f, r + 2], xlo[:, cp:cp + 1], xlo[:, cp + 1:cp + 2],
                                       xhi[:, cp:cp + 1], xhi[:, cp + 1:cp + 2]))
            lo_s.append(lo)
            hi_s.append(hi)
            w.append(fourth(*shifted_ax(e[1, f, r + 2], xlo[:, ca:ca + 1], xlo[:, ca + 1:ca + 2],
                                        xhi[:, ca:ca + 1], xhi[:, ca + 1:ca + 2])))
        part = flux_pair(lo_s, hi_s, 2)
        balance = [b + p for b, p in zip(balance, part)]
        weight = [a + b for a, b in zip(weight, w)]
        total = weight[0] * balance[0]
        for f in range(1, fields):
            total = total + weight[f] * balance[f]
        value = jnp.abs(total)
        out_ref[r] = value
        return carry + value

    acc = lax.fori_loop(2, rows - 2, row_body, jnp.zeros((n_a, n_x), jnp.float32))
    for cond, c in recvs[:2]:
        when(cond, c.wait_recv)
    acc = lax.fori_loop(0, 2, row_body, acc)
    acc = lax.fori_loop(rows - 2, rows, row_body, acc)
    per_azi, per_ax = n_a // BLK, n_x // BLK
    width = per_azi * per_ax
    lane_l = lax.broadcasted_iota(jnp.int32, (n_x, width), 0)
    col_j = lax.broadcasted_iota(jnp.int32, (n_x, width), 1)
    means = None
    for ba in range(per_azi):
        half = jnp.sum(acc[ba * BLK:(ba + 1) * BLK], axis=0, keepdims=True)
        pick = jnp.where((col_j // per_ax == ba) & (lane_l // BLK == col_j % per_ax), 1.0, 0.0)
        part = jnp.dot(half, pick, precision=lax.Precision.HIGHEST, preferred_element_type=jnp.float32)
        means = part if means is None else means + part
    pay[0, 0] = means / float(rows * BLK * BLK)
    sends_g = gen_gather_kernel(sizes, groups, pay, g_out, glsem, gssem, grsem, with_barrier=False)

    for cond, c in sends:
        when(cond, c.wait_send)
    for c in sends_g:
        c.wait_send()


def stencil(primal, adjoint, groups=((2, 1), (0,))):
    fields, rows, n_a, n_x = primal.shape
    anywhere = pl.BlockSpec(memory_space=pltpu.HBM)
    sizes = tuple(lax.axis_size(a) for a in AXES)
    width = (n_a // BLK) * (n_x // BLK)
    links = sum(len(offs) for _, offs in stage_plan(sizes, groups))
    return pl.pallas_call(
        functools.partial(stencil_kernel, groups),
        out_shape=(jax.ShapeDtypeStruct((rows, n_a, n_x), jnp.float32), jax.ShapeDtypeStruct(sizes + (width,), jnp.float32)),
        in_specs=[anywhere, anywhere],
        out_specs=(pl.BlockSpec(memory_space=pltpu.VMEM), pl.BlockSpec(memory_space=pltpu.VMEM)),
        scratch_shapes=[
            pltpu.VMEM((2, fields, rows + 4, n_a, n_x), jnp.float32),
            pltpu.VMEM((2, 2 * fields * rows * 2, n_x), jnp.float32),
            pltpu.VMEM((2, 2 * fields * rows * 2, n_x), jnp.float32),
            pltpu.VMEM((2, rows, 2 * fields, 8, n_x), jnp.float32),
            pltpu.VMEM((2, -(-4 * fields // 8) * 8, rows * n_a), jnp.float32),
            pltpu.VMEM((2, 128, rows * n_a), jnp.float32),
            pltpu.VMEM((2, rows * n_a, 128), jnp.float32),
            pltpu.SemaphoreType.DMA((2,)),
            pltpu.SemaphoreType.DMA((6,)),
            pltpu.SemaphoreType.DMA((6,)),
            pltpu.VMEM((1, 1, 1, width), jnp.float32),
            pltpu.SemaphoreType.DMA(()),
            pltpu.SemaphoreType.DMA((links,)),
            pltpu.SemaphoreType.DMA((links,)),
        ],
        compiler_params=pltpu.CompilerParams(
            collective_id=2, has_side_effects=True, vmem_limit_bytes=67043328
        ),
    )(primal, adjoint)


def on_device(primal, adjoint, refine_flag, owner_map, migrate_weight, neighbor_list):
    indicator, gathered_means = stencil(primal, adjoint)
    rows_rad, rows_azi, rows_ax = indicator.shape
    per_rad = rows_rad // BLK
    per_azi = rows_azi // BLK
    per_ax = rows_ax // BLK
    block_mean = lax.dynamic_slice(
        gathered_means, (lax.axis_index("rad"), lax.axis_index("azi"), lax.axis_index("ax"), 0),
        (1, 1, 1, gathered_means.shape[3]),
    ).reshape(per_rad, per_azi, per_ax)
    size_rad = lax.axis_size("rad")
    size_azi = lax.axis_size("azi")
    size_ax = lax.axis_size("ax")
    blocks_azi = per_azi * size_azi
    blocks_ax = per_ax * size_ax
    block_rad = neighbor_list // (blocks_azi * blocks_ax)
    block_azi = neighbor_list // blocks_ax % blocks_azi
    block_ax = neighbor_list % blocks_ax
    owner_dev = (
        block_rad // per_rad * size_azi + block_azi // per_azi
    ) * size_ax + block_ax // per_ax
    local_pos = (block_rad % per_rad * per_azi + block_azi % per_azi) * per_ax + block_ax % per_ax
    dev_rad = owner_dev // (size_azi * size_ax)
    dev_azi = owner_dev // size_ax % size_azi
    dev_ax = owner_dev % size_ax
    beside_all = jnp.mean(gathered_means[dev_rad, dev_azi, dev_ax, local_pos], axis=-1)
    smooth = 0.5 * block_mean + 0.5 * beside_all
    own_index = (
        lax.axis_index("rad") * size_azi + lax.axis_index("azi")
    ) * size_ax + lax.axis_index("ax")
    moved = (owner_map != own_index).astype(jnp.float32)
    block_cost = (
        smooth * (1.0 + 7.0 * refine_flag.astype(jnp.float32))
        + 0.25 * migrate_weight.astype(jnp.float32) * moved
    )
    width = block_cost.size
    payload = jnp.concatenate([
        block_cost.reshape(-1), owner_map.reshape(-1).astype(jnp.float32),
        jnp.zeros((128 - 2 * width,), jnp.float32),
    ])
    owner_load = load_gather(payload, width)
    return (indicator, block_cost, owner_load)


def solution(mesh):
    return jax.shard_map(
        on_device,
        mesh=mesh,
        in_specs=(
            P(None, "rad", "azi", "ax"),
            P(None, "rad", "azi", "ax"),
            P("rad", "azi", "ax"),
            P("rad", "azi", "ax"),
            P("rad", "azi", "ax"),
            P("rad", "azi", "ax", None),
        ),
        out_specs=(P("rad", "azi", "ax"), P("rad", "azi", "ax"), P("rad", "azi", "ax")),
        check_vma=False,
    )
```

```python
import functools
import itertools
import jax
import jax.numpy as jnp
from jax import lax
from jax.experimental import pallas as pl
from jax.experimental.pallas import tpu as pltpu
from jax.sharding import PartitionSpec as P

BLK = 16
AXES = ("rad", "azi", "ax")
MESH = pl.DeviceIdType.MESH


def stage_plan(sizes, groups):
    plan = []
    for axes in groups:
        offs = [o for o in itertools.product(*[range(sizes[i]) for i in axes]) if any(o)]
        plan.append((axes, offs))
    return plan


def gen_gather_kernel(sizes, groups, x_ref, o_ref, lsem, ssem, rsem, with_barrier=True):
    me = tuple(lax.axis_index(a) for a in AXES)
    plan = stage_plan(sizes, groups)

    def shift(off_axes, off, sign):
        dev = list(me)
        for i, o in zip(off_axes, off):
            dev[i] = lax.rem(me[i] + (o if sign > 0 else sizes[i] - o), sizes[i])
        return tuple(dev)

    if with_barrier:
        barrier = pltpu.get_barrier_semaphore()
        count = 0
        for axes, offs in plan:
            for off in offs:
                pl.semaphore_signal(barrier, 1, device_id=shift(axes, off, 1), device_id_type=MESH)
                count += 1
        pl.semaphore_wait(barrier, count)

    covered = set()

    def region(dev):
        idx = []
        for i in range(3):
            if i in covered:
                break
            idx.append(pl.ds(dev[i], 1))
        return o_ref.at[tuple(idx)] if idx else o_ref

    def region_full(dev):
        n_fixed = 3 - len(covered)
        return o_ref.at[tuple(pl.ds(dev[i], 1) for i in range(n_fixed))]

    local = pltpu.make_async_copy(x_ref, o_ref.at[tuple(pl.ds(m, 1) for m in me)], lsem)
    local.start()
    sends = []
    slot = 0
    for stage, (axes, offs) in enumerate(plan):
        src = x_ref if stage == 0 else region_full(me)
        first = slot
        for off in offs:
            c = pltpu.make_async_remote_copy(src_ref=src, dst_ref=region_full(me), send_sem=ssem.at[slot],
                                             recv_sem=rsem.at[slot], device_id=shift(axes, off, 1), device_id_type=MESH)
            c.start()
            sends.append(c)
            slot += 1
        slot = first
        for off in offs:
            frm = shift(axes, off, -1)
            c = pltpu.make_async_remote_copy(src_ref=src, dst_ref=region_full(frm), send_sem=ssem.at[slot],
                                             recv_sem=rsem.at[slot], device_id=frm, device_id_type=MESH)
            c.wait_recv()
            slot += 1
        if stage == 0:
            local.wait()
        covered.update(axes)
    return sends


def gather_kernel(sizes, groups, x_ref, o_ref, lsem, ssem, rsem):
    for c in gen_gather_kernel(sizes, groups, x_ref, o_ref, lsem, ssem, rsem):
        c.wait_send()


def load_kernel(sizes, groups, width, x_ref, load_out, o_ref, lsem, ssem, rsem):
    sends = gen_gather_kernel(sizes, groups, x_ref, o_ref, lsem, ssem, rsem)
    me = (lax.axis_index("rad") * sizes[1] + lax.axis_index("azi")) * sizes[2] + lax.axis_index("ax")
    values = o_ref[...]
    owners = pltpu.roll(values, values.shape[-1] - width, 3)
    lane = lax.broadcasted_iota(jnp.int32, values.shape, 3)
    picked = jnp.where((lane < width) & (owners == me.astype(jnp.float32)), values, 0.0)
    part = jnp.sum(picked, axis=(0, 1))
    total = jnp.sum(part, axis=0, keepdims=True)
    total = jnp.sum(total, axis=1, keepdims=True)
    load_out[...] = (total / float(width)).reshape(1, 1, 1)
    for c in sends:
        c.wait_send()


def load_gather(payload, width, groups=((2, 1), (0,))):
    sizes = tuple(lax.axis_size(a) for a in AXES)
    lanes = payload.shape[0]
    links = sum(len(offs) for _, offs in stage_plan(sizes, groups))
    return pl.pallas_call(
        functools.partial(load_kernel, sizes, groups, width),
        out_shape=jax.ShapeDtypeStruct((1, 1, 1), jnp.float32),
        in_specs=[pl.BlockSpec(memory_space=pltpu.VMEM)],
        out_specs=pl.BlockSpec(memory_space=pltpu.VMEM),
        scratch_shapes=[
            pltpu.VMEM(sizes + (lanes,), jnp.float32),
            pltpu.SemaphoreType.DMA(()),
            pltpu.SemaphoreType.DMA((links,)),
            pltpu.SemaphoreType.DMA((links,)),
        ],
        compiler_params=pltpu.CompilerParams(collective_id=1, has_side_effects=True),
    )(payload.reshape(1, 1, 1, lanes))


def gather_all(values, cid, groups=((2, 1), (0,))):
    sizes = tuple(lax.axis_size(a) for a in AXES)
    width = values.shape[0]
    links = sum(len(offs) for _, offs in stage_plan(sizes, groups))
    out = pl.pallas_call(
        functools.partial(gather_kernel, sizes, groups),
        out_shape=jax.ShapeDtypeStruct(sizes + (width,), jnp.float32),
        in_specs=[pl.BlockSpec(memory_space=pltpu.VMEM)],
        out_specs=pl.BlockSpec(memory_space=pltpu.VMEM),
        scratch_shapes=[pltpu.SemaphoreType.DMA(()), pltpu.SemaphoreType.DMA((links,)), pltpu.SemaphoreType.DMA((links,))],
        compiler_params=pltpu.CompilerParams(collective_id=cid, has_side_effects=True),
    )(values.reshape(1, 1, 1, width))
    return out.reshape(-1)


def dense(x):
    return x.reshape(-1, 128)


def exchange(tail, head, axis, periodic):
    count = lax.axis_size(axis)
    forward = [(i, i + 1) for i in range(count - 1)]
    if periodic:
        forward.append((count - 1, 0))
    backward = [(target, source) for source, target in forward]
    low = lax.ppermute(dense(tail), axis, forward).reshape(tail.shape)
    high = lax.ppermute(dense(head), axis, backward).reshape(head.shape)
    return low, high


def flux_pair(state_lo, state_hi, along):
    return [h - l for h, l in zip(euler_flux(state_hi, along), euler_flux(state_lo, along))]


def euler_flux(s, along):
    density, m0, m1, m2, energy = s
    momenta = (m0, m1, m2)
    inv = 1.0 / density
    velocity = momenta[along] * inv
    kinetic = 0.5 * (m0 * m0 + m1 * m1 + m2 * m2) * inv
    pressure = 0.4 * (energy - kinetic)
    columns = [momenta[along], m0 * velocity, m1 * velocity, m2 * velocity, (energy + pressure) * velocity]
    columns[1 + along] = columns[1 + along] + pressure
    return columns


def faces(um2, um1, u, up1, up2):
    lower = (7.0 * um1 - um2) / 12.0 + (7.0 * u - up1) / 12.0
    upper = (7.0 * u - um1) / 12.0 + (7.0 * up1 - up2) / 12.0
    return lower, upper


def fourth(zm2, zm1, z, zp1, zp2):
    return (zm2 - 4.0 * zm1 + 6.0 * z - 4.0 * zp1 + zp2) / 12.0


def stencil_kernel(groups, p_hbm, a_hbm, out_ref, g_out, e, az_send, az_recv, az_exp, x_send, x_recv, xt, sems, ssem, rsem,
                   pay, glsem, gssem, grsem):
    _, fields, ext_rows, n_a, n_x = e.shape
    rows = ext_rows - 4
    n_r_dev, n_a_dev, n_x_dev = (lax.axis_size(ax) for ax in AXES)
    me_r, me_a, me_x = (lax.axis_index(ax) for ax in AXES)
    has_r_lo, has_r_hi = me_r > 0, me_r < n_r_dev - 1
    has_x_lo, has_x_hi = me_x > 0, me_x < n_x_dev - 1
    r_lo, r_hi = (me_r - 1, me_a, me_x), (me_r + 1, me_a, me_x)
    a_lo = (me_r, lax.rem(me_a + n_a_dev - 1, n_a_dev), me_x)
    a_hi = (me_r, lax.rem(me_a + 1, n_a_dev), me_x)
    x_lo, x_hi = (me_r, me_a, me_x - 1), (me_r, me_a, me_x + 1)

    loads = [
        pltpu.make_async_copy(p_hbm, e.at[0, :, pl.ds(2, rows)], sems.at[0]),
        pltpu.make_async_copy(a_hbm, e.at[1, :, pl.ds(2, rows)], sems.at[1]),
    ]
    for c in loads:
        c.start()

    sizes = (n_r_dev, n_a_dev, n_x_dev)
    me = (me_r, me_a, me_x)
    barrier = pltpu.get_barrier_semaphore()
    n_peers = 0
    for axes, offs in stage_plan(sizes, groups):
        for off in offs:
            dev = list(me)
            for i, o in zip(axes, off):
                dev[i] = lax.rem(me[i] + o, sizes[i])
            pl.semaphore_signal(barrier, 1, device_id=tuple(dev), device_id_type=MESH)
            n_peers += 1

    x_recv[:, x_send.shape[1]:, :] = jnp.zeros((2, x_recv.shape[1] - x_send.shape[1], x_recv.shape[2]), jnp.float32)
    x_send[:, 4 * fields:, :] = jnp.zeros((2, x_send.shape[1] - 4 * fields, x_send.shape[2]), jnp.float32)
    for c in loads:
        c.wait()

    def remote(src, dst, i, dev):
        return pltpu.make_async_remote_copy(
            src_ref=src, dst_ref=dst, send_sem=ssem.at[i], recv_sem=rsem.at[i],
            device_id=dev, device_id_type=MESH,
        )

    n_kx = x_send.shape[1]
    sends = [
        (has_r_hi, remote(e.at[:, :, pl.ds(rows, 2)], e.at[:, :, pl.ds(0, 2)], 0, r_hi)),
        (has_r_lo, remote(e.at[:, :, pl.ds(2, 2)], e.at[:, :, pl.ds(rows + 2, 2)], 1, r_lo)),
        (None, remote(az_send.at[1], az_recv.at[0], 2, a_hi)),
        (None, remote(az_send.at[0], az_recv.at[1], 3, a_lo)),
        (has_x_hi, remote(x_send.at[1], x_recv.at[0, pl.ds(0, n_kx)], 4, x_hi)),
        (has_x_lo, remote(x_send.at[0], x_recv.at[1, pl.ds(0, n_kx)], 5, x_lo)),
    ]
    recvs = [
        (has_r_lo, remote(e.at[:, :, pl.ds(rows, 2)], e.at[:, :, pl.ds(0, 2)], 0, r_lo)),
        (has_r_hi, remote(e.at[:, :, pl.ds(2, 2)], e.at[:, :, pl.ds(rows + 2, 2)], 1, r_hi)),
        (None, remote(az_send.at[1], az_recv.at[0], 2, a_lo)),
        (None, remote(az_send.at[0], az_recv.at[1], 3, a_hi)),
        (has_x_lo, remote(x_send.at[1], x_recv.at[0, pl.ds(0, n_kx)], 4, x_lo)),
        (has_x_hi, remote(x_send.at[0], x_recv.at[1, pl.ds(0, n_kx)], 5, x_hi)),
    ]

    def when(cond, fn):
        if cond is None:
            fn()
        else:
            pl.when(cond)(fn)

    for k in range(2):
        for f in range(fields):
            for r in range(rows):
                row = ((k * fields + f) * rows + r) * 2
                az_send[0, row:row + 2, :] = e[k, f, 2 + r, 0:2, :]
                az_send[1, row:row + 2, :] = e[k, f, 2 + r, n_a - 2:n_a, :]
            plane = e[k, f, 2:2 + rows].reshape(rows * n_a, n_x)
            cols = plane.T
            row = (k * fields + f) * 2
            x_send[0, row:row + 2, :] = cols[0:2]
            x_send[1, row:row + 2, :] = cols[n_x - 2:n_x]

    pl.semaphore_wait(barrier, n_peers)
    for cond, c in sends:
        when(cond, c.start)

    @pl.when(jnp.logical_not(has_r_lo))
    def _():
        e[:, :, 0:2] = jnp.zeros((2, fields, 2, n_a, n_x), jnp.float32)

    @pl.when(jnp.logical_not(has_r_hi))
    def _():
        e[:, :, rows + 2:rows + 4] = jnp.zeros((2, fields, 2, n_a, n_x), jnp.float32)

    @pl.when(jnp.logical_not(has_x_lo))
    def _():
        x_recv[0, 0:n_kx, :] = jnp.zeros((n_kx, x_recv.shape[2]), jnp.float32)

    @pl.when(jnp.logical_not(has_x_hi))
    def _():
        x_recv[1, 0:n_kx, :] = jnp.zeros((n_kx, x_recv.shape[2]), jnp.float32)

    for cond, c in recvs[2:]:
        when(cond, c.wait_recv)

    for side in range(2):
        xt[side] = x_recv[side].T
        for k in range(2):
            for f in range(fields):
                for r in range(rows):
                    row = ((k * fields + f) * rows + r) * 2
                    az_exp[side, r, k * fields + f, 0:2, :] = az_recv[side, row:row + 2, :]

    sub = lax.broadcasted_iota(jnp.int32, (n_a, n_x), 0)
    lane = lax.broadcasted_iota(jnp.int32, (n_a, n_x), 1)

    def shifted_azi(u, lo, hi):
        um1 = jnp.where(sub == 0, jnp.broadcast_to(lo[1:2], u.shape), pltpu.roll(u, 1, 0))
        um2 = jnp.where(sub == 0, jnp.broadcast_to(lo[0:1], u.shape),
                        jnp.where(sub == 1, jnp.broadcast_to(lo[1:2], u.shape), pltpu.roll(u, 2, 0)))
        up1 = jnp.where(sub == n_a - 1, jnp.broadcast_to(hi[0:1], u.shape), pltpu.roll(u, n_a - 1, 0))
        up2 = jnp.where(sub == n_a - 1, jnp.broadcast_to(hi[1:2], u.shape),
                        jnp.where(sub == n_a - 2, jnp.broadcast_to(hi[0:1], u.shape), pltpu.roll(u, n_a - 2, 0)))
        return um2, um1, u, up1, up2

    def shifted_ax(u, lo0, lo1, hi0, hi1):
        um1 = jnp.where(lane == 0, jnp.broadcast_to(lo1, u.shape), pltpu.roll(u, 1, 1))
        um2 = jnp.where(lane == 0, jnp.broadcast_to(lo0, u.shape),
                        jnp.where(lane == 1, jnp.broadcast_to(lo1, u.shape), pltpu.roll(u, 2, 1)))
        up1 = jnp.where(lane == n_x - 1, jnp.broadcast_to(hi0, u.shape), pltpu.roll(u, n_x - 1, 1))
        up2 = jnp.where(lane == n_x - 1, jnp.broadcast_to(hi1, u.shape),
                        jnp.where(lane == n_x - 2, jnp.broadcast_to(hi0, u.shape), pltpu.roll(u, n_x - 2, 1)))
        return um2, um1, u, up1, up2

    def row_body(r, carry):
        base = pl.multiple_of(r * n_a, n_a)
        xlo = xt[0, pl.ds(base, n_a), :]
        xhi = xt[1, pl.ds(base, n_a), :]
        lo_s, hi_s, w = [], [], []
        for f in range(fields):
            lo, hi = faces(*[e[0, f, r + k] for k in range(5)])
            lo_s.append(lo)
            hi_s.append(hi)
            w.append(fourth(*[e[1, f, r + k] for k in range(5)]))
        balance = flux_pair(lo_s, hi_s, 0)
        weight = w
        lo_s, hi_s, w = [], [], []
        for f in range(fields):
            lo, hi = faces(*shifted_azi(e[0, f, r + 2], az_exp[0, r, f], az_exp[1, r, f]))
            lo_s.append(lo)
            hi_s.append(hi)
            w.append(fourth(*shifted_azi(e[1, f, r + 2], az_exp[0, r, fields + f], az_exp[1, r, fields + f])))
        part = flux_pair(lo_s, hi_s, 1)
        balance = [b + p for b, p in zip(balance, part)]
        weight = [a + b for a, b in zip(weight, w)]
        lo_s, hi_s, w = [], [], []
        for f in range(fields):
            cp, ca = 2 * f, 2 * (fields + f)
            lo, hi = faces(*shifted_ax(e[0, f, r + 2], xlo[:, cp:cp + 1], xlo[:, cp + 1:cp + 2],
                                       xhi[:, cp:cp + 1], xhi[:, cp + 1:cp + 2]))
            lo_s.append(lo)
            hi_s.append(hi)
            w.append(fourth(*shifted_ax(e[1, f, r + 2], xlo[:, ca:ca + 1], xlo[:, ca + 1:ca + 2],
                                        xhi[:, ca:ca + 1], xhi[:, ca + 1:ca + 2])))
        part = flux_pair(lo_s, hi_s, 2)
        balance = [b + p for b, p in zip(balance, part)]
        weight = [a + b for a, b in zip(weight, w)]
        total = weight[0] * balance[0]
        for f in range(1, fields):
            total = total + weight[f] * balance[f]
        value = jnp.abs(total)
        out_ref[r] = value
        return carry + value

    acc = lax.fori_loop(2, rows - 2, row_body, jnp.zeros((n_a, n_x), jnp.float32))
    for cond, c in recvs[:2]:
        when(cond, c.wait_recv)
    acc = lax.fori_loop(0, 2, row_body, acc)
    acc = lax.fori_loop(rows - 2, rows, row_body, acc)
    per_azi, per_ax = n_a // BLK, n_x // BLK
    width = per_azi * per_ax
    lane_l = lax.broadcasted_iota(jnp.int32, (n_x, width), 0)
    col_j = lax.broadcasted_iota(jnp.int32, (n_x, width), 1)
    means = None
    for ba in range(per_azi):
        half = jnp.sum(acc[ba * BLK:(ba + 1) * BLK], axis=0, keepdims=True)
        pick = jnp.where((col_j // per_ax == ba) & (lane_l // BLK == col_j % per_ax), 1.0, 0.0)
        part = jnp.dot(half, pick, precision=lax.Precision.HIGHEST, preferred_element_type=jnp.float32)
        means = part if means is None else means + part
    pay[0, 0] = means / float(rows * BLK * BLK)
    sends_g = gen_gather_kernel(sizes, groups, pay, g_out, glsem, gssem, grsem, with_barrier=False)

    for cond, c in sends:
        when(cond, c.wait_send)
    for c in sends_g:
        c.wait_send()


def stencil(primal, adjoint, groups=((2, 1), (0,))):
    fields, rows, n_a, n_x = primal.shape
    anywhere = pl.BlockSpec(memory_space=pltpu.HBM)
    sizes = tuple(lax.axis_size(a) for a in AXES)
    width = (n_a // BLK) * (n_x // BLK)
    links = sum(len(offs) for _, offs in stage_plan(sizes, groups))
    return pl.pallas_call(
        functools.partial(stencil_kernel, groups),
        out_shape=(jax.ShapeDtypeStruct((rows, n_a, n_x), jnp.float32), jax.ShapeDtypeStruct(sizes + (width,), jnp.float32)),
        in_specs=[anywhere, anywhere],
        out_specs=(pl.BlockSpec(memory_space=pltpu.VMEM), pl.BlockSpec(memory_space=pltpu.VMEM)),
        scratch_shapes=[
            pltpu.VMEM((2, fields, rows + 4, n_a, n_x), jnp.float32),
            pltpu.VMEM((2, 2 * fields * rows * 2, n_x), jnp.float32),
            pltpu.VMEM((2, 2 * fields * rows * 2, n_x), jnp.float32),
            pltpu.VMEM((2, rows, 2 * fields, 8, n_x), jnp.float32),
            pltpu.VMEM((2, -(-4 * fields // 8) * 8, rows * n_a), jnp.float32),
            pltpu.VMEM((2, 128, rows * n_a), jnp.float32),
            pltpu.VMEM((2, rows * n_a, 128), jnp.float32),
            pltpu.SemaphoreType.DMA((2,)),
            pltpu.SemaphoreType.DMA((6,)),
            pltpu.SemaphoreType.DMA((6,)),
            pltpu.VMEM((1, 1, 1, width), jnp.float32),
            pltpu.SemaphoreType.DMA(()),
            pltpu.SemaphoreType.DMA((links,)),
            pltpu.SemaphoreType.DMA((links,)),
        ],
        compiler_params=pltpu.CompilerParams(
            collective_id=2, has_side_effects=True, vmem_limit_bytes=67043328
        ),
    )(primal, adjoint)


def on_device(primal, adjoint, refine_flag, owner_map, migrate_weight, neighbor_list):
    indicator, gathered_means = stencil(primal, adjoint)
    rows_rad, rows_azi, rows_ax = indicator.shape
    per_rad = rows_rad // BLK
    per_azi = rows_azi // BLK
    per_ax = rows_ax // BLK
    block_mean = lax.dynamic_slice(
        gathered_means, (lax.axis_index("rad"), lax.axis_index("azi"), lax.axis_index("ax"), 0),
        (1, 1, 1, gathered_means.shape[3]),
    ).reshape(per_rad, per_azi, per_ax)
    size_rad = lax.axis_size("rad")
    size_azi = lax.axis_size("azi")
    size_ax = lax.axis_size("ax")
    blocks_azi = per_azi * size_azi
    blocks_ax = per_ax * size_ax
    block_rad = neighbor_list // (blocks_azi * blocks_ax)
    block_azi = neighbor_list // blocks_ax % blocks_azi
    block_ax = neighbor_list % blocks_ax
    owner_dev = (
        block_rad // per_rad * size_azi + block_azi // per_azi
    ) * size_ax + block_ax // per_ax
    local_pos = (block_rad % per_rad * per_azi + block_azi % per_azi) * per_ax + block_ax % per_ax
    dev_rad = owner_dev // (size_azi * size_ax)
    dev_azi = owner_dev // size_ax % size_azi
    dev_ax = owner_dev % size_ax
    beside_all = jnp.mean(gathered_means[dev_rad, dev_azi, dev_ax, local_pos], axis=-1)
    smooth = 0.5 * block_mean + 0.5 * beside_all
    own_index = (
        lax.axis_index("rad") * size_azi + lax.axis_index("azi")
    ) * size_ax + lax.axis_index("ax")
    moved = (owner_map != own_index).astype(jnp.float32)
    block_cost = (
        smooth * (1.0 + 7.0 * refine_flag.astype(jnp.float32))
        + 0.25 * migrate_weight.astype(jnp.float32) * moved
    )
    width = block_cost.size
    payload = jnp.concatenate([
        block_cost.reshape(-1), owner_map.reshape(-1).astype(jnp.float32),
        jnp.zeros((128 - 2 * width,), jnp.float32),
    ])
    owner_load = load_gather(payload, width)
    return (indicator, block_cost, owner_load)


def solution(mesh):
    return jax.shard_map(
        on_device,
        mesh=mesh,
        in_specs=(
            P(None, "rad", "azi", "ax"),
            P(None, "rad", "azi", "ax"),
            P("rad", "azi", "ax"),
            P("rad", "azi", "ax"),
            P("rad", "azi", "ax"),
            P("rad", "azi", "ax", None),
        ),
        out_specs=(P("rad", "azi", "ax"), P("rad", "azi", "ax"), P("rad", "azi", "ax")),
        check_vma=False,
    )
```

```python
import functools
import itertools
import jax
import jax.numpy as jnp
from jax import lax
from jax.experimental import pallas as pl
from jax.experimental.pallas import tpu as pltpu
from jax.sharding import PartitionSpec as P

BLK = 16
AXES = ("rad", "azi", "ax")
MESH = pl.DeviceIdType.MESH


def stage_plan(sizes, groups):
    plan = []
    for axes in groups:
        offs = [o for o in itertools.product(*[range(sizes[i]) for i in axes]) if any(o)]
        plan.append((axes, offs))
    return plan


def gen_gather_kernel(sizes, groups, x_ref, o_ref, lsem, ssem, rsem, with_barrier=True):
    me = tuple(lax.axis_index(a) for a in AXES)
    plan = stage_plan(sizes, groups)

    def shift(off_axes, off, sign):
        dev = list(me)
        for i, o in zip(off_axes, off):
            dev[i] = lax.rem(me[i] + (o if sign > 0 else sizes[i] - o), sizes[i])
        return tuple(dev)

    if with_barrier:
        barrier = pltpu.get_barrier_semaphore()
        count = 0
        for axes, offs in plan:
            for off in offs:
                pl.semaphore_signal(barrier, 1, device_id=shift(axes, off, 1), device_id_type=MESH)
                count += 1
        pl.semaphore_wait(barrier, count)

    covered = set()

    def region(dev):
        idx = []
        for i in range(3):
            if i in covered:
                break
            idx.append(pl.ds(dev[i], 1))
        return o_ref.at[tuple(idx)] if idx else o_ref

    def region_full(dev):
        n_fixed = 3 - len(covered)
        return o_ref.at[tuple(pl.ds(dev[i], 1) for i in range(n_fixed))]

    local = pltpu.make_async_copy(x_ref, o_ref.at[tuple(pl.ds(m, 1) for m in me)], lsem)
    local.start()
    sends = []
    slot = 0
    for stage, (axes, offs) in enumerate(plan):
        src = x_ref if stage == 0 else region_full(me)
        first = slot
        for off in offs:
            c = pltpu.make_async_remote_copy(src_ref=src, dst_ref=region_full(me), send_sem=ssem.at[slot],
                                             recv_sem=rsem.at[slot], device_id=shift(axes, off, 1), device_id_type=MESH)
            c.start()
            sends.append(c)
            slot += 1
        slot = first
        for off in offs:
            frm = shift(axes, off, -1)
            c = pltpu.make_async_remote_copy(src_ref=src, dst_ref=region_full(frm), send_sem=ssem.at[slot],
                                             recv_sem=rsem.at[slot], device_id=frm, device_id_type=MESH)
            c.wait_recv()
            slot += 1
        if stage == 0:
            local.wait()
        covered.update(axes)
    return sends


def gather_kernel(sizes, groups, x_ref, o_ref, lsem, ssem, rsem):
    for c in gen_gather_kernel(sizes, groups, x_ref, o_ref, lsem, ssem, rsem):
        c.wait_send()


def load_kernel(sizes, groups, width, x_ref, load_out, o_ref, lsem, ssem, rsem):
    sends = gen_gather_kernel(sizes, groups, x_ref, o_ref, lsem, ssem, rsem)
    me = (lax.axis_index("rad") * sizes[1] + lax.axis_index("azi")) * sizes[2] + lax.axis_index("ax")
    values = o_ref[...]
    owners = pltpu.roll(values, values.shape[-1] - width, 3)
    lane = lax.broadcasted_iota(jnp.int32, values.shape, 3)
    picked = jnp.where((lane < width) & (owners == me.astype(jnp.float32)), values, 0.0)
    part = jnp.sum(picked, axis=(0, 1))
    total = jnp.sum(part, axis=0, keepdims=True)
    total = jnp.sum(total, axis=1, keepdims=True)
    load_out[...] = (total / float(width)).reshape(1, 1, 1)
    for c in sends:
        c.wait_send()


def load_gather(payload, width, groups=((2, 1), (0,))):
    sizes = tuple(lax.axis_size(a) for a in AXES)
    lanes = payload.shape[0]
    links = sum(len(offs) for _, offs in stage_plan(sizes, groups))
    return pl.pallas_call(
        functools.partial(load_kernel, sizes, groups, width),
        out_shape=jax.ShapeDtypeStruct((1, 1, 1), jnp.float32),
        in_specs=[pl.BlockSpec(memory_space=pltpu.VMEM)],
        out_specs=pl.BlockSpec(memory_space=pltpu.VMEM),
        scratch_shapes=[
            pltpu.VMEM(sizes + (lanes,), jnp.float32),
            pltpu.SemaphoreType.DMA(()),
            pltpu.SemaphoreType.DMA((links,)),
            pltpu.SemaphoreType.DMA((links,)),
        ],
        compiler_params=pltpu.CompilerParams(collective_id=1, has_side_effects=True),
    )(payload.reshape(1, 1, 1, lanes))


def cost_load_kernel(sizes, groups, blocks, nl_ref, gm_ref, aux_ref, cost_out, load_out,
                     gm_s, sums_s, sums_v, pay, o_ref, csem, lsem, ssem, rsem):
    n_r, n_a, n_x = sizes
    per_rad, per_azi, per_ax = blocks
    width = per_rad * per_azi * per_ax
    me = tuple(lax.axis_index(a) for a in AXES)
    barrier = pltpu.get_barrier_semaphore()
    n_peers = 0
    for axes, offs in stage_plan(sizes, groups):
        for off in offs:
            dev = list(me)
            for i, o in zip(axes, off):
                dev[i] = lax.rem(me[i] + o, sizes[i])
            pl.semaphore_signal(barrier, 1, device_id=tuple(dev), device_id_type=MESH)
            n_peers += 1
    to_smem = pltpu.make_async_copy(gm_ref, gm_s, csem.at[0])
    to_smem.start()

    def clear(i, carry):
        sums_s[0, i] = 0.0
        sums_s[1, i] = 0.0
        return carry

    lax.fori_loop(0, sums_s.shape[1], clear, 0)
    to_smem.wait()
    blocks_azi = per_azi * n_a
    blocks_ax = per_ax * n_x
    for b in range(width):
        total = None
        for k in range(6):
            v = nl_ref[b * 6 + k]
            br = v // (blocks_azi * blocks_ax)
            ba = v // blocks_ax % blocks_azi
            bx = v % blocks_ax
            local = (br % per_rad * per_azi + ba % per_azi) * per_ax + bx % per_ax
            val = gm_s[br // per_rad, ba // per_azi, bx // per_ax, local]
            total = val if total is None else total + val
        sums_s[0, b] = total
        sums_s[1, b] = gm_s[me[0], me[1], me[2], b]
    to_vmem = pltpu.make_async_copy(sums_s, sums_v, csem.at[1])
    to_vmem.start()
    to_vmem.wait()
    me_f = ((me[0] * n_a + me[1]) * n_x + me[2]).astype(jnp.float32)
    both = sums_v[...]
    aux = aux_ref[...]
    refine, migrate, owner = aux[0:1], aux[1:2], aux[2:3]
    smooth = 0.5 * both[1:2] + 0.5 * (both[0:1] / 6.0)
    moved = jnp.where(owner != me_f, 1.0, 0.0)
    cost = smooth * (1.0 + 7.0 * refine) + 0.25 * migrate * moved
    cost_out[...] = cost
    lane = lax.broadcasted_iota(jnp.int32, cost.shape, 1)
    pay[0, 0] = jnp.where(lane < width, cost, pltpu.roll(owner, width, 1))
    pl.semaphore_wait(barrier, n_peers)
    sends = gen_gather_kernel(sizes, groups, pay, o_ref, lsem, ssem, rsem, with_barrier=False)
    values = o_ref[...]
    owners = pltpu.roll(values, values.shape[-1] - width, 3)
    lane4 = lax.broadcasted_iota(jnp.int32, values.shape, 3)
    picked = jnp.where((lane4 < width) & (owners == me_f), values, 0.0)
    part = jnp.sum(picked, axis=(0, 1))
    total = jnp.sum(part, axis=0, keepdims=True)
    total = jnp.sum(total, axis=1, keepdims=True)
    load_out[...] = (total / float(width)).reshape(1, 1, 1)
    for c in sends:
        c.wait_send()


def cost_load(gathered_means, neighbor_list, refine_flag, migrate_weight, owner_map, blocks, groups=((2, 1), (0,))):
    sizes = tuple(lax.axis_size(a) for a in AXES)
    width = refine_flag.size
    lanes = 128
    links = sum(len(offs) for _, offs in stage_plan(sizes, groups))
    aux = jnp.stack([refine_flag.reshape(-1), migrate_weight.reshape(-1), owner_map.reshape(-1)]).astype(jnp.float32)
    aux = jnp.pad(aux, ((0, 0), (0, lanes - width)))
    vmem = pl.BlockSpec(memory_space=pltpu.VMEM)
    cost, load = pl.pallas_call(
        functools.partial(cost_load_kernel, sizes, groups, blocks),
        out_shape=(jax.ShapeDtypeStruct((1, lanes), jnp.float32), jax.ShapeDtypeStruct((1, 1, 1), jnp.float32)),
        in_specs=[pl.BlockSpec(memory_space=pltpu.SMEM), vmem, vmem],
        out_specs=(vmem, vmem),
        scratch_shapes=[
            pltpu.SMEM(gathered_means.shape, jnp.float32),
            pltpu.SMEM((2, lanes), jnp.float32),
            pltpu.VMEM((2, lanes), jnp.float32),
            pltpu.VMEM((1, 1, 1, lanes), jnp.float32),
            pltpu.VMEM(sizes + (lanes,), jnp.float32),
            pltpu.SemaphoreType.DMA((2,)),
            pltpu.SemaphoreType.DMA(()),
            pltpu.SemaphoreType.DMA((links,)),
            pltpu.SemaphoreType.DMA((links,)),
        ],
        compiler_params=pltpu.CompilerParams(collective_id=1, has_side_effects=True),
    )(neighbor_list.reshape(-1), gathered_means, aux)
    return cost[0, :width].reshape(refine_flag.shape), load


def gather_all(values, cid, groups=((2, 1), (0,))):
    sizes = tuple(lax.axis_size(a) for a in AXES)
    width = values.shape[0]
    links = sum(len(offs) for _, offs in stage_plan(sizes, groups))
    out = pl.pallas_call(
        functools.partial(gather_kernel, sizes, groups),
        out_shape=jax.ShapeDtypeStruct(sizes + (width,), jnp.float32),
        in_specs=[pl.BlockSpec(memory_space=pltpu.VMEM)],
        out_specs=pl.BlockSpec(memory_space=pltpu.VMEM),
        scratch_shapes=[pltpu.SemaphoreType.DMA(()), pltpu.SemaphoreType.DMA((links,)), pltpu.SemaphoreType.DMA((links,))],
        compiler_params=pltpu.CompilerParams(collective_id=cid, has_side_effects=True),
    )(values.reshape(1, 1, 1, width))
    return out.reshape(-1)


def dense(x):
    return x.reshape(-1, 128)


def exchange(tail, head, axis, periodic):
    count = lax.axis_size(axis)
    forward = [(i, i + 1) for i in range(count - 1)]
    if periodic:
        forward.append((count - 1, 0))
    backward = [(target, source) for source, target in forward]
    low = lax.ppermute(dense(tail), axis, forward).reshape(tail.shape)
    high = lax.ppermute(dense(head), axis, backward).reshape(head.shape)
    return low, high


def flux_pair(state_lo, state_hi, along):
    return [h - l for h, l in zip(euler_flux(state_hi, along), euler_flux(state_lo, along))]


def euler_flux(s, along):
    density, m0, m1, m2, energy = s
    momenta = (m0, m1, m2)
    inv = 1.0 / density
    velocity = momenta[along] * inv
    kinetic = 0.5 * (m0 * m0 + m1 * m1 + m2 * m2) * inv
    pressure = 0.4 * (energy - kinetic)
    columns = [momenta[along], m0 * velocity, m1 * velocity, m2 * velocity, (energy + pressure) * velocity]
    columns[1 + along] = columns[1 + along] + pressure
    return columns


def faces(um2, um1, u, up1, up2):
    lower = (7.0 * um1 - um2) / 12.0 + (7.0 * u - up1) / 12.0
    upper = (7.0 * u - um1) / 12.0 + (7.0 * up1 - up2) / 12.0
    return lower, upper


def fourth(zm2, zm1, z, zp1, zp2):
    return (zm2 - 4.0 * zm1 + 6.0 * z - 4.0 * zp1 + zp2) / 12.0


def stencil_kernel(groups, p_hbm, a_hbm, out_ref, g_out, e, az_send, az_recv, az_exp, x_send, x_recv, xt, sems, ssem, rsem,
                   pay, glsem, gssem, grsem):
    _, fields, ext_rows, n_a, n_x = e.shape
    rows = ext_rows - 4
    n_r_dev, n_a_dev, n_x_dev = (lax.axis_size(ax) for ax in AXES)
    me_r, me_a, me_x = (lax.axis_index(ax) for ax in AXES)
    has_r_lo, has_r_hi = me_r > 0, me_r < n_r_dev - 1
    has_x_lo, has_x_hi = me_x > 0, me_x < n_x_dev - 1
    r_lo, r_hi = (me_r - 1, me_a, me_x), (me_r + 1, me_a, me_x)
    a_lo = (me_r, lax.rem(me_a + n_a_dev - 1, n_a_dev), me_x)
    a_hi = (me_r, lax.rem(me_a + 1, n_a_dev), me_x)
    x_lo, x_hi = (me_r, me_a, me_x - 1), (me_r, me_a, me_x + 1)

    loads = [
        pltpu.make_async_copy(p_hbm, e.at[0, :, pl.ds(2, rows)], sems.at[0]),
        pltpu.make_async_copy(a_hbm, e.at[1, :, pl.ds(2, rows)], sems.at[1]),
    ]
    for c in loads:
        c.start()

    sizes = (n_r_dev, n_a_dev, n_x_dev)
    me = (me_r, me_a, me_x)
    barrier = pltpu.get_barrier_semaphore()
    n_peers = 0
    for axes, offs in stage_plan(sizes, groups):
        for off in offs:
            dev = list(me)
            for i, o in zip(axes, off):
                dev[i] = lax.rem(me[i] + o, sizes[i])
            pl.semaphore_signal(barrier, 1, device_id=tuple(dev), device_id_type=MESH)
            n_peers += 1

    x_recv[:, x_send.shape[1]:, :] = jnp.zeros((2, x_recv.shape[1] - x_send.shape[1], x_recv.shape[2]), jnp.float32)
    x_send[:, 4 * fields:, :] = jnp.zeros((2, x_send.shape[1] - 4 * fields, x_send.shape[2]), jnp.float32)
    for c in loads:
        c.wait()

    def remote(src, dst, i, dev):
        return pltpu.make_async_remote_copy(
            src_ref=src, dst_ref=dst, send_sem=ssem.at[i], recv_sem=rsem.at[i],
            device_id=dev, device_id_type=MESH,
        )

    n_kx = x_send.shape[1]
    sends = [
        (has_r_hi, remote(e.at[:, :, pl.ds(rows, 2)], e.at[:, :, pl.ds(0, 2)], 0, r_hi)),
        (has_r_lo, remote(e.at[:, :, pl.ds(2, 2)], e.at[:, :, pl.ds(rows + 2, 2)], 1, r_lo)),
        (None, remote(az_send.at[1], az_recv.at[0], 2, a_hi)),
        (None, remote(az_send.at[0], az_recv.at[1], 3, a_lo)),
        (has_x_hi, remote(x_send.at[1], x_recv.at[0, pl.ds(0, n_kx)], 4, x_hi)),
        (has_x_lo, remote(x_send.at[0], x_recv.at[1, pl.ds(0, n_kx)], 5, x_lo)),
    ]
    recvs = [
        (has_r_lo, remote(e.at[:, :, pl.ds(rows, 2)], e.at[:, :, pl.ds(0, 2)], 0, r_lo)),
        (has_r_hi, remote(e.at[:, :, pl.ds(2, 2)], e.at[:, :, pl.ds(rows + 2, 2)], 1, r_hi)),
        (None, remote(az_send.at[1], az_recv.at[0], 2, a_lo)),
        (None, remote(az_send.at[0], az_recv.at[1], 3, a_hi)),
        (has_x_lo, remote(x_send.at[1], x_recv.at[0, pl.ds(0, n_kx)], 4, x_lo)),
        (has_x_hi, remote(x_send.at[0], x_recv.at[1, pl.ds(0, n_kx)], 5, x_hi)),
    ]

    def when(cond, fn):
        if cond is None:
            fn()
        else:
            pl.when(cond)(fn)

    for k in range(2):
        for f in range(fields):
            for r in range(rows):
                row = ((k * fields + f) * rows + r) * 2
                az_send[0, row:row + 2, :] = e[k, f, 2 + r, 0:2, :]
                az_send[1, row:row + 2, :] = e[k, f, 2 + r, n_a - 2:n_a, :]
            plane = e[k, f, 2:2 + rows].reshape(rows * n_a, n_x)
            cols = plane.T
            row = (k * fields + f) * 2
            x_send[0, row:row + 2, :] = cols[0:2]
            x_send[1, row:row + 2, :] = cols[n_x - 2:n_x]

    pl.semaphore_wait(barrier, n_peers)
    for cond, c in sends:
        when(cond, c.start)

    @pl.when(jnp.logical_not(has_r_lo))
    def _():
        e[:, :, 0:2] = jnp.zeros((2, fields, 2, n_a, n_x), jnp.float32)

    @pl.when(jnp.logical_not(has_r_hi))
    def _():
        e[:, :, rows + 2:rows + 4] = jnp.zeros((2, fields, 2, n_a, n_x), jnp.float32)

    @pl.when(jnp.logical_not(has_x_lo))
    def _():
        x_recv[0, 0:n_kx, :] = jnp.zeros((n_kx, x_recv.shape[2]), jnp.float32)

    @pl.when(jnp.logical_not(has_x_hi))
    def _():
        x_recv[1, 0:n_kx, :] = jnp.zeros((n_kx, x_recv.shape[2]), jnp.float32)

    for cond, c in recvs[2:]:
        when(cond, c.wait_recv)

    for side in range(2):
        xt[side] = x_recv[side].T
        for k in range(2):
            for f in range(fields):
                for r in range(rows):
                    row = ((k * fields + f) * rows + r) * 2
                    az_exp[side, r, k * fields + f, 0:2, :] = az_recv[side, row:row + 2, :]

    sub = lax.broadcasted_iota(jnp.int32, (n_a, n_x), 0)
    lane = lax.broadcasted_iota(jnp.int32, (n_a, n_x), 1)

    def shifted_azi(u, lo, hi):
        um1 = jnp.where(sub == 0, jnp.broadcast_to(lo[1:2], u.shape), pltpu.roll(u, 1, 0))
        um2 = jnp.where(sub == 0, jnp.broadcast_to(lo[0:1], u.shape),
                        jnp.where(sub == 1, jnp.broadcast_to(lo[1:2], u.shape), pltpu.roll(u, 2, 0)))
        up1 = jnp.where(sub == n_a - 1, jnp.broadcast_to(hi[0:1], u.shape), pltpu.roll(u, n_a - 1, 0))
        up2 = jnp.where(sub == n_a - 1, jnp.broadcast_to(hi[1:2], u.shape),
                        jnp.where(sub == n_a - 2, jnp.broadcast_to(hi[0:1], u.shape), pltpu.roll(u, n_a - 2, 0)))
        return um2, um1, u, up1, up2

    def shifted_ax(u, lo0, lo1, hi0, hi1):
        um1 = jnp.where(lane == 0, jnp.broadcast_to(lo1, u.shape), pltpu.roll(u, 1, 1))
        um2 = jnp.where(lane == 0, jnp.broadcast_to(lo0, u.shape),
                        jnp.where(lane == 1, jnp.broadcast_to(lo1, u.shape), pltpu.roll(u, 2, 1)))
        up1 = jnp.where(lane == n_x - 1, jnp.broadcast_to(hi0, u.shape), pltpu.roll(u, n_x - 1, 1))
        up2 = jnp.where(lane == n_x - 1, jnp.broadcast_to(hi1, u.shape),
                        jnp.where(lane == n_x - 2, jnp.broadcast_to(hi0, u.shape), pltpu.roll(u, n_x - 2, 1)))
        return um2, um1, u, up1, up2

    def row_body(r, carry):
        base = pl.multiple_of(r * n_a, n_a)
        xlo = xt[0, pl.ds(base, n_a), :]
        xhi = xt[1, pl.ds(base, n_a), :]
        lo_s, hi_s, w = [], [], []
        for f in range(fields):
            lo, hi = faces(*[e[0, f, r + k] for k in range(5)])
            lo_s.append(lo)
            hi_s.append(hi)
            w.append(fourth(*[e[1, f, r + k] for k in range(5)]))
        balance = flux_pair(lo_s, hi_s, 0)
        weight = w
        lo_s, hi_s, w = [], [], []
        for f in range(fields):
            lo, hi = faces(*shifted_azi(e[0, f, r + 2], az_exp[0, r, f], az_exp[1, r, f]))
            lo_s.append(lo)
            hi_s.append(hi)
            w.append(fourth(*shifted_azi(e[1, f, r + 2], az_exp[0, r, fields + f], az_exp[1, r, fields + f])))
        part = flux_pair(lo_s, hi_s, 1)
        balance = [b + p for b, p in zip(balance, part)]
        weight = [a + b for a, b in zip(weight, w)]
        lo_s, hi_s, w = [], [], []
        for f in range(fields):
            cp, ca = 2 * f, 2 * (fields + f)
            lo, hi = faces(*shifted_ax(e[0, f, r + 2], xlo[:, cp:cp + 1], xlo[:, cp + 1:cp + 2],
                                       xhi[:, cp:cp + 1], xhi[:, cp + 1:cp + 2]))
            lo_s.append(lo)
            hi_s.append(hi)
            w.append(fourth(*shifted_ax(e[1, f, r + 2], xlo[:, ca:ca + 1], xlo[:, ca + 1:ca + 2],
                                        xhi[:, ca:ca + 1], xhi[:, ca + 1:ca + 2])))
        part = flux_pair(lo_s, hi_s, 2)
        balance = [b + p for b, p in zip(balance, part)]
        weight = [a + b for a, b in zip(weight, w)]
        total = weight[0] * balance[0]
        for f in range(1, fields):
            total = total + weight[f] * balance[f]
        value = jnp.abs(total)
        out_ref[r] = value
        return carry + value

    acc = lax.fori_loop(2, rows - 2, row_body, jnp.zeros((n_a, n_x), jnp.float32))
    for cond, c in recvs[:2]:
        when(cond, c.wait_recv)
    acc = lax.fori_loop(0, 2, row_body, acc)
    acc = lax.fori_loop(rows - 2, rows, row_body, acc)
    per_azi, per_ax = n_a // BLK, n_x // BLK
    width = per_azi * per_ax
    lane_l = lax.broadcasted_iota(jnp.int32, (n_x, width), 0)
    col_j = lax.broadcasted_iota(jnp.int32, (n_x, width), 1)
    means = None
    for ba in range(per_azi):
        half = jnp.sum(acc[ba * BLK:(ba + 1) * BLK], axis=0, keepdims=True)
        pick = jnp.where((col_j // per_ax == ba) & (lane_l // BLK == col_j % per_ax), 1.0, 0.0)
        part = jnp.dot(half, pick, precision=lax.Precision.HIGHEST, preferred_element_type=jnp.float32)
        means = part if means is None else means + part
    pay[0, 0] = means / float(rows * BLK * BLK)
    sends_g = gen_gather_kernel(sizes, groups, pay, g_out, glsem, gssem, grsem, with_barrier=False)

    for cond, c in sends:
        when(cond, c.wait_send)
    for c in sends_g:
        c.wait_send()


def stencil(primal, adjoint, groups=((2, 1), (0,))):
    fields, rows, n_a, n_x = primal.shape
    anywhere = pl.BlockSpec(memory_space=pltpu.HBM)
    sizes = tuple(lax.axis_size(a) for a in AXES)
    width = (n_a // BLK) * (n_x // BLK)
    links = sum(len(offs) for _, offs in stage_plan(sizes, groups))
    return pl.pallas_call(
        functools.partial(stencil_kernel, groups),
        out_shape=(jax.ShapeDtypeStruct((rows, n_a, n_x), jnp.float32), jax.ShapeDtypeStruct(sizes + (width,), jnp.float32)),
        in_specs=[anywhere, anywhere],
        out_specs=(pl.BlockSpec(memory_space=pltpu.VMEM), pl.BlockSpec(memory_space=pltpu.VMEM)),
        scratch_shapes=[
            pltpu.VMEM((2, fields, rows + 4, n_a, n_x), jnp.float32),
            pltpu.VMEM((2, 2 * fields * rows * 2, n_x), jnp.float32),
            pltpu.VMEM((2, 2 * fields * rows * 2, n_x), jnp.float32),
            pltpu.VMEM((2, rows, 2 * fields, 8, n_x), jnp.float32),
            pltpu.VMEM((2, -(-4 * fields // 8) * 8, rows * n_a), jnp.float32),
            pltpu.VMEM((2, 128, rows * n_a), jnp.float32),
            pltpu.VMEM((2, rows * n_a, 128), jnp.float32),
            pltpu.SemaphoreType.DMA((2,)),
            pltpu.SemaphoreType.DMA((6,)),
            pltpu.SemaphoreType.DMA((6,)),
            pltpu.VMEM((1, 1, 1, width), jnp.float32),
            pltpu.SemaphoreType.DMA(()),
            pltpu.SemaphoreType.DMA((links,)),
            pltpu.SemaphoreType.DMA((links,)),
        ],
        compiler_params=pltpu.CompilerParams(
            collective_id=2, has_side_effects=True, vmem_limit_bytes=67043328
        ),
    )(primal, adjoint)


def on_device(primal, adjoint, refine_flag, owner_map, migrate_weight, neighbor_list):
    indicator, gathered_means = stencil(primal, adjoint)
    rows_rad, rows_azi, rows_ax = indicator.shape
    per_rad = rows_rad // BLK
    per_azi = rows_azi // BLK
    per_ax = rows_ax // BLK
    block_cost, owner_load = cost_load(gathered_means, neighbor_list, refine_flag, migrate_weight, owner_map, (per_rad, per_azi, per_ax))
    return (indicator, block_cost, owner_load)


def solution(mesh):
    return jax.shard_map(
        on_device,
        mesh=mesh,
        in_specs=(
            P(None, "rad", "azi", "ax"),
            P(None, "rad", "azi", "ax"),
            P("rad", "azi", "ax"),
            P("rad", "azi", "ax"),
            P("rad", "azi", "ax"),
            P("rad", "azi", "ax", None),
        ),
        out_specs=(P("rad", "azi", "ax"), P("rad", "azi", "ax"), P("rad", "azi", "ax")),
        check_vma=False,
    )
```

```python
import functools
import itertools
import jax
import jax.numpy as jnp
from jax import lax
from jax.experimental import pallas as pl
from jax.experimental.pallas import tpu as pltpu
from jax.sharding import PartitionSpec as P

BLK = 16
AXES = ("rad", "azi", "ax")
MESH = pl.DeviceIdType.MESH


def stage_plan(sizes, groups):
    plan = []
    for axes in groups:
        offs = [o for o in itertools.product(*[range(sizes[i]) for i in axes]) if any(o)]
        plan.append((axes, offs))
    return plan


def gen_gather_kernel(sizes, groups, x_ref, o_ref, lsem, ssem, rsem, with_barrier=True):
    me = tuple(lax.axis_index(a) for a in AXES)
    plan = stage_plan(sizes, groups)

    def shift(off_axes, off, sign):
        dev = list(me)
        for i, o in zip(off_axes, off):
            dev[i] = lax.rem(me[i] + (o if sign > 0 else sizes[i] - o), sizes[i])
        return tuple(dev)

    if with_barrier:
        barrier = pltpu.get_barrier_semaphore()
        count = 0
        for axes, offs in plan:
            for off in offs:
                pl.semaphore_signal(barrier, 1, device_id=shift(axes, off, 1), device_id_type=MESH)
                count += 1
        pl.semaphore_wait(barrier, count)

    covered = set()

    def region(dev):
        idx = []
        for i in range(3):
            if i in covered:
                break
            idx.append(pl.ds(dev[i], 1))
        return o_ref.at[tuple(idx)] if idx else o_ref

    def region_full(dev):
        n_fixed = 3 - len(covered)
        return o_ref.at[tuple(pl.ds(dev[i], 1) for i in range(n_fixed))]

    local = pltpu.make_async_copy(x_ref, o_ref.at[tuple(pl.ds(m, 1) for m in me)], lsem)
    local.start()
    sends = []
    slot = 0
    for stage, (axes, offs) in enumerate(plan):
        src = x_ref if stage == 0 else region_full(me)
        first = slot
        for off in offs:
            c = pltpu.make_async_remote_copy(src_ref=src, dst_ref=region_full(me), send_sem=ssem.at[slot],
                                             recv_sem=rsem.at[slot], device_id=shift(axes, off, 1), device_id_type=MESH)
            c.start()
            sends.append(c)
            slot += 1
        slot = first
        for off in offs:
            frm = shift(axes, off, -1)
            c = pltpu.make_async_remote_copy(src_ref=src, dst_ref=region_full(frm), send_sem=ssem.at[slot],
                                             recv_sem=rsem.at[slot], device_id=frm, device_id_type=MESH)
            c.wait_recv()
            slot += 1
        if stage == 0:
            local.wait()
        covered.update(axes)
    return sends


def gather_kernel(sizes, groups, x_ref, o_ref, lsem, ssem, rsem):
    for c in gen_gather_kernel(sizes, groups, x_ref, o_ref, lsem, ssem, rsem):
        c.wait_send()


def load_kernel(sizes, groups, width, x_ref, load_out, o_ref, lsem, ssem, rsem):
    sends = gen_gather_kernel(sizes, groups, x_ref, o_ref, lsem, ssem, rsem)
    me = (lax.axis_index("rad") * sizes[1] + lax.axis_index("azi")) * sizes[2] + lax.axis_index("ax")
    values = o_ref[...]
    owners = pltpu.roll(values, values.shape[-1] - width, 3)
    lane = lax.broadcasted_iota(jnp.int32, values.shape, 3)
    picked = jnp.where((lane < width) & (owners == me.astype(jnp.float32)), values, 0.0)
    part = jnp.sum(picked, axis=(0, 1))
    total = jnp.sum(part, axis=0, keepdims=True)
    total = jnp.sum(total, axis=1, keepdims=True)
    load_out[...] = (total / float(width)).reshape(1, 1, 1)
    for c in sends:
        c.wait_send()


def load_gather(payload, width, groups=((2, 1), (0,))):
    sizes = tuple(lax.axis_size(a) for a in AXES)
    lanes = payload.shape[0]
    links = sum(len(offs) for _, offs in stage_plan(sizes, groups))
    return pl.pallas_call(
        functools.partial(load_kernel, sizes, groups, width),
        out_shape=jax.ShapeDtypeStruct((1, 1, 1), jnp.float32),
        in_specs=[pl.BlockSpec(memory_space=pltpu.VMEM)],
        out_specs=pl.BlockSpec(memory_space=pltpu.VMEM),
        scratch_shapes=[
            pltpu.VMEM(sizes + (lanes,), jnp.float32),
            pltpu.SemaphoreType.DMA(()),
            pltpu.SemaphoreType.DMA((links,)),
            pltpu.SemaphoreType.DMA((links,)),
        ],
        compiler_params=pltpu.CompilerParams(collective_id=1, has_side_effects=True),
    )(payload.reshape(1, 1, 1, lanes))


def cost_load_kernel(sizes, groups, blocks, nl_ref, gm_ref, rf_ref, mw_ref, ow_ref, cost_out, load_out,
                     gm_s, sums_s, sums_v, pay, o_ref, csem, lsem, ssem, rsem):
    n_r, n_a, n_x = sizes
    per_rad, per_azi, per_ax = blocks
    width = per_rad * per_azi * per_ax
    me = tuple(lax.axis_index(a) for a in AXES)
    barrier = pltpu.get_barrier_semaphore()
    n_peers = 0
    for axes, offs in stage_plan(sizes, groups):
        for off in offs:
            dev = list(me)
            for i, o in zip(axes, off):
                dev[i] = lax.rem(me[i] + o, sizes[i])
            pl.semaphore_signal(barrier, 1, device_id=tuple(dev), device_id_type=MESH)
            n_peers += 1
    to_smem = pltpu.make_async_copy(gm_ref, gm_s, csem.at[0])
    to_smem.start()

    def clear(i, carry):
        sums_s[0, i] = 0.0
        sums_s[1, i] = 0.0
        return carry

    lax.fori_loop(0, sums_s.shape[1], clear, 0)
    to_smem.wait()
    blocks_azi = per_azi * n_a
    blocks_ax = per_ax * n_x
    for b in range(width):
        total = None
        for k in range(6):
            v = nl_ref[b * 6 + k]
            br = v // (blocks_azi * blocks_ax)
            ba = v // blocks_ax % blocks_azi
            bx = v % blocks_ax
            local = (br % per_rad * per_azi + ba % per_azi) * per_ax + bx % per_ax
            val = gm_s[br // per_rad, ba // per_azi, bx // per_ax, local]
            total = val if total is None else total + val
        sums_s[0, b] = total
        sums_s[1, b] = gm_s[me[0], me[1], me[2], b]
    me_i = (me[0] * n_a + me[1]) * n_x + me[2]
    me_f = me_i.astype(jnp.float32)
    for b in range(width):
        i0, i1 = b // per_ax, b % per_ax
        smooth = 0.5 * sums_s[1, b] + 0.5 * (sums_s[0, b] * (1.0 / 6.0))
        own = ow_ref[0, i0, i1]
        gain = 1.0 + 7.0 * rf_ref[0, i0, i1].astype(jnp.float32)
        extra = jnp.where(own != me_i, 0.25 * mw_ref[0, i0, i1].astype(jnp.float32), 0.0)
        c = smooth * gain + extra
        cost_out[0, i0, i1] = c
        sums_s[0, b] = c
        sums_s[0, width + b] = own.astype(jnp.float32)
    to_vmem = pltpu.make_async_copy(sums_s, sums_v, csem.at[1])
    to_vmem.start()
    to_vmem.wait()
    pay[0, 0] = sums_v[0:1]
    pl.semaphore_wait(barrier, n_peers)
    sends = gen_gather_kernel(sizes, groups, pay, o_ref, lsem, ssem, rsem, with_barrier=False)
    values = o_ref[...]
    owners = pltpu.roll(values, values.shape[-1] - width, 3)
    lane4 = lax.broadcasted_iota(jnp.int32, values.shape, 3)
    picked = jnp.where((lane4 < width) & (owners == me_f), values, 0.0)
    part = jnp.sum(picked, axis=(0, 1))
    total = jnp.sum(part, axis=0, keepdims=True)
    total = jnp.sum(total, axis=1, keepdims=True)
    load_out[...] = (total / float(width)).reshape(1, 1, 1)
    for c in sends:
        c.wait_send()


def cost_load(gathered_means, neighbor_list, refine_flag, migrate_weight, owner_map, blocks, groups=((2, 1), (0,))):
    sizes = tuple(lax.axis_size(a) for a in AXES)
    width = refine_flag.size
    lanes = 128
    links = sum(len(offs) for _, offs in stage_plan(sizes, groups))
    smem = pl.BlockSpec(memory_space=pltpu.SMEM)
    vmem = pl.BlockSpec(memory_space=pltpu.VMEM)
    cost, load = pl.pallas_call(
        functools.partial(cost_load_kernel, sizes, groups, blocks),
        out_shape=(jax.ShapeDtypeStruct(refine_flag.shape, jnp.float32), jax.ShapeDtypeStruct((1, 1, 1), jnp.float32)),
        in_specs=[smem, vmem, smem, smem, smem],
        out_specs=(smem, vmem),
        scratch_shapes=[
            pltpu.SMEM(gathered_means.shape, jnp.float32),
            pltpu.SMEM((2, lanes), jnp.float32),
            pltpu.VMEM((2, lanes), jnp.float32),
            pltpu.VMEM((1, 1, 1, lanes), jnp.float32),
            pltpu.VMEM(sizes + (lanes,), jnp.float32),
            pltpu.SemaphoreType.DMA((2,)),
            pltpu.SemaphoreType.DMA(()),
            pltpu.SemaphoreType.DMA((links,)),
            pltpu.SemaphoreType.DMA((links,)),
        ],
        compiler_params=pltpu.CompilerParams(collective_id=1, has_side_effects=True),
    )(neighbor_list.reshape(-1), gathered_means, refine_flag, migrate_weight, owner_map)
    return cost, load


def gather_all(values, cid, groups=((2, 1), (0,))):
    sizes = tuple(lax.axis_size(a) for a in AXES)
    width = values.shape[0]
    links = sum(len(offs) for _, offs in stage_plan(sizes, groups))
    out = pl.pallas_call(
        functools.partial(gather_kernel, sizes, groups),
        out_shape=jax.ShapeDtypeStruct(sizes + (width,), jnp.float32),
        in_specs=[pl.BlockSpec(memory_space=pltpu.VMEM)],
        out_specs=pl.BlockSpec(memory_space=pltpu.VMEM),
        scratch_shapes=[pltpu.SemaphoreType.DMA(()), pltpu.SemaphoreType.DMA((links,)), pltpu.SemaphoreType.DMA((links,))],
        compiler_params=pltpu.CompilerParams(collective_id=cid, has_side_effects=True),
    )(values.reshape(1, 1, 1, width))
    return out.reshape(-1)


def dense(x):
    return x.reshape(-1, 128)


def exchange(tail, head, axis, periodic):
    count = lax.axis_size(axis)
    forward = [(i, i + 1) for i in range(count - 1)]
    if periodic:
        forward.append((count - 1, 0))
    backward = [(target, source) for source, target in forward]
    low = lax.ppermute(dense(tail), axis, forward).reshape(tail.shape)
    high = lax.ppermute(dense(head), axis, backward).reshape(head.shape)
    return low, high


def flux_pair(state_lo, state_hi, along):
    return [h - l for h, l in zip(euler_flux(state_hi, along), euler_flux(state_lo, along))]


def euler_flux(s, along):
    density, m0, m1, m2, energy = s
    momenta = (m0, m1, m2)
    inv = 1.0 / density
    velocity = momenta[along] * inv
    kinetic = 0.5 * (m0 * m0 + m1 * m1 + m2 * m2) * inv
    pressure = 0.4 * (energy - kinetic)
    columns = [momenta[along], m0 * velocity, m1 * velocity, m2 * velocity, (energy + pressure) * velocity]
    columns[1 + along] = columns[1 + along] + pressure
    return columns


def faces(um2, um1, u, up1, up2):
    lower = (7.0 * um1 - um2) / 12.0 + (7.0 * u - up1) / 12.0
    upper = (7.0 * u - um1) / 12.0 + (7.0 * up1 - up2) / 12.0
    return lower, upper


def fourth(zm2, zm1, z, zp1, zp2):
    return (zm2 - 4.0 * zm1 + 6.0 * z - 4.0 * zp1 + zp2) / 12.0


def stencil_kernel(groups, p_hbm, a_hbm, out_ref, g_out, e, az_send, az_recv, az_exp, x_send, x_recv, xt, sems, ssem, rsem,
                   pay, glsem, gssem, grsem):
    _, fields, ext_rows, n_a, n_x = e.shape
    rows = ext_rows - 4
    n_r_dev, n_a_dev, n_x_dev = (lax.axis_size(ax) for ax in AXES)
    me_r, me_a, me_x = (lax.axis_index(ax) for ax in AXES)
    has_r_lo, has_r_hi = me_r > 0, me_r < n_r_dev - 1
    has_x_lo, has_x_hi = me_x > 0, me_x < n_x_dev - 1
    r_lo, r_hi = (me_r - 1, me_a, me_x), (me_r + 1, me_a, me_x)
    a_lo = (me_r, lax.rem(me_a + n_a_dev - 1, n_a_dev), me_x)
    a_hi = (me_r, lax.rem(me_a + 1, n_a_dev), me_x)
    x_lo, x_hi = (me_r, me_a, me_x - 1), (me_r, me_a, me_x + 1)

    loads = [
        pltpu.make_async_copy(p_hbm, e.at[0, :, pl.ds(2, rows)], sems.at[0]),
        pltpu.make_async_copy(a_hbm, e.at[1, :, pl.ds(2, rows)], sems.at[1]),
    ]
    for c in loads:
        c.start()

    sizes = (n_r_dev, n_a_dev, n_x_dev)
    me = (me_r, me_a, me_x)
    barrier = pltpu.get_barrier_semaphore()
    n_peers = 0
    for axes, offs in stage_plan(sizes, groups):
        for off in offs:
            dev = list(me)
            for i, o in zip(axes, off):
                dev[i] = lax.rem(me[i] + o, sizes[i])
            pl.semaphore_signal(barrier, 1, device_id=tuple(dev), device_id_type=MESH)
            n_peers += 1

    x_recv[:, x_send.shape[1]:, :] = jnp.zeros((2, x_recv.shape[1] - x_send.shape[1], x_recv.shape[2]), jnp.float32)
    x_send[:, 4 * fields:, :] = jnp.zeros((2, x_send.shape[1] - 4 * fields, x_send.shape[2]), jnp.float32)
    for c in loads:
        c.wait()

    def remote(src, dst, i, dev):
        return pltpu.make_async_remote_copy(
            src_ref=src, dst_ref=dst, send_sem=ssem.at[i], recv_sem=rsem.at[i],
            device_id=dev, device_id_type=MESH,
        )

    n_kx = x_send.shape[1]
    sends = [
        (has_r_hi, remote(e.at[:, :, pl.ds(rows, 2)], e.at[:, :, pl.ds(0, 2)], 0, r_hi)),
        (has_r_lo, remote(e.at[:, :, pl.ds(2, 2)], e.at[:, :, pl.ds(rows + 2, 2)], 1, r_lo)),
        (None, remote(az_send.at[1], az_recv.at[0], 2, a_hi)),
        (None, remote(az_send.at[0], az_recv.at[1], 3, a_lo)),
        (has_x_hi, remote(x_send.at[1], x_recv.at[0, pl.ds(0, n_kx)], 4, x_hi)),
        (has_x_lo, remote(x_send.at[0], x_recv.at[1, pl.ds(0, n_kx)], 5, x_lo)),
    ]
    recvs = [
        (has_r_lo, remote(e.at[:, :, pl.ds(rows, 2)], e.at[:, :, pl.ds(0, 2)], 0, r_lo)),
        (has_r_hi, remote(e.at[:, :, pl.ds(2, 2)], e.at[:, :, pl.ds(rows + 2, 2)], 1, r_hi)),
        (None, remote(az_send.at[1], az_recv.at[0], 2, a_lo)),
        (None, remote(az_send.at[0], az_recv.at[1], 3, a_hi)),
        (has_x_lo, remote(x_send.at[1], x_recv.at[0, pl.ds(0, n_kx)], 4, x_lo)),
        (has_x_hi, remote(x_send.at[0], x_recv.at[1, pl.ds(0, n_kx)], 5, x_hi)),
    ]

    def when(cond, fn):
        if cond is None:
            fn()
        else:
            pl.when(cond)(fn)

    for k in range(2):
        for f in range(fields):
            for r in range(rows):
                row = ((k * fields + f) * rows + r) * 2
                az_send[0, row:row + 2, :] = e[k, f, 2 + r, 0:2, :]
                az_send[1, row:row + 2, :] = e[k, f, 2 + r, n_a - 2:n_a, :]
            plane = e[k, f, 2:2 + rows].reshape(rows * n_a, n_x)
            cols = plane.T
            row = (k * fields + f) * 2
            x_send[0, row:row + 2, :] = cols[0:2]
            x_send[1, row:row + 2, :] = cols[n_x - 2:n_x]

    pl.semaphore_wait(barrier, n_peers)
    for cond, c in sends:
        when(cond, c.start)

    @pl.when(jnp.logical_not(has_r_lo))
    def _():
        e[:, :, 0:2] = jnp.zeros((2, fields, 2, n_a, n_x), jnp.float32)

    @pl.when(jnp.logical_not(has_r_hi))
    def _():
        e[:, :, rows + 2:rows + 4] = jnp.zeros((2, fields, 2, n_a, n_x), jnp.float32)

    @pl.when(jnp.logical_not(has_x_lo))
    def _():
        x_recv[0, 0:n_kx, :] = jnp.zeros((n_kx, x_recv.shape[2]), jnp.float32)

    @pl.when(jnp.logical_not(has_x_hi))
    def _():
        x_recv[1, 0:n_kx, :] = jnp.zeros((n_kx, x_recv.shape[2]), jnp.float32)

    for cond, c in recvs[2:]:
        when(cond, c.wait_recv)

    for side in range(2):
        xt[side] = x_recv[side].T
        for k in range(2):
            for f in range(fields):
                for r in range(rows):
                    row = ((k * fields + f) * rows + r) * 2
                    az_exp[side, r, k * fields + f, 0:2, :] = az_recv[side, row:row + 2, :]

    sub = lax.broadcasted_iota(jnp.int32, (n_a, n_x), 0)
    lane = lax.broadcasted_iota(jnp.int32, (n_a, n_x), 1)

    def shifted_azi(u, lo, hi):
        um1 = jnp.where(sub == 0, jnp.broadcast_to(lo[1:2], u.shape), pltpu.roll(u, 1, 0))
        um2 = jnp.where(sub == 0, jnp.broadcast_to(lo[0:1], u.shape),
                        jnp.where(sub == 1, jnp.broadcast_to(lo[1:2], u.shape), pltpu.roll(u, 2, 0)))
        up1 = jnp.where(sub == n_a - 1, jnp.broadcast_to(hi[0:1], u.shape), pltpu.roll(u, n_a - 1, 0))
        up2 = jnp.where(sub == n_a - 1, jnp.broadcast_to(hi[1:2], u.shape),
                        jnp.where(sub == n_a - 2, jnp.broadcast_to(hi[0:1], u.shape), pltpu.roll(u, n_a - 2, 0)))
        return um2, um1, u, up1, up2

    def shifted_ax(u, lo0, lo1, hi0, hi1):
        um1 = jnp.where(lane == 0, jnp.broadcast_to(lo1, u.shape), pltpu.roll(u, 1, 1))
        um2 = jnp.where(lane == 0, jnp.broadcast_to(lo0, u.shape),
                        jnp.where(lane == 1, jnp.broadcast_to(lo1, u.shape), pltpu.roll(u, 2, 1)))
        up1 = jnp.where(lane == n_x - 1, jnp.broadcast_to(hi0, u.shape), pltpu.roll(u, n_x - 1, 1))
        up2 = jnp.where(lane == n_x - 1, jnp.broadcast_to(hi1, u.shape),
                        jnp.where(lane == n_x - 2, jnp.broadcast_to(hi0, u.shape), pltpu.roll(u, n_x - 2, 1)))
        return um2, um1, u, up1, up2

    def row_body(r, carry):
        base = pl.multiple_of(r * n_a, n_a)
        xlo = xt[0, pl.ds(base, n_a), :]
        xhi = xt[1, pl.ds(base, n_a), :]
        lo_s, hi_s, w = [], [], []
        for f in range(fields):
            lo, hi = faces(*[e[0, f, r + k] for k in range(5)])
            lo_s.append(lo)
            hi_s.append(hi)
            w.append(fourth(*[e[1, f, r + k] for k in range(5)]))
        balance = flux_pair(lo_s, hi_s, 0)
        weight = w
        lo_s, hi_s, w = [], [], []
        for f in range(fields):
            lo, hi = faces(*shifted_azi(e[0, f, r + 2], az_exp[0, r, f], az_exp[1, r, f]))
            lo_s.append(lo)
            hi_s.append(hi)
            w.append(fourth(*shifted_azi(e[1, f, r + 2], az_exp[0, r, fields + f], az_exp[1, r, fields + f])))
        part = flux_pair(lo_s, hi_s, 1)
        balance = [b + p for b, p in zip(balance, part)]
        weight = [a + b for a, b in zip(weight, w)]
        lo_s, hi_s, w = [], [], []
        for f in range(fields):
            cp, ca = 2 * f, 2 * (fields + f)
            lo, hi = faces(*shifted_ax(e[0, f, r + 2], xlo[:, cp:cp + 1], xlo[:, cp + 1:cp + 2],
                                       xhi[:, cp:cp + 1], xhi[:, cp + 1:cp + 2]))
            lo_s.append(lo)
            hi_s.append(hi)
            w.append(fourth(*shifted_ax(e[1, f, r + 2], xlo[:, ca:ca + 1], xlo[:, ca + 1:ca + 2],
                                        xhi[:, ca:ca + 1], xhi[:, ca + 1:ca + 2])))
        part = flux_pair(lo_s, hi_s, 2)
        balance = [b + p for b, p in zip(balance, part)]
        weight = [a + b for a, b in zip(weight, w)]
        total = weight[0] * balance[0]
        for f in range(1, fields):
            total = total + weight[f] * balance[f]
        value = jnp.abs(total)
        out_ref[r] = value
        return carry + value

    acc = lax.fori_loop(2, rows - 2, row_body, jnp.zeros((n_a, n_x), jnp.float32))
    for cond, c in recvs[:2]:
        when(cond, c.wait_recv)
    acc = lax.fori_loop(0, 2, row_body, acc)
    acc = lax.fori_loop(rows - 2, rows, row_body, acc)
    per_azi, per_ax = n_a // BLK, n_x // BLK
    width = per_azi * per_ax
    lane_l = lax.broadcasted_iota(jnp.int32, (n_x, width), 0)
    col_j = lax.broadcasted_iota(jnp.int32, (n_x, width), 1)
    means = None
    for ba in range(per_azi):
        half = jnp.sum(acc[ba * BLK:(ba + 1) * BLK], axis=0, keepdims=True)
        pick = jnp.where((col_j // per_ax == ba) & (lane_l // BLK == col_j % per_ax), 1.0, 0.0)
        part = jnp.dot(half, pick, precision=lax.Precision.HIGHEST, preferred_element_type=jnp.float32)
        means = part if means is None else means + part
    pay[0, 0] = means / float(rows * BLK * BLK)
    sends_g = gen_gather_kernel(sizes, groups, pay, g_out, glsem, gssem, grsem, with_barrier=False)

    for cond, c in sends:
        when(cond, c.wait_send)
    for c in sends_g:
        c.wait_send()


def stencil(primal, adjoint, groups=((2, 1), (0,))):
    fields, rows, n_a, n_x = primal.shape
    anywhere = pl.BlockSpec(memory_space=pltpu.HBM)
    sizes = tuple(lax.axis_size(a) for a in AXES)
    width = (n_a // BLK) * (n_x // BLK)
    links = sum(len(offs) for _, offs in stage_plan(sizes, groups))
    return pl.pallas_call(
        functools.partial(stencil_kernel, groups),
        out_shape=(jax.ShapeDtypeStruct((rows, n_a, n_x), jnp.float32), jax.ShapeDtypeStruct(sizes + (width,), jnp.float32)),
        in_specs=[anywhere, anywhere],
        out_specs=(pl.BlockSpec(memory_space=pltpu.VMEM), pl.BlockSpec(memory_space=pltpu.VMEM)),
        scratch_shapes=[
            pltpu.VMEM((2, fields, rows + 4, n_a, n_x), jnp.float32),
            pltpu.VMEM((2, 2 * fields * rows * 2, n_x), jnp.float32),
            pltpu.VMEM((2, 2 * fields * rows * 2, n_x), jnp.float32),
            pltpu.VMEM((2, rows, 2 * fields, 8, n_x), jnp.float32),
            pltpu.VMEM((2, -(-4 * fields // 8) * 8, rows * n_a), jnp.float32),
            pltpu.VMEM((2, 128, rows * n_a), jnp.float32),
            pltpu.VMEM((2, rows * n_a, 128), jnp.float32),
            pltpu.SemaphoreType.DMA((2,)),
            pltpu.SemaphoreType.DMA((6,)),
            pltpu.SemaphoreType.DMA((6,)),
            pltpu.VMEM((1, 1, 1, width), jnp.float32),
            pltpu.SemaphoreType.DMA(()),
            pltpu.SemaphoreType.DMA((links,)),
            pltpu.SemaphoreType.DMA((links,)),
        ],
        compiler_params=pltpu.CompilerParams(
            collective_id=2, has_side_effects=True, vmem_limit_bytes=67043328
        ),
    )(primal, adjoint)


def on_device(primal, adjoint, refine_flag, owner_map, migrate_weight, neighbor_list):
    indicator, gathered_means = stencil(primal, adjoint)
    rows_rad, rows_azi, rows_ax = indicator.shape
    per_rad = rows_rad // BLK
    per_azi = rows_azi // BLK
    per_ax = rows_ax // BLK
    block_cost, owner_load = cost_load(gathered_means, neighbor_list, refine_flag, migrate_weight, owner_map, (per_rad, per_azi, per_ax))
    return (indicator, block_cost, owner_load)


def solution(mesh):
    return jax.shard_map(
        on_device,
        mesh=mesh,
        in_specs=(
            P(None, "rad", "azi", "ax"),
            P(None, "rad", "azi", "ax"),
            P("rad", "azi", "ax"),
            P("rad", "azi", "ax"),
            P("rad", "azi", "ax"),
            P("rad", "azi", "ax", None),
        ),
        out_specs=(P("rad", "azi", "ax"), P("rad", "azi", "ax"), P("rad", "azi", "ax")),
        check_vma=False,
    )
```

```python
import functools
import itertools
import jax
import jax.numpy as jnp
from jax import lax
from jax.experimental import pallas as pl
from jax.experimental.pallas import tpu as pltpu
from jax.sharding import PartitionSpec as P

BLK = 16
AXES = ("rad", "azi", "ax")
MESH = pl.DeviceIdType.MESH


def stage_plan(sizes, groups):
    plan = []
    for axes in groups:
        offs = [o for o in itertools.product(*[range(sizes[i]) for i in axes]) if any(o)]
        plan.append((axes, offs))
    return plan


def gen_gather_kernel(sizes, groups, x_ref, o_ref, lsem, ssem, rsem, with_barrier=True):
    me = tuple(lax.axis_index(a) for a in AXES)
    plan = stage_plan(sizes, groups)

    def shift(off_axes, off, sign):
        dev = list(me)
        for i, o in zip(off_axes, off):
            dev[i] = lax.rem(me[i] + (o if sign > 0 else sizes[i] - o), sizes[i])
        return tuple(dev)

    if with_barrier:
        barrier = pltpu.get_barrier_semaphore()
        count = 0
        for axes, offs in plan:
            for off in offs:
                pl.semaphore_signal(barrier, 1, device_id=shift(axes, off, 1), device_id_type=MESH)
                count += 1
        pl.semaphore_wait(barrier, count)

    covered = set()

    def region(dev):
        idx = []
        for i in range(3):
            if i in covered:
                break
            idx.append(pl.ds(dev[i], 1))
        return o_ref.at[tuple(idx)] if idx else o_ref

    def region_full(dev):
        n_fixed = 3 - len(covered)
        return o_ref.at[tuple(pl.ds(dev[i], 1) for i in range(n_fixed))]

    local = pltpu.make_async_copy(x_ref, o_ref.at[tuple(pl.ds(m, 1) for m in me)], lsem)
    local.start()
    sends = []
    slot = 0
    for stage, (axes, offs) in enumerate(plan):
        src = x_ref if stage == 0 else region_full(me)
        first = slot
        for off in offs:
            c = pltpu.make_async_remote_copy(src_ref=src, dst_ref=region_full(me), send_sem=ssem.at[slot],
                                             recv_sem=rsem.at[slot], device_id=shift(axes, off, 1), device_id_type=MESH)
            c.start()
            sends.append(c)
            slot += 1
        slot = first
        for off in offs:
            frm = shift(axes, off, -1)
            c = pltpu.make_async_remote_copy(src_ref=src, dst_ref=region_full(frm), send_sem=ssem.at[slot],
                                             recv_sem=rsem.at[slot], device_id=frm, device_id_type=MESH)
            c.wait_recv()
            slot += 1
        if stage == 0:
            local.wait()
        covered.update(axes)
    return sends


def gather_kernel(sizes, groups, x_ref, o_ref, lsem, ssem, rsem):
    for c in gen_gather_kernel(sizes, groups, x_ref, o_ref, lsem, ssem, rsem):
        c.wait_send()


def load_kernel(sizes, groups, width, x_ref, load_out, o_ref, lsem, ssem, rsem):
    sends = gen_gather_kernel(sizes, groups, x_ref, o_ref, lsem, ssem, rsem)
    me = (lax.axis_index("rad") * sizes[1] + lax.axis_index("azi")) * sizes[2] + lax.axis_index("ax")
    values = o_ref[...]
    owners = pltpu.roll(values, values.shape[-1] - width, 3)
    lane = lax.broadcasted_iota(jnp.int32, values.shape, 3)
    picked = jnp.where((lane < width) & (owners == me.astype(jnp.float32)), values, 0.0)
    part = jnp.sum(picked, axis=(0, 1))
    total = jnp.sum(part, axis=0, keepdims=True)
    total = jnp.sum(total, axis=1, keepdims=True)
    load_out[...] = (total / float(width)).reshape(1, 1, 1)
    for c in sends:
        c.wait_send()


def load_gather(payload, width, groups=((2, 1), (0,))):
    sizes = tuple(lax.axis_size(a) for a in AXES)
    lanes = payload.shape[0]
    links = sum(len(offs) for _, offs in stage_plan(sizes, groups))
    return pl.pallas_call(
        functools.partial(load_kernel, sizes, groups, width),
        out_shape=jax.ShapeDtypeStruct((1, 1, 1), jnp.float32),
        in_specs=[pl.BlockSpec(memory_space=pltpu.VMEM)],
        out_specs=pl.BlockSpec(memory_space=pltpu.VMEM),
        scratch_shapes=[
            pltpu.VMEM(sizes + (lanes,), jnp.float32),
            pltpu.SemaphoreType.DMA(()),
            pltpu.SemaphoreType.DMA((links,)),
            pltpu.SemaphoreType.DMA((links,)),
        ],
        compiler_params=pltpu.CompilerParams(collective_id=1, has_side_effects=True),
    )(payload.reshape(1, 1, 1, lanes))


def gather_all(values, cid, groups=((2, 1), (0,))):
    sizes = tuple(lax.axis_size(a) for a in AXES)
    width = values.shape[0]
    links = sum(len(offs) for _, offs in stage_plan(sizes, groups))
    out = pl.pallas_call(
        functools.partial(gather_kernel, sizes, groups),
        out_shape=jax.ShapeDtypeStruct(sizes + (width,), jnp.float32),
        in_specs=[pl.BlockSpec(memory_space=pltpu.VMEM)],
        out_specs=pl.BlockSpec(memory_space=pltpu.VMEM),
        scratch_shapes=[pltpu.SemaphoreType.DMA(()), pltpu.SemaphoreType.DMA((links,)), pltpu.SemaphoreType.DMA((links,))],
        compiler_params=pltpu.CompilerParams(collective_id=cid, has_side_effects=True),
    )(values.reshape(1, 1, 1, width))
    return out.reshape(-1)


def dense(x):
    return x.reshape(-1, 128)


def exchange(tail, head, axis, periodic):
    count = lax.axis_size(axis)
    forward = [(i, i + 1) for i in range(count - 1)]
    if periodic:
        forward.append((count - 1, 0))
    backward = [(target, source) for source, target in forward]
    low = lax.ppermute(dense(tail), axis, forward).reshape(tail.shape)
    high = lax.ppermute(dense(head), axis, backward).reshape(head.shape)
    return low, high


def flux_pair(state_lo, state_hi, along):
    return [h - l for h, l in zip(euler_flux(state_hi, along), euler_flux(state_lo, along))]


def euler_flux(s, along):
    density, m0, m1, m2, energy = s
    momenta = (m0, m1, m2)
    inv = 1.0 / density
    velocity = momenta[along] * inv
    kinetic = 0.5 * (m0 * m0 + m1 * m1 + m2 * m2) * inv
    pressure = 0.4 * (energy - kinetic)
    columns = [momenta[along], m0 * velocity, m1 * velocity, m2 * velocity, (energy + pressure) * velocity]
    columns[1 + along] = columns[1 + along] + pressure
    return columns


def faces(um2, um1, u, up1, up2):
    lower = (7.0 * um1 - um2) / 12.0 + (7.0 * u - up1) / 12.0
    upper = (7.0 * u - um1) / 12.0 + (7.0 * up1 - up2) / 12.0
    return lower, upper


def fourth(zm2, zm1, z, zp1, zp2):
    return (zm2 - 4.0 * zm1 + 6.0 * z - 4.0 * zp1 + zp2) / 12.0


def stencil_kernel(groups, p_hbm, a_hbm, out_ref, g_out, e, az_send, az_recv, az_exp, x_send, x_recv, xt, sems, ssem, rsem,
                   pay, glsem, gssem, grsem):
    _, fields, ext_rows, n_a, n_x = e.shape
    rows = ext_rows - 4
    n_r_dev, n_a_dev, n_x_dev = (lax.axis_size(ax) for ax in AXES)
    me_r, me_a, me_x = (lax.axis_index(ax) for ax in AXES)
    has_r_lo, has_r_hi = me_r > 0, me_r < n_r_dev - 1
    has_x_lo, has_x_hi = me_x > 0, me_x < n_x_dev - 1
    r_lo, r_hi = (me_r - 1, me_a, me_x), (me_r + 1, me_a, me_x)
    a_lo = (me_r, lax.rem(me_a + n_a_dev - 1, n_a_dev), me_x)
    a_hi = (me_r, lax.rem(me_a + 1, n_a_dev), me_x)
    x_lo, x_hi = (me_r, me_a, me_x - 1), (me_r, me_a, me_x + 1)

    loads = [
        pltpu.make_async_copy(p_hbm, e.at[0, :, pl.ds(2, rows)], sems.at[0]),
        pltpu.make_async_copy(a_hbm, e.at[1, :, pl.ds(2, rows)], sems.at[1]),
    ]
    for c in loads:
        c.start()

    sizes = (n_r_dev, n_a_dev, n_x_dev)
    me = (me_r, me_a, me_x)
    barrier = pltpu.get_barrier_semaphore()
    n_peers = 0
    for axes, offs in stage_plan(sizes, groups):
        for off in offs:
            dev = list(me)
            for i, o in zip(axes, off):
                dev[i] = lax.rem(me[i] + o, sizes[i])
            pl.semaphore_signal(barrier, 1, device_id=tuple(dev), device_id_type=MESH)
            n_peers += 1

    x_recv[:, x_send.shape[1]:, :] = jnp.zeros((2, x_recv.shape[1] - x_send.shape[1], x_recv.shape[2]), jnp.float32)
    x_send[:, 4 * fields:, :] = jnp.zeros((2, x_send.shape[1] - 4 * fields, x_send.shape[2]), jnp.float32)
    for c in loads:
        c.wait()

    def remote(src, dst, i, dev):
        return pltpu.make_async_remote_copy(
            src_ref=src, dst_ref=dst, send_sem=ssem.at[i], recv_sem=rsem.at[i],
            device_id=dev, device_id_type=MESH,
        )

    n_kx = x_send.shape[1]
    sends = [
        (has_r_hi, remote(e.at[:, :, pl.ds(rows, 2)], e.at[:, :, pl.ds(0, 2)], 0, r_hi)),
        (has_r_lo, remote(e.at[:, :, pl.ds(2, 2)], e.at[:, :, pl.ds(rows + 2, 2)], 1, r_lo)),
        (None, remote(az_send.at[1], az_recv.at[0], 2, a_hi)),
        (None, remote(az_send.at[0], az_recv.at[1], 3, a_lo)),
        (has_x_hi, remote(x_send.at[1], x_recv.at[0, pl.ds(0, n_kx)], 4, x_hi)),
        (has_x_lo, remote(x_send.at[0], x_recv.at[1, pl.ds(0, n_kx)], 5, x_lo)),
    ]
    recvs = [
        (has_r_lo, remote(e.at[:, :, pl.ds(rows, 2)], e.at[:, :, pl.ds(0, 2)], 0, r_lo)),
        (has_r_hi, remote(e.at[:, :, pl.ds(2, 2)], e.at[:, :, pl.ds(rows + 2, 2)], 1, r_hi)),
        (None, remote(az_send.at[1], az_recv.at[0], 2, a_lo)),
        (None, remote(az_send.at[0], az_recv.at[1], 3, a_hi)),
        (has_x_lo, remote(x_send.at[1], x_recv.at[0, pl.ds(0, n_kx)], 4, x_lo)),
        (has_x_hi, remote(x_send.at[0], x_recv.at[1, pl.ds(0, n_kx)], 5, x_hi)),
    ]

    def when(cond, fn):
        if cond is None:
            fn()
        else:
            pl.when(cond)(fn)

    for k in range(2):
        for f in range(fields):
            for r in range(rows):
                row = ((k * fields + f) * rows + r) * 2
                az_send[0, row:row + 2, :] = e[k, f, 2 + r, 0:2, :]
                az_send[1, row:row + 2, :] = e[k, f, 2 + r, n_a - 2:n_a, :]
            plane = e[k, f, 2:2 + rows].reshape(rows * n_a, n_x)
            cols = plane.T
            row = (k * fields + f) * 2
            x_send[0, row:row + 2, :] = cols[0:2]
            x_send[1, row:row + 2, :] = cols[n_x - 2:n_x]

    pl.semaphore_wait(barrier, n_peers)
    for cond, c in sends:
        when(cond, c.start)

    @pl.when(jnp.logical_not(has_r_lo))
    def _():
        e[:, :, 0:2] = jnp.zeros((2, fields, 2, n_a, n_x), jnp.float32)

    @pl.when(jnp.logical_not(has_r_hi))
    def _():
        e[:, :, rows + 2:rows + 4] = jnp.zeros((2, fields, 2, n_a, n_x), jnp.float32)

    @pl.when(jnp.logical_not(has_x_lo))
    def _():
        x_recv[0, 0:n_kx, :] = jnp.zeros((n_kx, x_recv.shape[2]), jnp.float32)

    @pl.when(jnp.logical_not(has_x_hi))
    def _():
        x_recv[1, 0:n_kx, :] = jnp.zeros((n_kx, x_recv.shape[2]), jnp.float32)

    for cond, c in recvs[2:]:
        when(cond, c.wait_recv)

    for side in range(2):
        xt[side] = x_recv[side].T
        for k in range(2):
            for f in range(fields):
                for r in range(rows):
                    row = ((k * fields + f) * rows + r) * 2
                    az_exp[side, r, k * fields + f, 0:2, :] = az_recv[side, row:row + 2, :]

    sub = lax.broadcasted_iota(jnp.int32, (n_a, n_x), 0)
    lane = lax.broadcasted_iota(jnp.int32, (n_a, n_x), 1)

    def shifted_azi(u, lo, hi):
        um1 = jnp.where(sub == 0, jnp.broadcast_to(lo[1:2], u.shape), pltpu.roll(u, 1, 0))
        um2 = jnp.where(sub == 0, jnp.broadcast_to(lo[0:1], u.shape),
                        jnp.where(sub == 1, jnp.broadcast_to(lo[1:2], u.shape), pltpu.roll(u, 2, 0)))
        up1 = jnp.where(sub == n_a - 1, jnp.broadcast_to(hi[0:1], u.shape), pltpu.roll(u, n_a - 1, 0))
        up2 = jnp.where(sub == n_a - 1, jnp.broadcast_to(hi[1:2], u.shape),
                        jnp.where(sub == n_a - 2, jnp.broadcast_to(hi[0:1], u.shape), pltpu.roll(u, n_a - 2, 0)))
        return um2, um1, u, up1, up2

    def shifted_ax(u, lo0, lo1, hi0, hi1):
        um1 = jnp.where(lane == 0, jnp.broadcast_to(lo1, u.shape), pltpu.roll(u, 1, 1))
        um2 = jnp.where(lane == 0, jnp.broadcast_to(lo0, u.shape),
                        jnp.where(lane == 1, jnp.broadcast_to(lo1, u.shape), pltpu.roll(u, 2, 1)))
        up1 = jnp.where(lane == n_x - 1, jnp.broadcast_to(hi0, u.shape), pltpu.roll(u, n_x - 1, 1))
        up2 = jnp.where(lane == n_x - 1, jnp.broadcast_to(hi1, u.shape),
                        jnp.where(lane == n_x - 2, jnp.broadcast_to(hi0, u.shape), pltpu.roll(u, n_x - 2, 1)))
        return um2, um1, u, up1, up2

    def row_rest(r, balance, weight):
        base = pl.multiple_of(r * n_a, n_a)
        xlo = xt[0, pl.ds(base, n_a), :]
        xhi = xt[1, pl.ds(base, n_a), :]
        lo_s, hi_s, w = [], [], []
        for f in range(fields):
            lo, hi = faces(*shifted_azi(e[0, f, r + 2], az_exp[0, r, f], az_exp[1, r, f]))
            lo_s.append(lo)
            hi_s.append(hi)
            w.append(fourth(*shifted_azi(e[1, f, r + 2], az_exp[0, r, fields + f], az_exp[1, r, fields + f])))
        part = flux_pair(lo_s, hi_s, 1)
        balance = [b + p for b, p in zip(balance, part)]
        weight = [a + b for a, b in zip(weight, w)]
        lo_s, hi_s, w = [], [], []
        for f in range(fields):
            cp, ca = 2 * f, 2 * (fields + f)
            lo, hi = faces(*shifted_ax(e[0, f, r + 2], xlo[:, cp:cp + 1], xlo[:, cp + 1:cp + 2],
                                       xhi[:, cp:cp + 1], xhi[:, cp + 1:cp + 2]))
            lo_s.append(lo)
            hi_s.append(hi)
            w.append(fourth(*shifted_ax(e[1, f, r + 2], xlo[:, ca:ca + 1], xlo[:, ca + 1:ca + 2],
                                        xhi[:, ca:ca + 1], xhi[:, ca + 1:ca + 2])))
        part = flux_pair(lo_s, hi_s, 2)
        balance = [b + p for b, p in zip(balance, part)]
        weight = [a + b for a, b in zip(weight, w)]
        total = weight[0] * balance[0]
        for f in range(1, fields):
            total = total + weight[f] * balance[f]
        value = jnp.abs(total)
        out_ref[r] = value
        return value

    def radial_weight(r):
        return [fourth(*[e[1, f, r + k] for k in range(5)]) for f in range(fields)]

    def row_body(r, carry):
        lo_s, hi_s = [], []
        for f in range(fields):
            lo, hi = faces(*[e[0, f, r + k] for k in range(5)])
            lo_s.append(lo)
            hi_s.append(hi)
        return carry + row_rest(r, flux_pair(lo_s, hi_s, 0), radial_weight(r))

    def row_body_carry(r, carry):
        acc, flux_lo = carry
        flux_hi = euler_flux([faces(*[e[0, f, r + k] for k in range(5)])[1] for f in range(fields)], 0)
        balance = [h - l for h, l in zip(flux_hi, flux_lo)]
        return acc + row_rest(r, balance, radial_weight(r)), flux_hi

    first_lo = euler_flux([faces(*[e[0, f, 2 + k] for k in range(5)])[0] for f in range(fields)], 0)
    acc, _ = lax.fori_loop(2, rows - 2, row_body_carry, (jnp.zeros((n_a, n_x), jnp.float32), first_lo))
    for cond, c in recvs[:2]:
        when(cond, c.wait_recv)
    acc = lax.fori_loop(0, 2, row_body, acc)
    acc = lax.fori_loop(rows - 2, rows, row_body, acc)
    per_azi, per_ax = n_a // BLK, n_x // BLK
    width = per_azi * per_ax
    lane_l = lax.broadcasted_iota(jnp.int32, (n_x, width), 0)
    col_j = lax.broadcasted_iota(jnp.int32, (n_x, width), 1)
    means = None
    for ba in range(per_azi):
        half = jnp.sum(acc[ba * BLK:(ba + 1) * BLK], axis=0, keepdims=True)
        pick = jnp.where((col_j // per_ax == ba) & (lane_l // BLK == col_j % per_ax), 1.0, 0.0)
        part = jnp.dot(half, pick, precision=lax.Precision.HIGHEST, preferred_element_type=jnp.float32)
        means = part if means is None else means + part
    pay[0, 0] = means / float(rows * BLK * BLK)
    sends_g = gen_gather_kernel(sizes, groups, pay, g_out, glsem, gssem, grsem, with_barrier=False)

    for cond, c in sends:
        when(cond, c.wait_send)
    for c in sends_g:
        c.wait_send()


def stencil(primal, adjoint, groups=((2, 1), (0,))):
    fields, rows, n_a, n_x = primal.shape
    anywhere = pl.BlockSpec(memory_space=pltpu.HBM)
    sizes = tuple(lax.axis_size(a) for a in AXES)
    width = (n_a // BLK) * (n_x // BLK)
    links = sum(len(offs) for _, offs in stage_plan(sizes, groups))
    return pl.pallas_call(
        functools.partial(stencil_kernel, groups),
        out_shape=(jax.ShapeDtypeStruct((rows, n_a, n_x), jnp.float32), jax.ShapeDtypeStruct(sizes + (width,), jnp.float32)),
        in_specs=[anywhere, anywhere],
        out_specs=(pl.BlockSpec(memory_space=pltpu.VMEM), pl.BlockSpec(memory_space=pltpu.VMEM)),
        scratch_shapes=[
            pltpu.VMEM((2, fields, rows + 4, n_a, n_x), jnp.float32),
            pltpu.VMEM((2, 2 * fields * rows * 2, n_x), jnp.float32),
            pltpu.VMEM((2, 2 * fields * rows * 2, n_x), jnp.float32),
            pltpu.VMEM((2, rows, 2 * fields, 8, n_x), jnp.float32),
            pltpu.VMEM((2, -(-4 * fields // 8) * 8, rows * n_a), jnp.float32),
            pltpu.VMEM((2, 128, rows * n_a), jnp.float32),
            pltpu.VMEM((2, rows * n_a, 128), jnp.float32),
            pltpu.SemaphoreType.DMA((2,)),
            pltpu.SemaphoreType.DMA((6,)),
            pltpu.SemaphoreType.DMA((6,)),
            pltpu.VMEM((1, 1, 1, width), jnp.float32),
            pltpu.SemaphoreType.DMA(()),
            pltpu.SemaphoreType.DMA((links,)),
            pltpu.SemaphoreType.DMA((links,)),
        ],
        compiler_params=pltpu.CompilerParams(
            collective_id=2, has_side_effects=True, vmem_limit_bytes=67043328
        ),
    )(primal, adjoint)


def on_device(primal, adjoint, refine_flag, owner_map, migrate_weight, neighbor_list):
    indicator, gathered_means = stencil(primal, adjoint)
    rows_rad, rows_azi, rows_ax = indicator.shape
    per_rad = rows_rad // BLK
    per_azi = rows_azi // BLK
    per_ax = rows_ax // BLK
    block_mean = lax.dynamic_slice(
        gathered_means, (lax.axis_index("rad"), lax.axis_index("azi"), lax.axis_index("ax"), 0),
        (1, 1, 1, gathered_means.shape[3]),
    ).reshape(per_rad, per_azi, per_ax)
    size_rad = lax.axis_size("rad")
    size_azi = lax.axis_size("azi")
    size_ax = lax.axis_size("ax")
    blocks_azi = per_azi * size_azi
    blocks_ax = per_ax * size_ax
    block_rad = neighbor_list // (blocks_azi * blocks_ax)
    block_azi = neighbor_list // blocks_ax % blocks_azi
    block_ax = neighbor_list % blocks_ax
    owner_dev = (
        block_rad // per_rad * size_azi + block_azi // per_azi
    ) * size_ax + block_ax // per_ax
    local_pos = (block_rad % per_rad * per_azi + block_azi % per_azi) * per_ax + block_ax % per_ax
    dev_rad = owner_dev // (size_azi * size_ax)
    dev_azi = owner_dev // size_ax % size_azi
    dev_ax = owner_dev % size_ax
    beside_all = jnp.mean(gathered_means[dev_rad, dev_azi, dev_ax, local_pos], axis=-1)
    smooth = 0.5 * block_mean + 0.5 * beside_all
    own_index = (
        lax.axis_index("rad") * size_azi + lax.axis_index("azi")
    ) * size_ax + lax.axis_index("ax")
    moved = (owner_map != own_index).astype(jnp.float32)
    block_cost = (
        smooth * (1.0 + 7.0 * refine_flag.astype(jnp.float32))
        + 0.25 * migrate_weight.astype(jnp.float32) * moved
    )
    width = block_cost.size
    payload = jnp.concatenate([
        block_cost.reshape(-1), owner_map.reshape(-1).astype(jnp.float32),
        jnp.zeros((128 - 2 * width,), jnp.float32),
    ])
    owner_load = load_gather(payload, width)
    return (indicator, block_cost, owner_load)


def solution(mesh):
    return jax.shard_map(
        on_device,
        mesh=mesh,
        in_specs=(
            P(None, "rad", "azi", "ax"),
            P(None, "rad", "azi", "ax"),
            P("rad", "azi", "ax"),
            P("rad", "azi", "ax"),
            P("rad", "azi", "ax"),
            P("rad", "azi", "ax", None),
        ),
        out_specs=(P("rad", "azi", "ax"), P("rad", "azi", "ax"), P("rad", "azi", "ax")),
        check_vma=False,
    )
```

```python
import functools
import itertools
import jax
import jax.numpy as jnp
from jax import lax
from jax.experimental import pallas as pl
from jax.experimental.pallas import tpu as pltpu
from jax.sharding import PartitionSpec as P

BLK = 16
AXES = ("rad", "azi", "ax")
MESH = pl.DeviceIdType.MESH


def stage_plan(sizes, groups):
    plan = []
    for axes in groups:
        offs = [o for o in itertools.product(*[range(sizes[i]) for i in axes]) if any(o)]
        plan.append((axes, offs))
    return plan


def gen_gather_kernel(sizes, groups, x_ref, o_ref, lsem, ssem, rsem, with_barrier=True):
    me = tuple(lax.axis_index(a) for a in AXES)
    plan = stage_plan(sizes, groups)

    def shift(off_axes, off, sign):
        dev = list(me)
        for i, o in zip(off_axes, off):
            dev[i] = lax.rem(me[i] + (o if sign > 0 else sizes[i] - o), sizes[i])
        return tuple(dev)

    if with_barrier:
        barrier = pltpu.get_barrier_semaphore()
        count = 0
        for axes, offs in plan:
            for off in offs:
                pl.semaphore_signal(barrier, 1, device_id=shift(axes, off, 1), device_id_type=MESH)
                count += 1
        pl.semaphore_wait(barrier, count)

    covered = set()

    def region(dev):
        idx = []
        for i in range(3):
            if i in covered:
                break
            idx.append(pl.ds(dev[i], 1))
        return o_ref.at[tuple(idx)] if idx else o_ref

    def region_full(dev):
        n_fixed = 3 - len(covered)
        return o_ref.at[tuple(pl.ds(dev[i], 1) for i in range(n_fixed))]

    local = pltpu.make_async_copy(x_ref, o_ref.at[tuple(pl.ds(m, 1) for m in me)], lsem)
    local.start()
    sends = []
    slot = 0
    for stage, (axes, offs) in enumerate(plan):
        src = x_ref if stage == 0 else region_full(me)
        first = slot
        for off in offs:
            c = pltpu.make_async_remote_copy(src_ref=src, dst_ref=region_full(me), send_sem=ssem.at[slot],
                                             recv_sem=rsem.at[slot], device_id=shift(axes, off, 1), device_id_type=MESH)
            c.start()
            sends.append(c)
            slot += 1
        slot = first
        for off in offs:
            frm = shift(axes, off, -1)
            c = pltpu.make_async_remote_copy(src_ref=src, dst_ref=region_full(frm), send_sem=ssem.at[slot],
                                             recv_sem=rsem.at[slot], device_id=frm, device_id_type=MESH)
            c.wait_recv()
            slot += 1
        if stage == 0:
            local.wait()
        covered.update(axes)
    return sends


def gather_kernel(sizes, groups, x_ref, o_ref, lsem, ssem, rsem):
    for c in gen_gather_kernel(sizes, groups, x_ref, o_ref, lsem, ssem, rsem):
        c.wait_send()


def load_kernel(sizes, groups, width, x_ref, load_out, o_ref, lsem, ssem, rsem):
    sends = gen_gather_kernel(sizes, groups, x_ref, o_ref, lsem, ssem, rsem)
    me = (lax.axis_index("rad") * sizes[1] + lax.axis_index("azi")) * sizes[2] + lax.axis_index("ax")
    values = o_ref[...]
    owners = pltpu.roll(values, values.shape[-1] - width, 3)
    lane = lax.broadcasted_iota(jnp.int32, values.shape, 3)
    picked = jnp.where((lane < width) & (owners == me.astype(jnp.float32)), values, 0.0)
    part = jnp.sum(picked, axis=(0, 1))
    total = jnp.sum(part, axis=0, keepdims=True)
    total = jnp.sum(total, axis=1, keepdims=True)
    load_out[...] = (total / float(width)).reshape(1, 1, 1)
    for c in sends:
        c.wait_send()


def load_gather(payload, width, groups=((2, 1), (0,))):
    sizes = tuple(lax.axis_size(a) for a in AXES)
    lanes = payload.shape[0]
    links = sum(len(offs) for _, offs in stage_plan(sizes, groups))
    return pl.pallas_call(
        functools.partial(load_kernel, sizes, groups, width),
        out_shape=jax.ShapeDtypeStruct((1, 1, 1), jnp.float32),
        in_specs=[pl.BlockSpec(memory_space=pltpu.VMEM)],
        out_specs=pl.BlockSpec(memory_space=pltpu.VMEM),
        scratch_shapes=[
            pltpu.VMEM(sizes + (lanes,), jnp.float32),
            pltpu.SemaphoreType.DMA(()),
            pltpu.SemaphoreType.DMA((links,)),
            pltpu.SemaphoreType.DMA((links,)),
        ],
        compiler_params=pltpu.CompilerParams(collective_id=1, has_side_effects=True),
    )(payload.reshape(1, 1, 1, lanes))


def cost_load_kernel(sizes, groups, blocks, nl_ref, gm_ref, rf_ref, mw_ref, ow_ref, cost_out, load_out,
                     gm_s, sums_s, sums_v, pay, o_ref, csem, lsem, ssem, rsem, with_barrier=True):
    n_r, n_a, n_x = sizes
    per_rad, per_azi, per_ax = blocks
    width = per_rad * per_azi * per_ax
    me = tuple(lax.axis_index(a) for a in AXES)
    if with_barrier:
        barrier = pltpu.get_barrier_semaphore()
        n_peers = 0
        for axes, offs in stage_plan(sizes, groups):
            for off in offs:
                dev = list(me)
                for i, o in zip(axes, off):
                    dev[i] = lax.rem(me[i] + o, sizes[i])
                pl.semaphore_signal(barrier, 1, device_id=tuple(dev), device_id_type=MESH)
                n_peers += 1
    to_smem = pltpu.make_async_copy(gm_ref, gm_s, csem.at[0])
    to_smem.start()

    def clear(i, carry):
        sums_s[0, i] = 0.0
        sums_s[1, i] = 0.0
        return carry

    lax.fori_loop(0, sums_s.shape[1], clear, 0)
    to_smem.wait()
    blocks_azi = per_azi * n_a
    blocks_ax = per_ax * n_x
    for b in range(width):
        total = None
        for k in range(6):
            v = nl_ref[b * 6 + k]
            br = v // (blocks_azi * blocks_ax)
            ba = v // blocks_ax % blocks_azi
            bx = v % blocks_ax
            local = (br % per_rad * per_azi + ba % per_azi) * per_ax + bx % per_ax
            val = gm_s[br // per_rad, ba // per_azi, bx // per_ax, local]
            total = val if total is None else total + val
        sums_s[0, b] = total
        sums_s[1, b] = gm_s[me[0], me[1], me[2], b]
    me_i = (me[0] * n_a + me[1]) * n_x + me[2]
    me_f = me_i.astype(jnp.float32)
    for b in range(width):
        i0, i1 = b // per_ax, b % per_ax
        smooth = 0.5 * sums_s[1, b] + 0.5 * (sums_s[0, b] * (1.0 / 6.0))
        own = ow_ref[0, i0, i1]
        gain = 1.0 + 7.0 * rf_ref[0, i0, i1].astype(jnp.float32)
        extra = jnp.where(own != me_i, 0.25 * mw_ref[0, i0, i1].astype(jnp.float32), 0.0)
        c = smooth * gain + extra
        cost_out[0, i0, i1] = c
        sums_s[0, b] = c
        sums_s[0, width + b] = own.astype(jnp.float32)
    to_vmem = pltpu.make_async_copy(sums_s, sums_v, csem.at[1])
    to_vmem.start()
    to_vmem.wait()
    pay[0, 0] = sums_v[0:1]
    if with_barrier:
        pl.semaphore_wait(barrier, n_peers)
    sends = gen_gather_kernel(sizes, groups, pay, o_ref, lsem, ssem, rsem, with_barrier=False)
    values = o_ref[...]
    owners = pltpu.roll(values, values.shape[-1] - width, 3)
    lane4 = lax.broadcasted_iota(jnp.int32, values.shape, 3)
    picked = jnp.where((lane4 < width) & (owners == me_f), values, 0.0)
    part = jnp.sum(picked, axis=(0, 1))
    total = jnp.sum(part, axis=0, keepdims=True)
    total = jnp.sum(total, axis=1, keepdims=True)
    load_out[...] = (total / float(width)).reshape(1, 1, 1)
    for c in sends:
        c.wait_send()


def cost_load(gathered_means, neighbor_list, refine_flag, migrate_weight, owner_map, blocks, groups=((2, 1), (0,))):
    sizes = tuple(lax.axis_size(a) for a in AXES)
    width = refine_flag.size
    lanes = 128
    links = sum(len(offs) for _, offs in stage_plan(sizes, groups))
    smem = pl.BlockSpec(memory_space=pltpu.SMEM)
    vmem = pl.BlockSpec(memory_space=pltpu.VMEM)
    cost, load = pl.pallas_call(
        functools.partial(cost_load_kernel, sizes, groups, blocks),
        out_shape=(jax.ShapeDtypeStruct(refine_flag.shape, jnp.float32), jax.ShapeDtypeStruct((1, 1, 1), jnp.float32)),
        in_specs=[smem, vmem, smem, smem, smem],
        out_specs=(smem, vmem),
        scratch_shapes=[
            pltpu.SMEM(gathered_means.shape, jnp.float32),
            pltpu.SMEM((2, lanes), jnp.float32),
            pltpu.VMEM((2, lanes), jnp.float32),
            pltpu.VMEM((1, 1, 1, lanes), jnp.float32),
            pltpu.VMEM(sizes + (lanes,), jnp.float32),
            pltpu.SemaphoreType.DMA((2,)),
            pltpu.SemaphoreType.DMA(()),
            pltpu.SemaphoreType.DMA((links,)),
            pltpu.SemaphoreType.DMA((links,)),
        ],
        compiler_params=pltpu.CompilerParams(collective_id=1, has_side_effects=True),
    )(neighbor_list.reshape(-1), gathered_means, refine_flag, migrate_weight, owner_map)
    return cost, load


def gather_all(values, cid, groups=((2, 1), (0,))):
    sizes = tuple(lax.axis_size(a) for a in AXES)
    width = values.shape[0]
    links = sum(len(offs) for _, offs in stage_plan(sizes, groups))
    out = pl.pallas_call(
        functools.partial(gather_kernel, sizes, groups),
        out_shape=jax.ShapeDtypeStruct(sizes + (width,), jnp.float32),
        in_specs=[pl.BlockSpec(memory_space=pltpu.VMEM)],
        out_specs=pl.BlockSpec(memory_space=pltpu.VMEM),
        scratch_shapes=[pltpu.SemaphoreType.DMA(()), pltpu.SemaphoreType.DMA((links,)), pltpu.SemaphoreType.DMA((links,))],
        compiler_params=pltpu.CompilerParams(collective_id=cid, has_side_effects=True),
    )(values.reshape(1, 1, 1, width))
    return out.reshape(-1)


def dense(x):
    return x.reshape(-1, 128)


def exchange(tail, head, axis, periodic):
    count = lax.axis_size(axis)
    forward = [(i, i + 1) for i in range(count - 1)]
    if periodic:
        forward.append((count - 1, 0))
    backward = [(target, source) for source, target in forward]
    low = lax.ppermute(dense(tail), axis, forward).reshape(tail.shape)
    high = lax.ppermute(dense(head), axis, backward).reshape(head.shape)
    return low, high


def flux_pair(state_lo, state_hi, along):
    return [h - l for h, l in zip(euler_flux(state_hi, along), euler_flux(state_lo, along))]


def euler_flux(s, along):
    density, m0, m1, m2, energy = s
    momenta = (m0, m1, m2)
    inv = 1.0 / density
    velocity = momenta[along] * inv
    kinetic = 0.5 * (m0 * m0 + m1 * m1 + m2 * m2) * inv
    pressure = 0.4 * (energy - kinetic)
    columns = [momenta[along], m0 * velocity, m1 * velocity, m2 * velocity, (energy + pressure) * velocity]
    columns[1 + along] = columns[1 + along] + pressure
    return columns


def faces(um2, um1, u, up1, up2):
    lower = (7.0 * um1 - um2) / 12.0 + (7.0 * u - up1) / 12.0
    upper = (7.0 * u - um1) / 12.0 + (7.0 * up1 - up2) / 12.0
    return lower, upper


def fourth(zm2, zm1, z, zp1, zp2):
    return (zm2 - 4.0 * zm1 + 6.0 * z - 4.0 * zp1 + zp2) / 12.0


def stencil_kernel(groups, p_hbm, a_hbm, nl_ref, rf_ref, mw_ref, ow_ref, out_ref, cost_out, load_out, g_out, e, az_send, az_recv, az_exp, x_send, x_recv, xt, sems, ssem, rsem,
                   pay, glsem, gssem, grsem,
                   gm_s, sums_s, sums_v, pay2, o2, csem, lsem2, ssem2, rsem2):
    _, fields, ext_rows, n_a, n_x = e.shape
    rows = ext_rows - 4
    n_r_dev, n_a_dev, n_x_dev = (lax.axis_size(ax) for ax in AXES)
    me_r, me_a, me_x = (lax.axis_index(ax) for ax in AXES)
    has_r_lo, has_r_hi = me_r > 0, me_r < n_r_dev - 1
    has_x_lo, has_x_hi = me_x > 0, me_x < n_x_dev - 1
    r_lo, r_hi = (me_r - 1, me_a, me_x), (me_r + 1, me_a, me_x)
    a_lo = (me_r, lax.rem(me_a + n_a_dev - 1, n_a_dev), me_x)
    a_hi = (me_r, lax.rem(me_a + 1, n_a_dev), me_x)
    x_lo, x_hi = (me_r, me_a, me_x - 1), (me_r, me_a, me_x + 1)

    loads = [
        pltpu.make_async_copy(p_hbm, e.at[0, :, pl.ds(2, rows)], sems.at[0]),
        pltpu.make_async_copy(a_hbm, e.at[1, :, pl.ds(2, rows)], sems.at[1]),
    ]
    for c in loads:
        c.start()

    sizes = (n_r_dev, n_a_dev, n_x_dev)
    me = (me_r, me_a, me_x)
    barrier = pltpu.get_barrier_semaphore()
    n_peers = 0
    for axes, offs in stage_plan(sizes, groups):
        for off in offs:
            dev = list(me)
            for i, o in zip(axes, off):
                dev[i] = lax.rem(me[i] + o, sizes[i])
            pl.semaphore_signal(barrier, 1, device_id=tuple(dev), device_id_type=MESH)
            n_peers += 1

    x_recv[:, x_send.shape[1]:, :] = jnp.zeros((2, x_recv.shape[1] - x_send.shape[1], x_recv.shape[2]), jnp.float32)
    x_send[:, 4 * fields:, :] = jnp.zeros((2, x_send.shape[1] - 4 * fields, x_send.shape[2]), jnp.float32)
    for c in loads:
        c.wait()

    def remote(src, dst, i, dev):
        return pltpu.make_async_remote_copy(
            src_ref=src, dst_ref=dst, send_sem=ssem.at[i], recv_sem=rsem.at[i],
            device_id=dev, device_id_type=MESH,
        )

    n_kx = x_send.shape[1]
    sends = [
        (has_r_hi, remote(e.at[:, :, pl.ds(rows, 2)], e.at[:, :, pl.ds(0, 2)], 0, r_hi)),
        (has_r_lo, remote(e.at[:, :, pl.ds(2, 2)], e.at[:, :, pl.ds(rows + 2, 2)], 1, r_lo)),
        (None, remote(az_send.at[1], az_recv.at[0], 2, a_hi)),
        (None, remote(az_send.at[0], az_recv.at[1], 3, a_lo)),
        (has_x_hi, remote(x_send.at[1], x_recv.at[0, pl.ds(0, n_kx)], 4, x_hi)),
        (has_x_lo, remote(x_send.at[0], x_recv.at[1, pl.ds(0, n_kx)], 5, x_lo)),
    ]
    recvs = [
        (has_r_lo, remote(e.at[:, :, pl.ds(rows, 2)], e.at[:, :, pl.ds(0, 2)], 0, r_lo)),
        (has_r_hi, remote(e.at[:, :, pl.ds(2, 2)], e.at[:, :, pl.ds(rows + 2, 2)], 1, r_hi)),
        (None, remote(az_send.at[1], az_recv.at[0], 2, a_lo)),
        (None, remote(az_send.at[0], az_recv.at[1], 3, a_hi)),
        (has_x_lo, remote(x_send.at[1], x_recv.at[0, pl.ds(0, n_kx)], 4, x_lo)),
        (has_x_hi, remote(x_send.at[0], x_recv.at[1, pl.ds(0, n_kx)], 5, x_hi)),
    ]

    def when(cond, fn):
        if cond is None:
            fn()
        else:
            pl.when(cond)(fn)

    for k in range(2):
        for f in range(fields):
            for r in range(rows):
                row = ((k * fields + f) * rows + r) * 2
                az_send[0, row:row + 2, :] = e[k, f, 2 + r, 0:2, :]
                az_send[1, row:row + 2, :] = e[k, f, 2 + r, n_a - 2:n_a, :]
            plane = e[k, f, 2:2 + rows].reshape(rows * n_a, n_x)
            cols = plane.T
            row = (k * fields + f) * 2
            x_send[0, row:row + 2, :] = cols[0:2]
            x_send[1, row:row + 2, :] = cols[n_x - 2:n_x]

    pl.semaphore_wait(barrier, n_peers)
    for cond, c in sends:
        when(cond, c.start)

    @pl.when(jnp.logical_not(has_r_lo))
    def _():
        e[:, :, 0:2] = jnp.zeros((2, fields, 2, n_a, n_x), jnp.float32)

    @pl.when(jnp.logical_not(has_r_hi))
    def _():
        e[:, :, rows + 2:rows + 4] = jnp.zeros((2, fields, 2, n_a, n_x), jnp.float32)

    @pl.when(jnp.logical_not(has_x_lo))
    def _():
        x_recv[0, 0:n_kx, :] = jnp.zeros((n_kx, x_recv.shape[2]), jnp.float32)

    @pl.when(jnp.logical_not(has_x_hi))
    def _():
        x_recv[1, 0:n_kx, :] = jnp.zeros((n_kx, x_recv.shape[2]), jnp.float32)

    for cond, c in recvs[2:]:
        when(cond, c.wait_recv)

    for side in range(2):
        xt[side] = x_recv[side].T
        for k in range(2):
            for f in range(fields):
                for r in range(rows):
                    row = ((k * fields + f) * rows + r) * 2
                    az_exp[side, r, k * fields + f, 0:2, :] = az_recv[side, row:row + 2, :]

    sub = lax.broadcasted_iota(jnp.int32, (n_a, n_x), 0)
    lane = lax.broadcasted_iota(jnp.int32, (n_a, n_x), 1)

    def shifted_azi(u, lo, hi):
        um1 = jnp.where(sub == 0, jnp.broadcast_to(lo[1:2], u.shape), pltpu.roll(u, 1, 0))
        um2 = jnp.where(sub == 0, jnp.broadcast_to(lo[0:1], u.shape),
                        jnp.where(sub == 1, jnp.broadcast_to(lo[1:2], u.shape), pltpu.roll(u, 2, 0)))
        up1 = jnp.where(sub == n_a - 1, jnp.broadcast_to(hi[0:1], u.shape), pltpu.roll(u, n_a - 1, 0))
        up2 = jnp.where(sub == n_a - 1, jnp.broadcast_to(hi[1:2], u.shape),
                        jnp.where(sub == n_a - 2, jnp.broadcast_to(hi[0:1], u.shape), pltpu.roll(u, n_a - 2, 0)))
        return um2, um1, u, up1, up2

    def shifted_ax(u, lo0, lo1, hi0, hi1):
        um1 = jnp.where(lane == 0, jnp.broadcast_to(lo1, u.shape), pltpu.roll(u, 1, 1))
        um2 = jnp.where(lane == 0, jnp.broadcast_to(lo0, u.shape),
                        jnp.where(lane == 1, jnp.broadcast_to(lo1, u.shape), pltpu.roll(u, 2, 1)))
        up1 = jnp.where(lane == n_x - 1, jnp.broadcast_to(hi0, u.shape), pltpu.roll(u, n_x - 1, 1))
        up2 = jnp.where(lane == n_x - 1, jnp.broadcast_to(hi1, u.shape),
                        jnp.where(lane == n_x - 2, jnp.broadcast_to(hi0, u.shape), pltpu.roll(u, n_x - 2, 1)))
        return um2, um1, u, up1, up2

    def row_body(r, carry):
        base = pl.multiple_of(r * n_a, n_a)
        xlo = xt[0, pl.ds(base, n_a), :]
        xhi = xt[1, pl.ds(base, n_a), :]
        lo_s, hi_s, w = [], [], []
        for f in range(fields):
            lo, hi = faces(*[e[0, f, r + k] for k in range(5)])
            lo_s.append(lo)
            hi_s.append(hi)
            w.append(fourth(*[e[1, f, r + k] for k in range(5)]))
        balance = flux_pair(lo_s, hi_s, 0)
        weight = w
        lo_s, hi_s, w = [], [], []
        for f in range(fields):
            lo, hi = faces(*shifted_azi(e[0, f, r + 2], az_exp[0, r, f], az_exp[1, r, f]))
            lo_s.append(lo)
            hi_s.append(hi)
            w.append(fourth(*shifted_azi(e[1, f, r + 2], az_exp[0, r, fields + f], az_exp[1, r, fields + f])))
        part = flux_pair(lo_s, hi_s, 1)
        balance = [b + p for b, p in zip(balance, part)]
        weight = [a + b for a, b in zip(weight, w)]
        lo_s, hi_s, w = [], [], []
        for f in range(fields):
            cp, ca = 2 * f, 2 * (fields + f)
            lo, hi = faces(*shifted_ax(e[0, f, r + 2], xlo[:, cp:cp + 1], xlo[:, cp + 1:cp + 2],
                                       xhi[:, cp:cp + 1], xhi[:, cp + 1:cp + 2]))
            lo_s.append(lo)
            hi_s.append(hi)
            w.append(fourth(*shifted_ax(e[1, f, r + 2], xlo[:, ca:ca + 1], xlo[:, ca + 1:ca + 2],
                                        xhi[:, ca:ca + 1], xhi[:, ca + 1:ca + 2])))
        part = flux_pair(lo_s, hi_s, 2)
        balance = [b + p for b, p in zip(balance, part)]
        weight = [a + b for a, b in zip(weight, w)]
        total = weight[0] * balance[0]
        for f in range(1, fields):
            total = total + weight[f] * balance[f]
        value = jnp.abs(total)
        out_ref[r] = value
        return carry + value

    acc = lax.fori_loop(2, rows - 2, row_body, jnp.zeros((n_a, n_x), jnp.float32))
    for cond, c in recvs[:2]:
        when(cond, c.wait_recv)
    acc = lax.fori_loop(0, 2, row_body, acc)
    acc = lax.fori_loop(rows - 2, rows, row_body, acc)
    per_azi, per_ax = n_a // BLK, n_x // BLK
    width = per_azi * per_ax
    lane_l = lax.broadcasted_iota(jnp.int32, (n_x, width), 0)
    col_j = lax.broadcasted_iota(jnp.int32, (n_x, width), 1)
    means = None
    for ba in range(per_azi):
        half = jnp.sum(acc[ba * BLK:(ba + 1) * BLK], axis=0, keepdims=True)
        pick = jnp.where((col_j // per_ax == ba) & (lane_l // BLK == col_j % per_ax), 1.0, 0.0)
        part = jnp.dot(half, pick, precision=lax.Precision.HIGHEST, preferred_element_type=jnp.float32)
        means = part if means is None else means + part
    pay[0, 0] = means / float(rows * BLK * BLK)
    sends_g = gen_gather_kernel(sizes, groups, pay, g_out, glsem, gssem, grsem, with_barrier=False)

    for cond, c in sends:
        when(cond, c.wait_send)
    cost_load_kernel(sizes, groups, (rows // BLK, n_a // BLK, n_x // BLK), nl_ref, g_out, rf_ref, mw_ref, ow_ref,
                     cost_out, load_out, gm_s, sums_s, sums_v, pay2, o2, csem, lsem2, ssem2, rsem2, with_barrier=False)
    for c in sends_g:
        c.wait_send()


def stencil(primal, adjoint, neighbor_list, refine_flag, migrate_weight, owner_map, groups=((2, 1), (0,))):
    fields, rows, n_a, n_x = primal.shape
    anywhere = pl.BlockSpec(memory_space=pltpu.HBM)
    sizes = tuple(lax.axis_size(a) for a in AXES)
    width = (n_a // BLK) * (n_x // BLK)
    links = sum(len(offs) for _, offs in stage_plan(sizes, groups))
    return pl.pallas_call(
        functools.partial(stencil_kernel, groups),
        out_shape=(
            jax.ShapeDtypeStruct((rows, n_a, n_x), jnp.float32),
            jax.ShapeDtypeStruct(refine_flag.shape, jnp.float32),
            jax.ShapeDtypeStruct((1, 1, 1), jnp.float32),
        ),
        in_specs=[anywhere, anywhere] + [pl.BlockSpec(memory_space=pltpu.SMEM)] * 4,
        out_specs=(
            pl.BlockSpec(memory_space=pltpu.VMEM),
            pl.BlockSpec(memory_space=pltpu.SMEM),
            pl.BlockSpec(memory_space=pltpu.VMEM),
        ),
        scratch_shapes=[
            pltpu.VMEM(sizes + (width,), jnp.float32),
            pltpu.VMEM((2, fields, rows + 4, n_a, n_x), jnp.float32),
            pltpu.VMEM((2, 2 * fields * rows * 2, n_x), jnp.float32),
            pltpu.VMEM((2, 2 * fields * rows * 2, n_x), jnp.float32),
            pltpu.VMEM((2, rows, 2 * fields, 8, n_x), jnp.float32),
            pltpu.VMEM((2, -(-4 * fields // 8) * 8, rows * n_a), jnp.float32),
            pltpu.VMEM((2, 128, rows * n_a), jnp.float32),
            pltpu.VMEM((2, rows * n_a, 128), jnp.float32),
            pltpu.SemaphoreType.DMA((2,)),
            pltpu.SemaphoreType.DMA((6,)),
            pltpu.SemaphoreType.DMA((6,)),
            pltpu.VMEM((1, 1, 1, width), jnp.float32),
            pltpu.SemaphoreType.DMA(()),
            pltpu.SemaphoreType.DMA((links,)),
            pltpu.SemaphoreType.DMA((links,)),
            pltpu.SMEM(sizes + (width,), jnp.float32),
            pltpu.SMEM((2, 128), jnp.float32),
            pltpu.VMEM((2, 128), jnp.float32),
            pltpu.VMEM((1, 1, 1, 128), jnp.float32),
            pltpu.VMEM(sizes + (128,), jnp.float32),
            pltpu.SemaphoreType.DMA((2,)),
            pltpu.SemaphoreType.DMA(()),
            pltpu.SemaphoreType.DMA((links,)),
            pltpu.SemaphoreType.DMA((links,)),
        ],
        compiler_params=pltpu.CompilerParams(
            collective_id=2, has_side_effects=True, vmem_limit_bytes=67043328
        ),
    )(primal, adjoint, neighbor_list.reshape(-1), refine_flag, migrate_weight, owner_map)


def on_device(primal, adjoint, refine_flag, owner_map, migrate_weight, neighbor_list):
    indicator, block_cost, owner_load = stencil(primal, adjoint, neighbor_list, refine_flag, migrate_weight, owner_map)
    rows_rad, rows_azi, rows_ax = indicator.shape
    per_rad = rows_rad // BLK
    per_azi = rows_azi // BLK
    per_ax = rows_ax // BLK
    return (indicator, block_cost, owner_load)


def solution(mesh):
    return jax.shard_map(
        on_device,
        mesh=mesh,
        in_specs=(
            P(None, "rad", "azi", "ax"),
            P(None, "rad", "azi", "ax"),
            P("rad", "azi", "ax"),
            P("rad", "azi", "ax"),
            P("rad", "azi", "ax"),
            P("rad", "azi", "ax", None),
        ),
        out_specs=(P("rad", "azi", "ax"), P("rad", "azi", "ax"), P("rad", "azi", "ax")),
        check_vma=False,
    )
```
